256 devices in a mesh: ctx: 16 (over z, core), exp: 16 (over x, y).
Axes of the slice: x: 4, y: 4, z: 8, core: 2. Of those that a mesh axis runs over, the one named last changes fastest.
Arguments:
- query_input: bfloat16 [2048, 8192], P('ctx', 'exp'), may hold values from -6 to 6
- key_input: bfloat16 [2048, 8192], P('ctx', 'exp'), may hold values from -6 to 6
- value_input: bfloat16 [2048, 8192], P('ctx', 'exp'), may hold values from -6 to 6
- gate_logits: float32 [2, 2048, 64], P(None, 'ctx', 'exp'), may hold values from -6 to 6
- comp_weight: float32 [2, 32, 64], P(None, None, 'exp'), may hold values from -6 to 6
- out_proj: bfloat16 [8192, 7168], P('exp', 'ctx'), may hold values from -0.0625 to 0.0625
- residual_in: bfloat16 [2048, 7168], P(('ctx', 'exp')), may hold values from -3 to 3
- ffn_gain: float32 [7168], replicated, may hold values from 0.25 to 1.75
- expert_ids: int32 [2048, 2], P(('ctx', 'exp')), may hold values from 0 to 15, all different within a row; in each aligned block of 8 rows (0 to 7, 8 to 15, ...) at most 2 rows name the same one
- route_gates: float32 [2048, 2], P(('ctx', 'exp')), may hold values from 0.2 to 1
- expert_gate: bfloat16 [16, 7168, 2048], P('exp', None, 'ctx'), may hold values from -0.0625 to 0.0625
- expert_up: bfloat16 [16, 7168, 2048], P('exp', None, 'ctx'), may hold values from -0.0625 to 0.0625
- expert_down: bfloat16 [16, 2048, 7168], P('exp', 'ctx'), may hold values from -0.125 to 0.125
Outputs:
- layer_out: bfloat16 [2048, 7168], P(('ctx', 'exp'))
The draws below stay inside these ranges and needn't reach their ends.
Inputs may be any that keep to these rules, and one draw needn't show every extreme that they name: `expert_ids`: each token names 2 different experts. In every aligned block of 8 consecutive tokens no expert is named more than 2 times, a bound that some block reaches.
All inputs are finite; a program needn't handle non-finite values.
Results may differ from the reference program's by a relative error of at most 0.0085.
Values may be sent and summed in bfloat16 or wider, within the bound.
A program may use at most 128 MiB of HBM per device.

```python
import math
import jax
import jax.numpy as jnp
import numpy as np
from jax import lax

D = 7168
HEADS = 64
HD = 128
FF = 2048
BLOCK = 32
STRIDE = 16
WINDOW = 512
TOP = 2
TOK_DEV = 128
SEQ = 2048
EXPERTS = 16
CAP = 2
N_CTX = 16
N_EXP = 16


def level_of(stream_key, shape, split, least, largest):
    def one(position, shards_of):
        heights = jax.random.uniform(jax.random.fold_in(jax.random.fold_in(stream_key, 6), position), (shards_of,), jnp.float32, least / len(split), largest / len(split))
        return jnp.repeat(jnp.exp(heights), shape[position] // shards_of).reshape((-1,) + (1,) * (len(shape) - position - 1))

    loudness = one(*split[0])
    for cut in split[1:]:
        loudness = loudness * one(*cut)
    return loudness


def routed_block(key, own, number, rows, number_of, top, most, skew):
    sequence = jax.random.permutation(key, number_of)
    packed, ordinary = shares(number_of, rows * top, most, skew, True), shares(number_of, rows * top, most, skew, False)
    places = jnp.arange(number_of)

    def named(tallies, rotation):
        used = int((tallies > 0).sum())
        fixed = max(1, used // 4)
        passed = fixed + (places - fixed + rotation * (used - fixed)) % max(1, number_of - fixed)
        return jnp.zeros((number_of,), jnp.int32).at[sequence[jnp.where(places < fixed, places, passed)]].set(jnp.asarray(tallies, jnp.int32))

    tallies = jnp.where(number % 4 == 0, named(packed, number // 4), named(ordinary, number - number // 4 - 1))
    mixed = jax.random.permutation(jax.random.fold_in(own, 3), number_of)
    donor, sink = mixed[0:number_of // 2 * 2:2], mixed[1:number_of // 2 * 2:2]
    slack = jnp.minimum(tallies[donor] - 1, most - tallies[sink]) // 2
    slack = jnp.where((donor == sequence[0]) | (sink == sequence[0]) | (tallies[sink] == 0), 0, jnp.maximum(slack, 0))
    passed = jax.random.randint(jax.random.fold_in(own, 4), (number_of // 2,), 0, 1 << 20) % (slack + 1)
    tallies = tallies.at[donor].add(-passed).at[sink].add(passed)
    items = jnp.searchsorted(jnp.cumsum(tallies), jnp.arange(rows * top), side="right").astype(jnp.int32)
    listing = items.reshape(top, rows).T
    listing = listing[jax.random.permutation(jax.random.fold_in(own, 1), rows)]
    rotation = jax.random.randint(jax.random.fold_in(own, 2), (rows, 1), 0, top)
    return jnp.take_along_axis(listing, (jnp.arange(top)[None, :] + rotation) % top, axis=1)


def shares(amount, total, limit, skew, full):
    portions = [(1 << 20) // math.isqrt(standing ** skew) + 1 for standing in range(1, amount + 1)]
    largest = limit if full else min(limit, max(-(-total // amount), total * portions[0] // sum(portions)))
    least = 1 if total - largest >= amount - 1 else 0
    counts, surplus = [largest] + [least] * (amount - 1), total - largest - least * (amount - 1)
    while surplus > 0:
        movable = [i for i in range(1, amount) if counts[i] < largest] or [i for i in range(1, amount) if counts[i] < limit]
        mass, remaining = sum([portions[i] for i in movable]), surplus
        for i in movable:
            addition = min(limit - counts[i], max(1, remaining * portions[i] // mass), surplus)
            counts[i] = counts[i] + addition
            surplus = surplus - addition
    return np.array(counts)


def noise(own_key, extent, scale, reach, split=(), kind=jnp.bfloat16):
    entries = scale * jax.random.normal(own_key, extent, jnp.float32)
    if split:
        entries = entries * level_of(own_key, extent, split, -0.22, 0.18)
    return jnp.clip(entries, -reach, reach).astype(kind)


def setup_inputs(seed: int = 0) -> dict:
    seeds = jax.random.split(jax.random.key(seed), 14)
    query_input = noise(seeds[0], (SEQ, HEADS * HD), 1.0, 6.0, ((0, 16), (1, 16)))
    key_input = noise(seeds[1], (SEQ, HEADS * HD), 1.0, 6.0, ((0, 16), (1, 16)))
    value_input = noise(seeds[2], (SEQ, HEADS * HD), 1.0, 6.0, ((0, 16), (1, 16)))
    gate_logits = noise(seeds[3], (2, SEQ, HEADS), 1.5, 6.0, ((1, 16), (2, 16)), jnp.float32)
    comp_weight = noise(seeds[4], (2, BLOCK, HEADS), 1.2, 6.0, ((2, 16),), jnp.float32)
    out_proj = noise(seeds[5], (HEADS * HD, D), (HEADS * HD) ** -0.5, 0.0625, ((0, 16), (1, 16)))
    residual_in = noise(seeds[6], (SEQ, D), 0.5, 3.0, ((0, 256),))
    ffn_gain = jnp.clip(1.0 + 0.15 * jax.random.normal(seeds[7], (D,), jnp.float32), 0.25, 1.75)
    expert_ids_keys = jax.random.split(jax.random.fold_in(seeds[8], 1), SEQ // (TOK_DEV // N_EXP))
    expert_ids_turns = jax.random.permutation(jax.random.fold_in(seeds[8], 3), SEQ // (TOK_DEV // N_EXP))
    expert_ids = jax.vmap(lambda own, number: routed_block(jax.random.fold_in(seeds[8], 2), own, number, TOK_DEV // N_EXP, EXPERTS, TOP, CAP, 2))(expert_ids_keys, expert_ids_turns).reshape((SEQ, TOP))
    route_gates = jnp.clip(0.2 + 0.8 * jax.random.uniform(seeds[9], (SEQ, TOP), jnp.float32) ** level_of(seeds[9], (SEQ, TOP), ((0, 256),), -0.2, 0.2), 0.2, 1.0)
    expert_gate = noise(seeds[10], (EXPERTS, D, FF), D ** -0.5, 0.0625, ((0, 16), (2, 16)))
    expert_up = noise(seeds[11], (EXPERTS, D, FF), D ** -0.5, 0.0625, ((0, 16), (2, 16)))
    expert_down = noise(seeds[12], (EXPERTS, FF, D), FF ** -0.5, 0.125, ((0, 16), (1, 16)))
    return dict(query_input=query_input, key_input=key_input, value_input=value_input, gate_logits=gate_logits, comp_weight=comp_weight, out_proj=out_proj, residual_in=residual_in, ffn_gain=ffn_gain, expert_ids=expert_ids, route_gates=route_gates, expert_gate=expert_gate, expert_up=expert_up, expert_down=expert_down)


score_gain = 2.0
norm_eps = 1e-06

def head_norm(matrix, head_width):
    row_count = matrix.shape[0]
    shaped = matrix.reshape(row_count, -1, head_width).astype(jnp.float32)
    scaled = shaped * lax.rsqrt(lax.optimization_barrier(jnp.mean(shaped * shaped, axis=2, keepdims=True)) + norm_eps)
    return scaled.reshape(row_count, -1)

def compress(extended, position_weights, head_width):
    stride_len = position_weights.shape[0] // 2
    head_count = position_weights.shape[1]
    blocks = extended.reshape(-1, stride_len, head_count, head_width).astype(jnp.float32)
    first_half = jnp.einsum('nshd,sh->nhd', blocks[:-1], position_weights[:stride_len], precision=lax.Precision.HIGHEST)
    second_half = jnp.einsum('nshd,sh->nhd', blocks[1:], position_weights[stride_len:], precision=lax.Precision.HIGHEST)
    return (first_half + second_half).reshape(blocks.shape[0] - 1, head_count * head_width)

def reference(query_input, key_input, value_input, gate_logits, comp_weight, out_proj, residual_in, ffn_gain, expert_ids, route_gates, expert_gate, expert_up, expert_down):
    scale = score_gain / math.sqrt(HD)
    query_norm = head_norm(query_input, HD).astype(jnp.bfloat16)
    key_norm = head_norm(key_input, HD).astype(jnp.bfloat16)
    tail_rows = jnp.zeros((STRIDE, HEADS * HD), jnp.bfloat16)
    comp_keys = head_norm(compress(jnp.concatenate([key_input, tail_rows], 0), comp_weight[0], HD), HD).astype(jnp.bfloat16)
    comp_values = compress(jnp.concatenate([value_input, tail_rows], 0), comp_weight[1], HD).astype(jnp.bfloat16)
    positions = jnp.arange(SEQ, dtype=jnp.int32)
    query_heads = query_norm.reshape(SEQ, HEADS, HD).astype(jnp.float32)
    comp_count = comp_keys.shape[0]
    scores = jnp.einsum('thd,nhd->htn', query_heads, comp_keys.reshape(comp_count, HEADS, HD).astype(jnp.float32), precision=lax.Precision.HIGHEST)
    block_end = jnp.arange(comp_count, dtype=jnp.int32) * STRIDE + BLOCK - 1
    visible = block_end[None, :] <= positions[:, None]
    weights = jnp.where(visible[None], jnp.exp(scale * scores), 0.0)
    cmp_total = lax.optimization_barrier(jnp.sum(weights, axis=2)).T
    rounded = lax.optimization_barrier(weights.astype(jnp.bfloat16)).astype(jnp.float32)
    cmp_sum = jnp.einsum('htn,nhd->thd', rounded, comp_values.reshape(comp_count, HEADS, HD).astype(jnp.float32), precision=lax.Precision.HIGHEST)
    no_block = (positions < BLOCK - 1).astype(jnp.float32)
    cmp_out = cmp_sum / (cmp_total + no_block[:, None])[:, :, None]
    key_padded = jnp.concatenate([jnp.zeros((WINDOW, HEADS * HD), jnp.bfloat16), key_norm], 0)
    value_padded = jnp.concatenate([jnp.zeros((WINDOW, HEADS * HD), jnp.bfloat16), value_input], 0)

    def window_block(block_index):
        first_row = (block_index * TOK_DEV).astype(jnp.int32)
        block_queries = lax.dynamic_slice_in_dim(query_norm, first_row, TOK_DEV, 0).reshape(TOK_DEV, HEADS, HD).astype(jnp.float32)
        block_keys = lax.dynamic_slice_in_dim(key_padded, first_row, WINDOW + TOK_DEV, 0).reshape(-1, HEADS, HD).astype(jnp.float32)
        block_values = lax.dynamic_slice_in_dim(value_padded, first_row, WINDOW + TOK_DEV, 0).reshape(-1, HEADS, HD).astype(jnp.float32)
        query_pos = first_row + jnp.arange(TOK_DEV, dtype=jnp.int32)
        key_pos = first_row - WINDOW + jnp.arange(WINDOW + TOK_DEV, dtype=jnp.int32)
        local_scores = jnp.einsum('thd,shd->hts', block_queries, block_keys, precision=lax.Precision.HIGHEST)
        inside = (key_pos[None, :] <= query_pos[:, None]) & (key_pos[None, :] > query_pos[:, None] - WINDOW) & (key_pos[None, :] >= 0)
        local_weights = jnp.where(inside[None], jnp.exp(scale * local_scores), 0.0)
        local_total = lax.optimization_barrier(jnp.sum(local_weights, axis=2)).T
        local_rounded = lax.optimization_barrier(local_weights.astype(jnp.bfloat16)).astype(jnp.float32)
        local_sum = jnp.einsum('hts,shd->thd', local_rounded, block_values, precision=lax.Precision.HIGHEST)
        return local_sum / local_total[:, :, None]
    win_out = lax.map(window_block, jnp.arange(N_CTX, dtype=jnp.int32)).reshape(SEQ, HEADS, HD)
    branch_gates = jax.nn.sigmoid(gate_logits)
    attended = (branch_gates[0][:, :, None] * cmp_out + branch_gates[1][:, :, None] * win_out).reshape(SEQ, -1).astype(jnp.bfloat16)
    hidden_state = residual_in.astype(jnp.float32) + jnp.dot(attended, out_proj, preferred_element_type=jnp.float32)
    mean_square = lax.optimization_barrier(jnp.mean(hidden_state * hidden_state, axis=1, keepdims=True))
    normed = (hidden_state * lax.rsqrt(mean_square + norm_eps) * ffn_gain).astype(jnp.bfloat16)
    token_share = TOK_DEV // N_EXP
    device_count = N_CTX * N_EXP
    grouped_ids = expert_ids.reshape(device_count, token_share * TOP)
    chosen = (grouped_ids[:, :, None] == jnp.arange(EXPERTS, dtype=jnp.int32)[None, None, :]).astype(jnp.int32)
    slots = lax.optimization_barrier(jnp.sum((jnp.cumsum(chosen, axis=1) - chosen) * chosen, axis=2))
    row_index = (jnp.arange(device_count, dtype=jnp.int32)[:, None] * CAP + slots).reshape(-1)
    expert_index = grouped_ids.reshape(-1)
    token_index = jnp.arange(SEQ * TOP, dtype=jnp.int32) // TOP
    buffers = jnp.zeros((EXPERTS, device_count * CAP, D), jnp.bfloat16).at[expert_index, row_index].set(normed[token_index])
    ff_block = FF // N_CTX

    def run_expert(operands):
        expert_rows, gate_w, up_w, down_w = operands
        gate_part = jnp.dot(expert_rows, gate_w, preferred_element_type=jnp.float32)
        up_part = jnp.dot(expert_rows, up_w, preferred_element_type=jnp.float32)
        activated = (jax.nn.silu(gate_part) * up_part).astype(jnp.bfloat16)
        pieces = jnp.einsum('mcf,cfd->cmd', activated.reshape(-1, N_CTX, ff_block).astype(jnp.float32), down_w.reshape(N_CTX, ff_block, D).astype(jnp.float32), precision=lax.Precision.HIGHEST)
        rounded_pieces = lax.optimization_barrier(pieces.astype(jnp.bfloat16)).astype(jnp.float32)
        return lax.optimization_barrier(jnp.sum(rounded_pieces, axis=0)).astype(jnp.bfloat16)
    outputs = lax.map(run_expert, (buffers, expert_gate, expert_up, expert_down))
    picked = outputs[expert_index, row_index].reshape(SEQ, TOP, D).astype(jnp.float32)
    moe_out = lax.optimization_barrier(jnp.sum(route_gates[:, :, None] * picked, axis=1))
    return (hidden_state + moe_out).astype(jnp.bfloat16)
```

```python
import math

import jax
import jax.numpy as jnp
from jax import lax
from jax.experimental import pallas as pl
from jax.experimental.pallas import tpu as pltpu
from jax.sharding import PartitionSpec as P

MESH = pl.DeviceIdType.MESH
BF = jnp.bfloat16
F32 = jnp.float32
WINDOW = 512
SCALE = 2.0 / math.sqrt(128)
EPS = 1e-06


def place():
    c = lax.axis_index("ctx")
    e = lax.axis_index("exp")
    return lax.div(c, 2), lax.rem(c, 2), e


def greet(devices):
    bar = pltpu.get_barrier_semaphore()
    for d in devices:
        pl.semaphore_signal(bar, inc=1, device_id=d, device_id_type=MESH)
    pl.semaphore_wait(bar, len(devices))


def rcopy(src, dst, ss, rs, dev):
    return pltpu.make_async_remote_copy(
        src_ref=src, dst_ref=dst, send_sem=ss, recv_sem=rs, device_id=dev, device_id_type=MESH
    )


def unit(x):
    return x * lax.rsqrt(jnp.mean(x * x, axis=1, keepdims=True) + EPS)


def attention(
    q, k, v, g, cw, wo, eg, eu, ed,
    att, wpair, sg, su, sd,
    kb, vb, qb, gb, hk, hv, cb, tb, ss, rs,
):
    z, core, e = place()
    other = 1 - core
    up, down = lax.rem(z + 1, 8), lax.rem(z + 7, 8)
    sib = (2 * z + other, e)
    peers = [(2 * lax.rem(z + j, 8) + core, e) for j in range(1, 8)]
    greet([sib, (2 * up + other, e), (2 * down + other, e)] + peers)

    off_other = pl.multiple_of(other * 256, 256)
    off = pl.multiple_of(core * 256, 256)
    near = []
    for kk in range(2):
        for a, (src, dst) in enumerate(((k, kb), (v, vb))):
            near.append(
                rcopy(
                    src.at[:, pl.ds(kk * 256, 256)],
                    dst.at[1, core],
                    ss.at[8 + 2 * kk + a],
                    rs.at[8 + 2 * core + a],
                    (2 * up + kk, e),
                )
            )
    halo = []
    for kk in range(2):
        for a, (src, dst) in enumerate(((k, hk), (v, hv))):
            halo.append(
                rcopy(
                    src.at[pl.ds(0, 16), pl.ds(kk * 256, 256)],
                    dst,
                    ss.at[16 + 2 * kk + a],
                    rs.at[16 + a],
                    (2 * down + kk, e),
                )
            )

    @pl.when(core == 0)
    def _():
        for cp in halo:
            cp.start()

    swap = [
        rcopy(k.at[:, pl.ds(off_other, 256)], kb.at[2, core], ss.at[0], rs.at[0], sib),
        rcopy(v.at[:, pl.ds(off_other, 256)], vb.at[2, core], ss.at[1], rs.at[1], sib),
        rcopy(q.at[:, pl.ds(off_other, 256)], qb.at[core], ss.at[2], rs.at[2], sib),
        rcopy(g, gb.at[core], ss.at[3], rs.at[3], sib),
    ]
    for cp in swap:
        cp.start()
    for cp in near:
        cp.start()
    share = [
        rcopy(wo, wpair.at[core], ss.at[4], rs.at[4], sib),
        rcopy(eg, sg, ss.at[5], rs.at[5], sib),
        rcopy(eu, su, ss.at[6], rs.at[6], sib),
        rcopy(ed, sd, ss.at[7], rs.at[7], sib),
    ]
    for cp in share:
        cp.start()

    kb[2, core] = k[:, pl.ds(off, 256)]
    vb[2, core] = v[:, pl.ds(off, 256)]
    qb[core] = q[:, pl.ds(off, 256)]
    gb[core] = g[...]
    wpair[core] = wo[...]

    for cp in swap:
        cp.wait_recv()
    halo[0].wait_recv()
    halo[1].wait_recv()

    for a, (blocks, tail) in enumerate(((kb, hk), (vb, hv))):
        for h in range(2):
            hs = h * 128
            last = jnp.where(z == 7, 0.0, tail[:, hs : hs + 128].astype(F32))
            x = jnp.concatenate(
                [
                    blocks[2, 0, :, hs : hs + 128].astype(F32),
                    blocks[2, 1, :, hs : hs + 128].astype(F32),
                    last,
                ],
                0,
            ).reshape(17, 16, 128)
            w = cw[a, 2 * core + h]
            y = jnp.sum(x[:16] * w[None, :16], axis=1) + jnp.sum(x[1:] * w[None, 16:], axis=1)
            if a == 0:
                y = unit(y)
            cb[z, a, :, hs : hs + 128] = y.astype(BF)
    comps = [
        rcopy(cb.at[z], cb.at[z], ss.at[20 + j], rs.at[20 + j], peers[j - 1]) for j in range(1, 8)
    ]
    for cp in comps:
        cp.start()

    relay = []
    for s in range(2):
        for a, buf in enumerate((kb, vb)):
            rcopy(buf.at[1, s], buf.at[1, s], ss.at[8], rs.at[8 + 2 * s + a], sib).wait_recv()
            cp = rcopy(
                buf.at[1, s],
                buf.at[0, s],
                ss.at[12 + 2 * s + a],
                rs.at[12 + 2 * s + a],
                (2 * up + core, e),
            )
            cp.start()
            relay.append(cp)
    for cp in comps:
        cp.wait_recv()
    for cp in relay:
        cp.wait_recv()

    pos = z * 256 + lax.broadcasted_iota(jnp.int32, (256, 1), 0)
    block_end = lax.broadcasted_iota(jnp.int32, (1, 128), 1) * 16 + 31
    key_pos = (z - 2) * 256 + lax.broadcasted_iota(jnp.int32, (1, 768), 1)
    lane = lax.broadcasted_iota(jnp.int32, (1, 128), 1)
    gates = gb[...].reshape(256, 128)
    gates = 1.0 / (1.0 + jnp.exp(-gates))
    for h in range(2):
        hs = h * 128
        qn = unit(qb[:, :, hs : hs + 128].reshape(256, 128).astype(F32)).astype(BF)
        ck = cb[:, 0, :, hs : hs + 128].reshape(128, 128)
        cv = cb[:, 1, :, hs : hs + 128].reshape(128, 128)
        s1 = lax.dot_general(qn, ck, (((1,), (1,)), ((), ())), preferred_element_type=F32)
        w1 = jnp.where(block_end <= pos, jnp.exp(SCALE * s1), 0.0)
        t1 = jnp.sum(w1, axis=1, keepdims=True) + (pos < 31).astype(F32)
        o1 = jnp.dot(w1.astype(BF), cv, preferred_element_type=F32) / t1
        kn = unit(kb[:, :, :, hs : hs + 128].reshape(768, 128).astype(F32)).astype(BF)
        vn = vb[:, :, :, hs : hs + 128].reshape(768, 128)
        s2 = lax.dot_general(qn, kn, (((1,), (1,)), ((), ())), preferred_element_type=F32)
        inside = (key_pos <= pos) & (key_pos > pos - WINDOW) & (key_pos >= 0)
        w2 = jnp.where(inside, jnp.exp(SCALE * s2), 0.0)
        t2 = jnp.sum(w2, axis=1, keepdims=True)
        o2 = jnp.dot(w2.astype(BF), vn, preferred_element_type=F32) / t2
        g1 = jnp.sum(jnp.where(lane == 2 * core + h, gates, 0.0), axis=1, keepdims=True)
        g2 = jnp.sum(jnp.where(lane == 4 + 2 * core + h, gates, 0.0), axis=1, keepdims=True)
        tb[:, :, hs : hs + 128] = (g1 * o1 + g2 * o2).astype(BF).reshape(2, 128, 128)
    back = rcopy(tb.at[other], att.at[core], ss.at[28], rs.at[28], sib)
    back.start()
    att[core] = tb[core]

    @pl.when(core == 0)
    def _():
        for cp in halo:
            cp.wait_send()

    for cp in swap + near + comps + relay:
        cp.wait_send()
    for cp in share + [back]:
        cp.wait()


def run_attention(q, k, v, g, cw, wo, eg, eu, ed):
    vm = pl.BlockSpec(memory_space=pltpu.VMEM)
    hbm = pl.BlockSpec(memory_space=pl.ANY)
    return pl.pallas_call(
        attention,
        out_shape=(
            jax.ShapeDtypeStruct((2, 128, 256), BF),
            jax.ShapeDtypeStruct((2, 512, 448), BF),
            jax.ShapeDtypeStruct(eg.shape, BF),
            jax.ShapeDtypeStruct(eu.shape, BF),
            jax.ShapeDtypeStruct(ed.shape, BF),
        ),
        in_specs=[vm] * 6 + [hbm] * 3,
        out_specs=(vm, vm, hbm, hbm, hbm),
        scratch_shapes=[
            pltpu.VMEM((3, 2, 128, 256), BF),
            pltpu.VMEM((3, 2, 128, 256), BF),
            pltpu.VMEM((2, 128, 256), BF),
            pltpu.VMEM((2, 128, 128), F32),
            pltpu.VMEM((16, 256), BF),
            pltpu.VMEM((16, 256), BF),
            pltpu.VMEM((8, 2, 16, 256), BF),
            pltpu.VMEM((2, 128, 256), BF),
            pltpu.SemaphoreType.DMA((29,)),
            pltpu.SemaphoreType.DMA((29,)),
        ],
        compiler_params=pltpu.CompilerParams(
            collective_id=1, has_side_effects=True, vmem_limit_bytes=32 << 20
        ),
        name="attention",
    )(q, k, v, g, cw, wo, eg, eu, ed)


def z_ring(buf, z, core, e, ss, rs):
    up, down = lax.rem(z + 1, 8), lax.rem(z + 7, 8)

    def copy(way, step, chunk):
        block = lax.rem(z + 8 - step, 8) if way == 0 else lax.rem(z + step, 8)
        slot = way * 7 + 2 * step + (chunk if step < 3 else 0)
        return rcopy(
            buf.at[block, chunk],
            buf.at[block, chunk],
            ss.at[slot],
            rs.at[slot],
            (2 * (up if way == 0 else down) + core, e),
        )

    def chunks(way, step):
        return (0, 1) if step < 3 else ((0,) if way == 0 else (1,))

    return copy, chunks


def gather_start(copy, chunks, sent):
    for chunk in (0, 1):
        for way in (0, 1):
            cp = copy(way, 0, chunk)
            cp.start()
            sent.append(cp)


def gather_step(copy, chunks, step, sent):
    for chunk in (0, 1):
        for way in (0, 1):
            if chunk in chunks(way, step):
                copy(way, step, chunk).wait_recv()
                if step < 3 and chunk in chunks(way, step + 1):
                    cp = copy(way, step + 1, chunk)
                    cp.start()
                    sent.append(cp)


def project(
    att, wp,
    hid,
    xb, pb, a1, a2, a3, sb, c1, c2, c3, rb, ss, rs, s1, r1, s2, r2, s3, r3,
):
    z, core, e = place()
    ex, ey = lax.div(e, 4), lax.rem(e, 4)
    c = 2 * z + core
    ring = [
        (ex, lambda t: (c, 4 * lax.rem(t, 4) + ey)),
        (ey, lambda t: (c, 4 * ex + lax.rem(t, 4))),
    ]
    zp = [(2 * lax.rem(z + j, 8) + core, e) for j in range(1, 8)]
    greet([dev(p + j) for p, dev in ring for j in (1, 3)] + zp)

    xb[z] = att[...]
    copy, chunks = z_ring(xb, z, core, e, ss, rs)
    sent = []
    gather_start(copy, chunks, sent)

    def partial(block, r):
        x0, x1 = xb[block, 0], xb[block, 1]
        parts = [
            jnp.dot(x0, wp[n, :256], preferred_element_type=F32)
            + jnp.dot(x1, wp[n, 256:], preferred_element_type=F32)
            for n in range(2)
        ]
        pb[r] = jnp.concatenate(parts, 1).reshape(4, 4, 8, 896).astype(BF)

    partial(z, 0)
    for step in range(4):
        gather_step(copy, chunks, step, sent)
        partial(lax.rem(z + step + 1, 8), step + 1)
        if step < 3:
            partial(lax.rem(z + 7 - step, 8), 7 - step)

    def ring_sum(which, half, piece, first, second, mixed, ssem, rsem):
        p, dev = ring[which]
        nxt, prv = dev(p + 1), dev(p + 3)
        base = 6 * half
        far, nt, pt = lax.rem(p + 2, 4), lax.rem(p + 1, 4), lax.rem(p + 3, 4)
        cps = [
            rcopy(piece(far, 0), first.at[half, 0], ssem.at[base], rsem.at[base], nxt),
            rcopy(piece(far, 1), first.at[half, 1], ssem.at[base + 1], rsem.at[base + 1], prv),
            rcopy(piece(nt, 1), second.at[half, 0, pl.ds(2, 2)], ssem.at[base + 2], rsem.at[base + 2], nxt),
            rcopy(piece(pt, 0), second.at[half, 1, pl.ds(0, 2)], ssem.at[base + 3], rsem.at[base + 3], prv),
            rcopy(mixed.at[half, 0], second.at[half, 0, pl.ds(0, 2)], ssem.at[base + 4], rsem.at[base + 4], nxt),
            rcopy(mixed.at[half, 1], second.at[half, 1, pl.ds(2, 2)], ssem.at[base + 5], rsem.at[base + 5], prv),
        ]

        def start():
            for cp in cps[:4]:
                cp.start()

        def middle():
            cps[0].wait_recv()
            mixed[half, 0] = (first[half, 0].astype(F32) + piece(nt, 0)[...].astype(F32)).astype(BF)
            cps[4].start()
            cps[1].wait_recv()
            mixed[half, 1] = (first[half, 1].astype(F32) + piece(pt, 1)[...].astype(F32)).astype(BF)
            cps[5].start()

        def end():
            for cp in cps[2:]:
                cp.wait_recv()
            return [
                piece(p, n)[...].astype(F32)
                + second[half, 0, 2 * n : 2 * n + 2].astype(F32)
                + second[half, 1, 2 * n : 2 * n + 2].astype(F32)
                for n in range(2)
            ]

        def drain():
            for cp in cps:
                cp.wait_send()

        return start, middle, end, drain

    def piece_a(t, n):
        return pb.at[pl.ds(2 * n, 2), t]

    def piece_b(t, n):
        return pb.at[pl.ds(4 + 2 * n, 2), :, t]

    def piece_of(half):
        return lambda t, n: sb.at[half, pl.ds(2 * n, 2), t]

    wide = [
        ring_sum(0, 0, piece_a, a1, a2, a3, s1, r1),
        ring_sum(1, 1, piece_b, a1, a2, a3, s1, r1),
    ]
    thin = [
        ring_sum(1, 0, piece_of(0), c1, c2, c3, s2, r2),
        ring_sum(0, 1, piece_of(1), c1, c2, c3, s2, r2),
    ]
    for r in wide:
        r[0]()
    for r in wide:
        r[1]()
    for half in range(2):
        lo, hi = wide[half][2]()
        sb[half, 0:2] = lo.astype(BF)
        sb[half, 2:4] = hi.astype(BF)
        thin[half][0]()
    for r in thin:
        r[1]()
    out = []
    for half in range(2):
        lo, hi = thin[half][2]()
        rb[4 * half : 4 * half + 2] = lo.astype(BF)
        rb[4 * half + 2 : 4 * half + 4] = hi.astype(BF)
        for j in range(4 * half, 4 * half + 4):
            if j:
                cp = rcopy(rb.at[j], hid.at[z], s3.at[j], r3.at[j], zp[j - 1])
                cp.start()
                out.append(cp)
    hid[z] = rb[0]
    for cp in out:
        cp.wait()
    for cp in sent:
        cp.wait_send()
    for r in wide + thin:
        r[3]()


def run_project(att, wp):
    vm = pl.BlockSpec(memory_space=pltpu.VMEM)
    return pl.pallas_call(
        project,
        out_shape=jax.ShapeDtypeStruct((8, 8, 896), BF),
        in_specs=[vm] * 2,
        out_specs=vm,
        scratch_shapes=[
            pltpu.VMEM((8, 2, 128, 256), BF),
            pltpu.VMEM((8, 4, 4, 8, 896), BF),
            pltpu.VMEM((2, 2, 2, 4, 8, 896), BF),
            pltpu.VMEM((2, 2, 4, 4, 8, 896), BF),
            pltpu.VMEM((2, 2, 2, 4, 8, 896), BF),
            pltpu.VMEM((2, 4, 4, 8, 896), BF),
            pltpu.VMEM((2, 2, 2, 8, 896), BF),
            pltpu.VMEM((2, 2, 4, 8, 896), BF),
            pltpu.VMEM((2, 2, 2, 8, 896), BF),
            pltpu.VMEM((8, 8, 896), BF),
            pltpu.SemaphoreType.DMA((14,)),
            pltpu.SemaphoreType.DMA((14,)),
            pltpu.SemaphoreType.DMA((12,)),
            pltpu.SemaphoreType.DMA((12,)),
            pltpu.SemaphoreType.DMA((12,)),
            pltpu.SemaphoreType.DMA((12,)),
            pltpu.SemaphoreType.DMA((8,)),
            pltpu.SemaphoreType.DMA((8,)),
        ],
        compiler_params=pltpu.CompilerParams(
            collective_id=2, has_side_effects=True, vmem_limit_bytes=40 << 20
        ),
        name="project",
    )(att, wp)


def experts(
    outg, eg, eu, ed, sg, su, sd,
    ret,
    gw, dw, arr, xb, ob, rv, mx, fs, ro, ls, s0, r0, ss, rs, s1, r1, s2, r2,
):
    z, core, e = place()
    c = 2 * z + core
    up, down = (2 * lax.rem(z + 1, 8) + core, e), (2 * lax.rem(z + 7, 8) + core, e)
    plane = [(c, lax.rem(e + j, 16)) for j in range(1, 16)]
    greet(plane + [up, down])

    go = []
    for j in range(1, 16):
        cp = rcopy(outg.at[lax.rem(e + j, 16)], arr.at[e], s0.at[j], r0.at[j], plane[j - 1])
        cp.start()
        go.append(cp)
    load = [
        pltpu.make_async_copy(src, gw.at[:, pl.ds(128 * n, 128)], ls.at[n])
        for n, src in enumerate((eg, sg, eu, su))
    ] + [
        pltpu.make_async_copy(src, dw.at[pl.ds(128 * n, 128), :], ls.at[4 + n])
        for n, src in enumerate((ed, sd))
    ]
    for cp in load:
        cp.start()
    arr[e] = outg[e]
    for cp in go:
        cp.wait_recv()
    for i in range(16):
        fs[2 * i : 2 * i + 2, :] = arr[i].astype(F32)
    xb[z, 0] = fs[0:16].astype(BF)
    xb[z, 1] = fs[16:32].astype(BF)

    copy, chunks = z_ring(xb, z, core, e, ss, rs)
    sent = []
    gather_start(copy, chunks, sent)
    for cp in load:
        cp.wait()

    def work(a, b):
        x = jnp.concatenate([xb[a, 0], xb[a, 1], xb[b, 0], xb[b, 1]], 0)
        y = jnp.dot(x, gw[...], preferred_element_type=F32)
        gate, lift = y[:, :256], y[:, 256:]
        act = (gate / (1.0 + jnp.exp(-gate)) * lift).astype(BF)

        @pl.loop(0, 7)
        def _(n):
            cols = pl.ds(pl.multiple_of(n * 1024, 1024), 1024)
            out = jnp.dot(act, dw[:, cols], preferred_element_type=F32).astype(BF)
            ob[a, 0, :, cols] = out[0:16]
            ob[a, 1, :, cols] = out[16:32]
            ob[b, 0, :, cols] = out[32:48]
            ob[b, 1, :, cols] = out[48:64]

    for step in range(4):
        gather_step(copy, chunks, step, sent)
        if step < 3:
            work(lax.rem(z + step + 1, 8), lax.rem(z + 7 - step, 8))
        else:
            work(lax.rem(z + 4, 8), z)

    def leg(way, slot, src):
        return rcopy(
            src, rv.at[way, slot], s1.at[way * 7 + slot], r1.at[way * 7 + slot], up if way == 0 else down
        )

    def mine(way, dist, first):
        block = lax.rem(z + dist, 8) if way == 0 else lax.rem(z + 8 - dist, 8)
        chunk = first if way == 0 else 1 - first
        return ob.at[block, chunk]

    back = []

    def send(way, slot, src):
        cp = leg(way, slot, src)
        cp.start()
        back.append(cp)

    for way in (0, 1):
        send(way, 0, mine(way, 4, 0))
    for way in (0, 1):
        send(way, 2, mine(way, 3, 1))
    for slot, dist, first, source in ((1, 3, 0, 0), (3, 2, 0, 1), (4, 2, 1, 2), (5, 1, 0, 3), (6, 1, 1, 4)):
        for way in (0, 1):
            leg(way, source, rv.at[way, source]).wait_recv()
            mx[way, slot] = (
                rv[way, source].astype(F32) + mine(way, dist, first)[...].astype(F32)
            ).astype(BF)
            send(way, slot, mx.at[way, slot])
    for chunk in range(2):
        total = ob[z, chunk].astype(F32)
        for way in (0, 1):
            slot = 5 + (chunk if way == 0 else 1 - chunk)
            leg(way, slot, rv.at[way, slot]).wait_recv()
            total = total + rv[way, slot].astype(F32)
        fs[16 * chunk : 16 * chunk + 16] = total
    for i in range(16):
        ro[i] = fs[2 * i : 2 * i + 2, :].astype(BF)
    home = []
    for j in range(1, 16):
        cp = rcopy(ro.at[lax.rem(e + j, 16)], ret.at[e], s2.at[j], r2.at[j], plane[j - 1])
        cp.start()
        home.append(cp)
    ret[e] = ro[e]
    for cp in home:
        cp.wait()
    for cp in go + sent + back:
        cp.wait_send()


def run_experts(outg, eg, eu, ed, sg, su, sd):
    vm = pl.BlockSpec(memory_space=pltpu.VMEM)
    hbm = pl.BlockSpec(memory_space=pl.ANY)
    return pl.pallas_call(
        experts,
        out_shape=jax.ShapeDtypeStruct((16, 2, 7168), BF),
        in_specs=[vm] + [hbm] * 6,
        out_specs=vm,
        scratch_shapes=[
            pltpu.VMEM((7168, 512), BF),
            pltpu.VMEM((256, 7168), BF),
            pltpu.VMEM((16, 2, 7168), BF),
            pltpu.VMEM((8, 2, 16, 7168), BF),
            pltpu.VMEM((8, 2, 16, 7168), BF),
            pltpu.VMEM((2, 7, 16, 7168), BF),
            pltpu.VMEM((2, 7, 16, 7168), BF),
            pltpu.VMEM((32, 7168), F32),
            pltpu.VMEM((16, 2, 7168), BF),
            pltpu.SemaphoreType.DMA((6,)),
            pltpu.SemaphoreType.DMA((16,)),
            pltpu.SemaphoreType.DMA((16,)),
            pltpu.SemaphoreType.DMA((14,)),
            pltpu.SemaphoreType.DMA((14,)),
            pltpu.SemaphoreType.DMA((14,)),
            pltpu.SemaphoreType.DMA((14,)),
            pltpu.SemaphoreType.DMA((16,)),
            pltpu.SemaphoreType.DMA((16,)),
        ],
        compiler_params=pltpu.CompilerParams(
            collective_id=3, has_side_effects=True, vmem_limit_bytes=58 << 20
        ),
        name="experts",
    )(outg, eg, eu, ed, sg, su, sd)


def local(
    query_input,
    key_input,
    value_input,
    gate_logits,
    comp_weight,
    out_proj,
    residual_in,
    ffn_gain,
    expert_ids,
    route_gates,
    expert_gate,
    expert_up,
    expert_down,
):
    gates = jnp.pad(gate_logits.transpose(1, 0, 2).reshape(128, 8), ((0, 0), (0, 120)))
    cw = jnp.broadcast_to(comp_weight.transpose(0, 2, 1)[..., None], (2, 4, 32, 128))
    att, wpair, sg, su, sd = run_attention(
        query_input, key_input, value_input, gates, cw, out_proj,
        expert_gate[0], expert_up[0], expert_down[0],
    )
    projected = run_project(att, wpair)
    projected = projected.transpose(1, 0, 2).reshape(8, 7168).astype(F32)
    hidden_state = residual_in.astype(F32) + projected
    mean_square = jnp.mean(hidden_state * hidden_state, axis=1, keepdims=True)
    normed = (hidden_state * lax.rsqrt(mean_square + EPS) * ffn_gain).astype(BF)

    flat_ids = expert_ids.reshape(-1)
    chosen = (flat_ids[:, None] == jnp.arange(16, dtype=jnp.int32)[None, :]).astype(jnp.int32)
    slots = jnp.sum((jnp.cumsum(chosen, axis=0) - chosen) * chosen, axis=1)
    targets = (flat_ids * 2 + slots).reshape(8, 2)
    slot_range = jnp.arange(32, dtype=jnp.int32)
    dispatch_map = jnp.sum(
        (slot_range[:, None, None] == targets[None, :, :]).astype(F32), axis=2
    ).astype(BF)
    outgoing = (
        jnp.dot(dispatch_map, normed, preferred_element_type=F32).astype(BF).reshape(16, 2, 7168)
    )
    returned = run_experts(
        outgoing, expert_gate[0], expert_up[0], expert_down[0], sg, su, sd
    ).reshape(32, 7168)
    combine_map = jnp.sum(
        jnp.where(slot_range[None, None, :] == targets[:, :, None], route_gates[:, :, None], 0.0),
        axis=1,
    )
    moe_out = jnp.dot(combine_map, returned.astype(F32), precision=lax.Precision.HIGHEST)
    return (hidden_state + moe_out).astype(BF)


def solution(mesh):
    in_specs = (
        P("ctx", "exp"),
        P("ctx", "exp"),
        P("ctx", "exp"),
        P(None, "ctx", "exp"),
        P(None, None, "exp"),
        P("exp", "ctx"),
        P(("ctx", "exp"), None),
        P(),
        P(("ctx", "exp"), None),
        P(("ctx", "exp"), None),
        P("exp", None, "ctx"),
        P("exp", None, "ctx"),
        P("exp", "ctx", None),
    )
    out_specs = P(("ctx", "exp"), None)
    return jax.shard_map(local, mesh=mesh, in_specs=in_specs, out_specs=out_specs, check_vma=False)
```

```python
import math

import jax
import jax.numpy as jnp
from jax import lax
from jax.experimental import pallas as pl
from jax.experimental.pallas import tpu as pltpu
from jax.sharding import PartitionSpec as P

MESH = pl.DeviceIdType.MESH
BF = jnp.bfloat16
F32 = jnp.float32
WINDOW = 512
SCALE = 2.0 / math.sqrt(128)
EPS = 1e-06


def place():
    c = lax.axis_index("ctx")
    e = lax.axis_index("exp")
    return lax.div(c, 2), lax.rem(c, 2), e


def greet(devices):
    bar = pltpu.get_barrier_semaphore()
    for d in devices:
        pl.semaphore_signal(bar, inc=1, device_id=d, device_id_type=MESH)
    pl.semaphore_wait(bar, len(devices))


def rcopy(src, dst, ss, rs, dev):
    return pltpu.make_async_remote_copy(
        src_ref=src, dst_ref=dst, send_sem=ss, recv_sem=rs, device_id=dev, device_id_type=MESH
    )


def unit(x):
    return x * lax.rsqrt(jnp.mean(x * x, axis=1, keepdims=True) + EPS)


def attention(
    q, k, v, g, cw, wo,
    att, wpair,
    kb, vb, qb, gb, gs, hk, hv, cb, tb, ss, rs, ls,
):
    z, core, e = place()
    other = 1 - core
    up, down = lax.rem(z + 1, 8), lax.rem(z + 7, 8)
    sib = (2 * z + other, e)
    peers = [(2 * lax.rem(z + j, 8) + core, e) for j in range(1, 8)]
    greet([sib, (2 * up + other, e), (2 * down + other, e)] + peers)

    off_other = pl.multiple_of(other * 256, 256)
    off = pl.multiple_of(core * 256, 256)
    near = []
    for kk in range(2):
        for a, (src, dst) in enumerate(((k, kb), (v, vb))):
            near.append(
                rcopy(
                    src.at[:, pl.ds(kk * 256, 256)],
                    dst.at[1, core],
                    ss.at[8 + 2 * kk + a],
                    rs.at[8 + 2 * core + a],
                    (2 * up + kk, e),
                )
            )
    halo = []
    for kk in range(2):
        for a, (src, dst) in enumerate(((k, hk), (v, hv))):
            halo.append(
                rcopy(
                    src.at[pl.ds(0, 16), pl.ds(kk * 256, 256)],
                    dst,
                    ss.at[16 + 2 * kk + a],
                    rs.at[16 + a],
                    (2 * down + kk, e),
                )
            )

    @pl.when(core == 0)
    def _():
        for cp in halo:
            cp.start()

    rows = pl.ds(pl.multiple_of(core * 448, 64), 448)
    own = [
        pltpu.make_async_copy(k.at[:, pl.ds(off, 256)], kb.at[2, core], ls.at[0]),
        pltpu.make_async_copy(v.at[:, pl.ds(off, 256)], vb.at[2, core], ls.at[1]),
        pltpu.make_async_copy(q.at[:, pl.ds(off, 256)], qb.at[core], ls.at[2]),
        pltpu.make_async_copy(wo, wpair.at[rows], ls.at[3]),
    ]
    swap = [
        rcopy(k.at[:, pl.ds(off_other, 256)], kb.at[2, core], ss.at[0], rs.at[0], sib),
        rcopy(v.at[:, pl.ds(off_other, 256)], vb.at[2, core], ss.at[1], rs.at[1], sib),
        rcopy(q.at[:, pl.ds(off_other, 256)], qb.at[core], ss.at[2], rs.at[2], sib),
        rcopy(g, gb.at[core], ss.at[3], rs.at[3], sib),
    ]
    for cp in swap:
        cp.start()
    for cp in near:
        cp.start()
    for cp in own:
        cp.start()
    share = [
        rcopy(wo, wpair.at[rows], ss.at[4], rs.at[4], sib),
    ]
    for cp in share:
        cp.start()

    gb[core] = g[...]
    for cp in own:
        cp.wait()
    for cp in swap:
        cp.wait_recv()
    halo[0].wait_recv()
    halo[1].wait_recv()

    for a, (blocks, tail) in enumerate(((kb, hk), (vb, hv))):
        for h in range(2):
            hs = h * 128
            last = jnp.where(z == 7, 0.0, tail[:, hs : hs + 128].astype(F32))
            x = jnp.concatenate(
                [
                    blocks[2, 0, :, hs : hs + 128].astype(F32),
                    blocks[2, 1, :, hs : hs + 128].astype(F32),
                    last,
                ],
                0,
            ).reshape(17, 16, 128)
            w = cw[a, 2 * core + h]
            y = jnp.sum(x[:16] * w[None, :16], axis=1) + jnp.sum(x[1:] * w[None, 16:], axis=1)
            if a == 0:
                y = unit(y)
            cb[z, a, :, hs : hs + 128] = y.astype(BF)
    comps = [
        rcopy(cb.at[z], cb.at[z], ss.at[20 + j], rs.at[20 + j], peers[j - 1]) for j in range(1, 8)
    ]
    for cp in comps:
        cp.start()

    relay = []
    for s in range(2):
        for a, buf in enumerate((kb, vb)):
            rcopy(buf.at[1, s], buf.at[1, s], ss.at[8], rs.at[8 + 2 * s + a], sib).wait_recv()
            cp = rcopy(
                buf.at[1, s],
                buf.at[0, s],
                ss.at[12 + 2 * s + a],
                rs.at[12 + 2 * s + a],
                (2 * up + core, e),
            )
            cp.start()
            relay.append(cp)
    for cp in comps:
        cp.wait_recv()
    for cp in relay:
        cp.wait_recv()

    pos = z * 256 + lax.broadcasted_iota(jnp.int32, (256, 1), 0)
    block_end = lax.broadcasted_iota(jnp.int32, (1, 128), 1) * 16 + 31
    key_pos = (z - 2) * 256 + lax.broadcasted_iota(jnp.int32, (1, 768), 1)
    lane = lax.broadcasted_iota(jnp.int32, (1, 128), 1)
    gs[...] = jnp.zeros_like(gs)
    for n in range(2):
        gs[n, 0:4] = gb[n, 0]
        gs[n, 4:8] = gb[n, 1]
    gates = jnp.concatenate([gs[0].T, gs[1].T], 0)
    gates = 1.0 / (1.0 + jnp.exp(-gates))
    for h in range(2):
        hs = h * 128
        qn = unit(qb[:, :, hs : hs + 128].reshape(256, 128).astype(F32)).astype(BF)
        ck = cb[:, 0, :, hs : hs + 128].reshape(128, 128)
        cv = cb[:, 1, :, hs : hs + 128].reshape(128, 128)
        s1 = lax.dot_general(qn, ck, (((1,), (1,)), ((), ())), preferred_element_type=F32)
        w1 = jnp.where(block_end <= pos, jnp.exp(SCALE * s1), 0.0)
        t1 = jnp.sum(w1, axis=1, keepdims=True) + (pos < 31).astype(F32)
        o1 = jnp.dot(w1.astype(BF), cv, preferred_element_type=F32) / t1
        kn = unit(kb[:, :, :, hs : hs + 128].reshape(768, 128).astype(F32)).astype(BF)
        vn = vb[:, :, :, hs : hs + 128].reshape(768, 128)
        s2 = lax.dot_general(qn, kn, (((1,), (1,)), ((), ())), preferred_element_type=F32)
        inside = (key_pos <= pos) & (key_pos > pos - WINDOW) & (key_pos >= 0)
        w2 = jnp.where(inside, jnp.exp(SCALE * s2), 0.0)
        t2 = jnp.sum(w2, axis=1, keepdims=True)
        o2 = jnp.dot(w2.astype(BF), vn, preferred_element_type=F32) / t2
        g1 = jnp.sum(jnp.where(lane == 2 * core + h, gates, 0.0), axis=1, keepdims=True)
        g2 = jnp.sum(jnp.where(lane == 4 + 2 * core + h, gates, 0.0), axis=1, keepdims=True)
        tb[:, :, hs : hs + 128] = (g1 * o1 + g2 * o2).astype(BF).reshape(2, 128, 128)
    back = rcopy(tb.at[other], att.at[core], ss.at[28], rs.at[28], sib)
    back.start()
    att[core] = tb[core]

    @pl.when(core == 0)
    def _():
        for cp in halo:
            cp.wait_send()

    for cp in swap + near + comps + relay:
        cp.wait_send()
    for cp in share + [back]:
        cp.wait()


def run_attention(q, k, v, g, cw, wo):
    vm = pl.BlockSpec(memory_space=pltpu.VMEM)
    hbm = pl.BlockSpec(memory_space=pltpu.HBM)
    return pl.pallas_call(
        attention,
        out_shape=(
            jax.ShapeDtypeStruct((2, 128, 256), BF),
            jax.ShapeDtypeStruct((896, 512), BF),
        ),
        in_specs=[hbm] * 3 + [vm] * 2 + [hbm],
        out_specs=(vm, vm),
        scratch_shapes=[
            pltpu.VMEM((3, 2, 128, 256), BF),
            pltpu.VMEM((3, 2, 128, 256), BF),
            pltpu.VMEM((2, 128, 256), BF),
            pltpu.VMEM((2, 2, 4, 128), F32),
            pltpu.VMEM((2, 128, 128), F32),
            pltpu.VMEM((16, 256), BF),
            pltpu.VMEM((16, 256), BF),
            pltpu.VMEM((8, 2, 16, 256), BF),
            pltpu.VMEM((2, 128, 256), BF),
            pltpu.SemaphoreType.DMA((29,)),
            pltpu.SemaphoreType.DMA((29,)),
            pltpu.SemaphoreType.DMA((4,)),
        ],
        compiler_params=pltpu.CompilerParams(
            collective_id=1, has_side_effects=True, vmem_limit_bytes=67043328
        ),
        name="attention",
    )(q, k, v, g, cw, wo)


def z_ring(buf, z, core, e, ss, rs):
    up, down = lax.rem(z + 1, 8), lax.rem(z + 7, 8)

    def copy(way, step, chunk):
        block = lax.rem(z + 8 - step, 8) if way == 0 else lax.rem(z + step, 8)
        slot = way * 7 + 2 * step + (chunk if step < 3 else 0)
        return rcopy(
            buf.at[block, chunk],
            buf.at[block, chunk],
            ss.at[slot],
            rs.at[slot],
            (2 * (up if way == 0 else down) + core, e),
        )

    def chunks(way, step):
        return (0, 1) if step < 3 else ((0,) if way == 0 else (1,))

    return copy, chunks


def gather_start(copy, chunks, sent):
    for chunk in (0, 1):
        for way in (0, 1):
            cp = copy(way, 0, chunk)
            cp.start()
            sent.append(cp)


def gather_step(copy, chunks, step, sent):
    for chunk in (0, 1):
        for way in (0, 1):
            if chunk in chunks(way, step):
                copy(way, step, chunk).wait_recv()
                if step < 3 and chunk in chunks(way, step + 1):
                    cp = copy(way, step + 1, chunk)
                    cp.start()
                    sent.append(cp)


DA = 4096
DB = 7168 - DA
NEAR = ((0, 1, 7, 2), (6, 3, 5, 4))


def three(x):
    a = x.astype(BF)
    r = x - a.astype(F32)
    b = r.astype(BF)
    return jnp.concatenate([a, b, (r - b.astype(F32)).astype(BF)], 0)


def turned(x):
    if x.shape[0] < 128:
        x = jnp.concatenate([x, jnp.zeros((128 - x.shape[0], 128), F32)], 0)
    return x.T


def one(cond):
    return jnp.where(cond, 1.0, 0.0)


def tail(
    att, wp, res, gain, ids, gts, eg, eu, ed,
    out,
    sc, inf, hs, hid,
    xb, pb, a1, a2, a3, sb, c1, c2, c3, rb, ss, rs, s1, r1, s2, r2, s3, r3, si, ri,
    gw, dw, sw, rw, ls,
    oa, aa, xa, ya, rv, mx, fs, ro, ra, tk, tr, sB, aB, yB, rB, zs, zr,
    sa, qa, sg, qg, st, qt, sx, qx, sy, qy, sv, qv, sh, qh, sz, qz,
):
    z, core, e = place()
    ex, ey = lax.div(e, 4), lax.rem(e, 4)
    c = 2 * z + core
    sib = (2 * z + 1 - core, e)
    ring = [
        (ex, lambda t: (c, 4 * lax.rem(t, 4) + ey)),
        (ey, lambda t: (c, 4 * ex + lax.rem(t, 4))),
    ]
    zp = [(2 * lax.rem(z + j, 8) + core, e) for j in range(1, 8)]
    plane = [(c, lax.rem(e + j, 16)) for j in range(1, 16)]
    greet(plane + zp + [sib])

    xb[z] = att[...]
    copy, chunks = z_ring(xb, z, core, e, ss, rs)
    sent = []
    gather_start(copy, chunks, sent)

    share = []
    for n, src in enumerate((eg, eu)):
        share.append(rcopy(src, gw.at[:, pl.ds(256 * n + 128, 128)], sw.at[n], rw.at[n], sib))
    share.append(rcopy(ed, dw.at[pl.ds(128, 128), :], sw.at[2], rw.at[2], sib))
    load = [
        pltpu.make_async_copy(eg, gw.at[:, pl.ds(0, 128)], ls.at[0]),
        pltpu.make_async_copy(eu, gw.at[:, pl.ds(256, 128)], ls.at[1]),
        pltpu.make_async_copy(ed, dw.at[pl.ds(0, 128), :], ls.at[2]),
    ]
    for cp in share + load:
        cp.start()

    sc[...] = jnp.zeros_like(sc)
    sc[0:2, 0:8] = ids[...].astype(F32)
    sc[2:4, 0:8] = gts[...]
    cols = sc[...].T
    id0, id1, g0, g1 = (cols[0:8, n : n + 1] for n in range(4))
    lane = lax.broadcasted_iota(jnp.int32, (8, 128), 1)
    lanef = lane.astype(F32)
    named = one(lanef == id0) + one(lanef == id1)
    before, rows = jnp.zeros((1, 128), F32), []
    for t in range(8):
        rows.append(before)
        before = before + named[t : t + 1]
    count = jnp.concatenate(rows, 0)

    def target(i):
        return 2.0 * i + jnp.sum(jnp.where(lanef == i, count, 0.0), axis=1, keepdims=True)

    t0, t1 = target(id0), target(id1)
    inf[0] = jnp.where(
        lane == 0, t0, jnp.where(lane == 1, t1, jnp.where(lane == 2, g0, jnp.where(lane == 3, g1, 0.0)))
    )
    told = [rcopy(inf.at[0], inf.at[8 - j], si.at[j], ri.at[j], zp[j - 1]) for j in range(1, 8)]
    for cp in told:
        cp.start()

    def partial(block, r):
        x0, x1 = xb[block, 0], xb[block, 1]
        dims = (((1,), (1,)), ((), ()))
        y = lax.dot_general(x0, wp[:, :256], dims, preferred_element_type=F32)
        y = y + lax.dot_general(x1, wp[:, 256:], dims, preferred_element_type=F32)
        pb[r] = y.reshape(4, 4, 8, 896).astype(BF)

    partial(z, 0)
    for step in range(4):
        gather_step(copy, chunks, step, sent)
        partial(lax.rem(z + step + 1, 8), step + 1)
        if step < 3:
            partial(lax.rem(z + 7 - step, 8), 7 - step)

    def ring_sum(which, half, piece, first, second, mixed, ssem, rsem):
        p, dev = ring[which]
        nxt, prv = dev(p + 1), dev(p + 3)
        base = 6 * half
        far, nt, pt = lax.rem(p + 2, 4), lax.rem(p + 1, 4), lax.rem(p + 3, 4)
        cps = [
            rcopy(piece(far, 0), first.at[half, 0], ssem.at[base], rsem.at[base], nxt),
            rcopy(piece(far, 1), first.at[half, 1], ssem.at[base + 1], rsem.at[base + 1], prv),
            rcopy(piece(nt, 1), second.at[half, 0, pl.ds(2, 2)], ssem.at[base + 2], rsem.at[base + 2], nxt),
            rcopy(piece(pt, 0), second.at[half, 1, pl.ds(0, 2)], ssem.at[base + 3], rsem.at[base + 3], prv),
            rcopy(mixed.at[half, 0], second.at[half, 0, pl.ds(0, 2)], ssem.at[base + 4], rsem.at[base + 4], nxt),
            rcopy(mixed.at[half, 1], second.at[half, 1, pl.ds(2, 2)], ssem.at[base + 5], rsem.at[base + 5], prv),
        ]

        def start():
            for cp in cps[:4]:
                cp.start()

        def middle():
            cps[0].wait_recv()
            mixed[half, 0] = (first[half, 0].astype(F32) + piece(nt, 0)[...].astype(F32)).astype(BF)
            cps[4].start()
            cps[1].wait_recv()
            mixed[half, 1] = (first[half, 1].astype(F32) + piece(pt, 1)[...].astype(F32)).astype(BF)
            cps[5].start()

        def end():
            for cp in cps[2:]:
                cp.wait_recv()
            return [
                piece(p, n)[...].astype(F32)
                + second[half, 0, 2 * n : 2 * n + 2].astype(F32)
                + second[half, 1, 2 * n : 2 * n + 2].astype(F32)
                for n in range(2)
            ]

        def drain():
            for cp in cps:
                cp.wait_send()

        return start, middle, end, drain

    def piece_a(t, n):
        return pb.at[pl.ds(2 * n, 2), t]

    def piece_b(t, n):
        return pb.at[pl.ds(4 + 2 * n, 2), :, t]

    def piece_of(half):
        return lambda t, n: sb.at[half, pl.ds(2 * n, 2), t]

    wide = [
        ring_sum(0, 0, piece_a, a1, a2, a3, s1, r1),
        ring_sum(1, 1, piece_b, a1, a2, a3, s1, r1),
    ]
    thin = [
        ring_sum(1, 0, piece_of(0), c1, c2, c3, s2, r2),
        ring_sum(0, 1, piece_of(1), c1, c2, c3, s2, r2),
    ]
    for r in wide:
        r[0]()
    for r in wide:
        r[1]()
    for half in range(2):
        lo, hi = wide[half][2]()
        sb[half, 0:2] = lo.astype(BF)
        sb[half, 2:4] = hi.astype(BF)
        thin[half][0]()
    for r in thin:
        r[1]()
    moved = []
    for half in range(2):
        lo, hi = thin[half][2]()
        rb[4 * half : 4 * half + 2] = lo.astype(BF)
        rb[4 * half + 2 : 4 * half + 4] = hi.astype(BF)
        for j in range(4 * half, 4 * half + 4):
            if j:
                cp = rcopy(rb.at[j], hid.at[z], s3.at[j], r3.at[j], zp[j - 1])
                cp.start()
                moved.append(cp)
    hid[z] = rb[0]

    for cp in told:
        cp.wait_recv()
    mine0 = (lanef == t0) | (lanef == t1)
    spread_a = turned(one(mine0))[:32, :16].astype(BF)
    weigh_a = three((jnp.where(lanef == t0, g0, 0.0) + jnp.where(lanef == t1, g1, 0.0))[:, :32])
    slot = lax.broadcasted_iota(jnp.int32, (32, 128), 1)
    token = lax.broadcasted_iota(jnp.int32, (32, 128), 0)
    slotf = (2 * lax.div(slot, 8) + lax.rem(slot, 2)).astype(F32)
    same = lax.rem(lax.div(slot, 2), 4) == lax.div(token, 8)
    spread_b, weigh_b = [], []
    for g in range(2):
        t = jnp.concatenate([inf[r] for r in NEAR[g]], 0)
        hit0, hit1 = same & (slotf == t[:, 0:1]), same & (slotf == t[:, 1:2])
        spread_b.append(turned(one(hit0 | hit1))[:, :32].astype(BF))
        weigh_b.append(three(jnp.where(hit0, t[:, 2:3], 0.0) + jnp.where(hit1, t[:, 3:4], 0.0)))
    pr = lax.broadcasted_iota(jnp.int32, (128, 128), 0)
    pc = lax.broadcasted_iota(jnp.int32, (128, 128), 1)

    def plane_place(n):
        return lax.rem(lax.div(n, 2), 16) * 8 + lax.div(n, 32) * 2 + lax.rem(n, 2)

    order = one(pc == plane_place(pr)).astype(BF)
    unorder = one(pr == plane_place(pc)).astype(BF)

    for cp in moved:
        cp.wait_recv()
    for n in range(8):
        lo, hi = 896 * n, 896 * n + 896
        hs[:, lo:hi] = res[:, lo:hi].astype(F32) + hid[n].astype(F32)
    h = hs[...]
    normed = h * lax.rsqrt(jnp.mean(h * h, axis=1, keepdims=True) + EPS) * gain[...]

    tk[...] = normed[:, DA:].astype(BF)
    tr[0] = tk[...]
    spoke = []
    for j in (1, 7, 2, 6, 3, 5, 4):
        cp = rcopy(tk, tr.at[8 - j], st.at[j], qt.at[8 - j], zp[j - 1])
        cp.start()
        spoke.append(cp)

    padded = jnp.concatenate([normed[:, :DA], jnp.zeros((8, DA), F32)], 0).astype(BF)
    fs[...] = jnp.dot(spread_a, padded, preferred_element_type=F32)
    for i in range(16):
        oa[i] = fs[2 * i : 2 * i + 2, :].astype(BF)
    go = []
    for j in range(1, 16):
        cp = rcopy(oa.at[lax.rem(e + j, 16)], aa.at[e], sa.at[j], qa.at[j], plane[j - 1])
        cp.start()
        go.append(cp)
    aa[e] = oa[e]

    def heard(r):
        rcopy(tk, tr.at[r], st.at[0], qt.at[r], sib).wait_recv()

    def scatter(g):
        for r in NEAR[g]:
            if r:
                heard(r)
        x = jnp.concatenate([tr[r].astype(F32) for r in NEAR[g]], 0).astype(BF)
        y = jnp.dot(spread_b[g], x, preferred_element_type=F32)
        sB[g] = y.reshape(16, 8, DB).astype(BF)
        for j in range(1, 16):
            cp = rcopy(
                sB.at[g, lax.rem(e + j, 16)], aB.at[g, e], sg.at[g, j], qg.at[g, j], plane[j - 1]
            )
            cp.start()
            go.append(cp)
        aB[g, e] = sB[g, e]

    scatter(0)
    for cp in go[:15]:
        cp.wait_recv()
    for i in range(16):
        fs[2 * i : 2 * i + 2, :] = aa[i].astype(F32)
    xa[z, 0] = fs[0:16].astype(BF)
    xa[z, 1] = fs[16:32].astype(BF)
    copy2, chunks2 = z_ring(xa, z, core, e, sx, qx)
    sent2 = []
    gather_start(copy2, chunks2, sent2)
    scatter(1)
    for cp in load:
        cp.wait()
    for cp in share:
        cp.wait_recv()

    home = []

    def work(g):
        blocks = [lax.rem(z + r, 8) for r in NEAR[g]]
        x = jnp.concatenate([xa[b, n] for b in blocks for n in range(2)], 0)
        y = jnp.dot(x, gw[0:DA, :], preferred_element_type=F32)
        for j in range(1, 16):
            rcopy(sB.at[g, 0], aB.at[g, 0], sg.at[g, j], qg.at[g, j], sib).wait_recv()
        x = aB[g].astype(F32).reshape(128, DB).astype(BF)
        x = jnp.dot(order, x, preferred_element_type=F32).astype(BF)
        y = y + jnp.dot(x, gw[DA:, :], preferred_element_type=F32)
        gate, lift = y[:, :256], y[:, 256:]
        act = (gate / (1.0 + jnp.exp(-gate)) * lift).astype(BF)
        actp = jnp.dot(unorder, act, preferred_element_type=F32).astype(BF)

        @pl.loop(0, DB // 512)
        def _(n):
            cols = pl.ds(pl.multiple_of(n * 512, 512), 512)
            dcols = pl.ds(pl.multiple_of(DA + n * 512, 512), 512)
            y = jnp.dot(actp, dw[:, dcols], preferred_element_type=F32)
            yB[g, :, :, cols] = y.reshape(16, 8, 512).astype(BF)

        for j in range(1, 16):
            cp = rcopy(
                yB.at[g, lax.rem(e + j, 16)], rB.at[g, e], sy.at[g, j], qy.at[g, j], plane[j - 1]
            )
            cp.start()
            home.append(cp)
        rB[g, e] = yB[g, e]

        @pl.loop(0, DA // 512)
        def _(n):
            cols = pl.ds(pl.multiple_of(n * 512, 512), 512)
            y = jnp.dot(act, dw[:, cols], preferred_element_type=F32).astype(BF)
            for i, b in enumerate(blocks):
                ya[b, 0, :, cols] = y[32 * i : 32 * i + 16]
                ya[b, 1, :, cols] = y[32 * i + 16 : 32 * i + 32]

    gather_step(copy2, chunks2, 0, sent2)
    gather_step(copy2, chunks2, 1, sent2)
    work(0)
    gather_step(copy2, chunks2, 2, sent2)
    gather_step(copy2, chunks2, 3, sent2)
    work(1)

    up, down = zp[0], zp[6]

    def leg(way, n, src):
        return rcopy(
            src, rv.at[way, n], sv.at[way * 7 + n], qv.at[way * 7 + n], up if way == 0 else down
        )

    def mine(way, dist, first):
        block = lax.rem(z + dist, 8) if way == 0 else lax.rem(z + 8 - dist, 8)
        return ya.at[block, first if way == 0 else 1 - first]

    back = []

    def send(way, n, src):
        cp = leg(way, n, src)
        cp.start()
        back.append(cp)

    for way in (0, 1):
        send(way, 0, mine(way, 4, 0))
    for way in (0, 1):
        send(way, 2, mine(way, 3, 1))

    def along(n, dist, first, source):
        for way in (0, 1):
            leg(way, source, rv.at[way, source]).wait_recv()
            mx[way, n] = (
                rv[way, source].astype(F32) + mine(way, dist, first)[...].astype(F32)
            ).astype(BF)
            send(way, n, mx.at[way, n])

    part = []

    def gather_home(g):
        for j in range(1, 16):
            rcopy(yB.at[g, 0], rB.at[g, 0], sy.at[g, j], qy.at[g, j], sib).wait_recv()
        x = rB[g].astype(F32).reshape(128, DB).astype(BF)
        y = jnp.dot(weigh_b[g], x, preferred_element_type=F32)
        y = y[0:32] + y[32:64] + y[64:96]
        for i, r in enumerate(NEAR[g]):
            zs[r] = y[8 * i : 8 * i + 8].astype(BF)
            if r:
                cp = rcopy(zs.at[r], zr.at[8 - r], sz.at[r], qz.at[8 - r], zp[r - 1])
                cp.start()
                part.append(cp)

    along(1, 3, 0, 0)
    along(3, 2, 0, 1)
    along(4, 2, 1, 2)
    gather_home(0)
    along(5, 1, 0, 3)
    along(6, 1, 1, 4)
    for chunk in range(2):
        total = ya[z, chunk].astype(F32)
        for way in (0, 1):
            n = 5 + (chunk if way == 0 else 1 - chunk)
            leg(way, n, rv.at[way, n]).wait_recv()
            total = total + rv[way, n].astype(F32)
        fs[16 * chunk : 16 * chunk + 16] = total
    for i in range(16):
        ro[i] = fs[2 * i : 2 * i + 2, :].astype(BF)
    last = []
    for j in range(1, 16):
        cp = rcopy(ro.at[lax.rem(e + j, 16)], ra.at[e], sh.at[j], qh.at[j], plane[j - 1])
        cp.start()
        last.append(cp)
    ra[e] = ro[e]
    gather_home(1)
    for cp in last:
        cp.wait_recv()
    for i in range(16):
        fs[2 * i : 2 * i + 2, :] = ra[i].astype(F32)
    y = jnp.dot(weigh_a, fs[...].astype(BF), preferred_element_type=F32)
    out[:, :DA] = (hs[:, :DA] + (y[0:8] + y[8:16] + y[16:24])).astype(BF)
    total = hs[:, DA:] + zs[0].astype(F32)
    for r in range(1, 8):
        rcopy(zs.at[0], zr.at[r], sz.at[0], qz.at[r], sib).wait_recv()
        total = total + zr[r].astype(F32)
    out[:, DA:] = total.astype(BF)

    for r in wide + thin:
        r[3]()
    for cp in sent + share + told + moved + spoke + go + sent2 + home + back + part + last:
        cp.wait_send()


def run_tail(att, wp, res, gain, ids, gts, eg, eu, ed):
    vm = pl.BlockSpec(memory_space=pltpu.VMEM)
    hbm = pl.BlockSpec(memory_space=pltpu.HBM)

    def dma(*shape):
        return pltpu.SemaphoreType.DMA(shape)

    return pl.pallas_call(
        tail,
        out_shape=jax.ShapeDtypeStruct((8, 7168), BF),
        in_specs=[vm] * 6 + [hbm] * 3,
        out_specs=vm,
        scratch_shapes=[
            pltpu.VMEM((128, 128), F32),
            pltpu.VMEM((8, 8, 128), F32),
            pltpu.VMEM((8, 7168), F32),
            pltpu.VMEM((8, 8, 896), BF),
            pltpu.VMEM((8, 2, 128, 256), BF),
            pltpu.VMEM((8, 4, 4, 8, 896), BF),
            pltpu.VMEM((2, 2, 2, 4, 8, 896), BF),
            pltpu.VMEM((2, 2, 4, 4, 8, 896), BF),
            pltpu.VMEM((2, 2, 2, 4, 8, 896), BF),
            pltpu.VMEM((2, 4, 4, 8, 896), BF),
            pltpu.VMEM((2, 2, 2, 8, 896), BF),
            pltpu.VMEM((2, 2, 4, 8, 896), BF),
            pltpu.VMEM((2, 2, 2, 8, 896), BF),
            pltpu.VMEM((8, 8, 896), BF),
            dma(14), dma(14), dma(12), dma(12), dma(12), dma(12), dma(8), dma(8), dma(8), dma(8),
            pltpu.VMEM((7168, 512), BF),
            pltpu.VMEM((256, 7168), BF),
            dma(3), dma(3), dma(3),
            pltpu.VMEM((16, 2, DA), BF),
            pltpu.VMEM((16, 2, DA), BF),
            pltpu.VMEM((8, 2, 16, DA), BF),
            pltpu.VMEM((8, 2, 16, DA), BF),
            pltpu.VMEM((2, 7, 16, DA), BF),
            pltpu.VMEM((2, 7, 16, DA), BF),
            pltpu.VMEM((32, DA), F32),
            pltpu.VMEM((16, 2, DA), BF),
            pltpu.VMEM((16, 2, DA), BF),
            pltpu.VMEM((8, DB), BF),
            pltpu.VMEM((8, 8, DB), BF),
            pltpu.VMEM((2, 16, 8, DB), BF),
            pltpu.VMEM((2, 16, 8, DB), BF),
            pltpu.VMEM((2, 16, 8, DB), BF),
            pltpu.VMEM((2, 16, 8, DB), BF),
            pltpu.VMEM((8, 8, DB), BF),
            pltpu.VMEM((8, 8, DB), BF),
            dma(16), dma(16), dma(2, 16), dma(2, 16), dma(8), dma(8), dma(14), dma(14),
            dma(2, 16), dma(2, 16), dma(14), dma(14), dma(16), dma(16), dma(8), dma(8),
        ],
        compiler_params=pltpu.CompilerParams(
            collective_id=2, has_side_effects=True, vmem_limit_bytes=67043328
        ),
        name="tail",
    )(att, wp, res, gain, ids, gts, eg, eu, ed)


def local(
    query_input,
    key_input,
    value_input,
    gate_logits,
    comp_weight,
    out_proj,
    residual_in,
    ffn_gain,
    expert_ids,
    route_gates,
    expert_gate,
    expert_up,
    expert_down,
):
    gates = gate_logits.transpose(0, 2, 1)
    cw = jnp.broadcast_to(comp_weight.transpose(0, 2, 1)[..., None], (2, 4, 32, 128))
    att, wpair = run_attention(query_input, key_input, value_input, gates, cw, out_proj.T)
    return run_tail(
        att, wpair, residual_in, ffn_gain.reshape(1, 7168), expert_ids.T, route_gates.T,
        expert_gate[0], expert_up[0], expert_down[0],
    )


def solution(mesh):
    in_specs = (
        P("ctx", "exp"),
        P("ctx", "exp"),
        P("ctx", "exp"),
        P(None, "ctx", "exp"),
        P(None, None, "exp"),
        P("exp", "ctx"),
        P(("ctx", "exp"), None),
        P(),
        P(("ctx", "exp"), None),
        P(("ctx", "exp"), None),
        P("exp", None, "ctx"),
        P("exp", None, "ctx"),
        P("exp", "ctx", None),
    )
    out_specs = P(("ctx", "exp"), None)
    return jax.shard_map(local, mesh=mesh, in_specs=in_specs, out_specs=out_specs, check_vma=False)
```

```python
import math

import jax
import jax.numpy as jnp
from jax import lax
from jax.experimental import pallas as pl
from jax.experimental.pallas import tpu as pltpu
from jax.sharding import PartitionSpec as P

MESH = pl.DeviceIdType.MESH
BF = jnp.bfloat16
F32 = jnp.float32
WINDOW = 512
SCALE = 2.0 / math.sqrt(128)
EPS = 1e-06


def place():
    c = lax.axis_index("ctx")
    e = lax.axis_index("exp")
    return lax.div(c, 2), lax.rem(c, 2), e


def greet(devices):
    bar = pltpu.get_barrier_semaphore()
    for d in devices:
        pl.semaphore_signal(bar, inc=1, device_id=d, device_id_type=MESH)
    pl.semaphore_wait(bar, len(devices))


def rcopy(src, dst, ss, rs, dev):
    return pltpu.make_async_remote_copy(
        src_ref=src, dst_ref=dst, send_sem=ss, recv_sem=rs, device_id=dev, device_id_type=MESH
    )


def unit(x):
    return x * lax.rsqrt(jnp.mean(x * x, axis=1, keepdims=True) + EPS)


def attend(z, core, e, q, k, v, g, cw, wo, wpair, xb, kb, vb, qb, gb, gs, hk, hv, cb, tb, ss, rs, ls):
    other = 1 - core
    up, down = lax.rem(z + 1, 8), lax.rem(z + 7, 8)
    sib = (2 * z + other, e)
    peers = [(2 * lax.rem(z + j, 8) + core, e) for j in range(1, 8)]
    off_other = pl.multiple_of(other * 256, 256)
    off = pl.multiple_of(core * 256, 256)
    near = []
    for kk in range(2):
        for a, (src, dst) in enumerate(((k, kb), (v, vb))):
            near.append(
                rcopy(
                    src.at[:, pl.ds(kk * 256, 256)],
                    dst.at[1, core],
                    ss.at[8 + 2 * kk + a],
                    rs.at[8 + 2 * core + a],
                    (2 * up + kk, e),
                )
            )
    halo = []
    for kk in range(2):
        for a, (src, dst) in enumerate(((k, hk), (v, hv))):
            halo.append(
                rcopy(
                    src.at[pl.ds(0, 16), pl.ds(kk * 256, 256)],
                    dst,
                    ss.at[16 + 2 * kk + a],
                    rs.at[16 + a],
                    (2 * down + kk, e),
                )
            )

    @pl.when(core == 0)
    def _():
        for cp in halo:
            cp.start()

    rows = pl.ds(pl.multiple_of(core * 448, 64), 448)
    own = [
        pltpu.make_async_copy(k.at[:, pl.ds(off, 256)], kb.at[2, core], ls.at[0]),
        pltpu.make_async_copy(v.at[:, pl.ds(off, 256)], vb.at[2, core], ls.at[1]),
        pltpu.make_async_copy(q.at[:, pl.ds(off, 256)], qb.at[core], ls.at[2]),
        pltpu.make_async_copy(wo, wpair.at[rows], ls.at[3]),
    ]
    swap = [
        rcopy(k.at[:, pl.ds(off_other, 256)], kb.at[2, core], ss.at[0], rs.at[0], sib),
        rcopy(v.at[:, pl.ds(off_other, 256)], vb.at[2, core], ss.at[1], rs.at[1], sib),
        rcopy(q.at[:, pl.ds(off_other, 256)], qb.at[core], ss.at[2], rs.at[2], sib),
        rcopy(g, gb.at[core], ss.at[3], rs.at[3], sib),
    ]
    for cp in swap:
        cp.start()
    for cp in near:
        cp.start()
    for cp in own:
        cp.start()
    share = [
        rcopy(wo, wpair.at[rows], ss.at[4], rs.at[4], sib),
    ]
    for cp in share:
        cp.start()

    gb[core] = g[...]

    relay = []

    def pass_on(n):
        for a, buf in enumerate((kb, vb)):
            rcopy(buf.at[1, n], buf.at[1, n], ss.at[8], rs.at[8 + 2 * n + a], sib).wait_recv()
            cp = rcopy(
                buf.at[1, n],
                buf.at[0, n],
                ss.at[12 + 2 * n + a],
                rs.at[12 + 2 * n + a],
                (2 * up + core, e),
            )
            cp.start()
            relay.append(cp)

    gs[...] = jnp.zeros_like(gs)
    gs[0, 0:4, 0:32] = cw[0]
    gs[0, 4:8, 0:32] = cw[1]
    weights = gs[0].T[0:32]
    lane = lax.broadcasted_iota(jnp.int32, (1, 128), 1)

    def squeeze(a, blocks, tail):
        for h in range(2):
            hs = h * 128
            last = jnp.where(z == 7, 0.0, tail[:, hs : hs + 128].astype(F32))
            x = jnp.concatenate(
                [
                    blocks[2, 0, :, hs : hs + 128].astype(F32),
                    blocks[2, 1, :, hs : hs + 128].astype(F32),
                    last,
                ],
                0,
            ).reshape(17, 16, 128)
            w = jnp.sum(jnp.where(lane == 4 * a + 2 * core + h, weights, 0.0), axis=1, keepdims=True)
            w = jnp.broadcast_to(w, (32, 128))
            y = jnp.sum(x[:16] * w[None, :16], axis=1) + jnp.sum(x[1:] * w[None, 16:], axis=1)
            if a == 0:
                y = unit(y)
            cb[z, a, :, hs : hs + 128] = y.astype(BF)

    for cp in own:
        cp.wait()
    pass_on(0)
    for cp in swap:
        cp.wait_recv()
    for cp in halo[:2]:
        cp.wait_recv()
    squeeze(0, kb, hk)
    pass_on(1)
    squeeze(1, vb, hv)
    comps = [
        rcopy(cb.at[z], cb.at[z], ss.at[20 + j], rs.at[20 + j], peers[j - 1]) for j in range(1, 8)
    ]
    for cp in comps:
        cp.start()
    for cp in comps:
        cp.wait_recv()
    for cp in relay:
        cp.wait_recv()

    pos = z * 256 + lax.broadcasted_iota(jnp.int32, (256, 1), 0)
    block_end = lax.broadcasted_iota(jnp.int32, (1, 128), 1) * 16 + 31
    key_pos = (z - 2) * 256 + lax.broadcasted_iota(jnp.int32, (1, 768), 1)
    for n in range(2):
        gs[n, 0:4] = gb[n, 0]
        gs[n, 4:8] = gb[n, 1]
    gates = jnp.concatenate([gs[0].T, gs[1].T], 0)
    gates = 1.0 / (1.0 + jnp.exp(-gates))
    for h in range(2):
        hs = h * 128
        qn = unit(qb[:, :, hs : hs + 128].reshape(256, 128).astype(F32)).astype(BF)
        ck = cb[:, 0, :, hs : hs + 128].reshape(128, 128)
        cv = cb[:, 1, :, hs : hs + 128].reshape(128, 128)
        s1 = lax.dot_general(qn, ck, (((1,), (1,)), ((), ())), preferred_element_type=F32)
        w1 = jnp.where(block_end <= pos, jnp.exp(SCALE * s1), 0.0)
        t1 = jnp.sum(w1, axis=1, keepdims=True) + (pos < 31).astype(F32)
        o1 = jnp.dot(w1.astype(BF), cv, preferred_element_type=F32) / t1
        kn = unit(kb[:, :, :, hs : hs + 128].reshape(768, 128).astype(F32)).astype(BF)
        vn = vb[:, :, :, hs : hs + 128].reshape(768, 128)
        s2 = lax.dot_general(qn, kn, (((1,), (1,)), ((), ())), preferred_element_type=F32)
        inside = (key_pos <= pos) & (key_pos > pos - WINDOW) & (key_pos >= 0)
        w2 = jnp.where(inside, jnp.exp(SCALE * s2), 0.0)
        t2 = jnp.sum(w2, axis=1, keepdims=True)
        o2 = jnp.dot(w2.astype(BF), vn, preferred_element_type=F32) / t2
        g1 = jnp.sum(jnp.where(lane == 2 * core + h, gates, 0.0), axis=1, keepdims=True)
        g2 = jnp.sum(jnp.where(lane == 4 + 2 * core + h, gates, 0.0), axis=1, keepdims=True)
        tb[:, :, hs : hs + 128] = (g1 * o1 + g2 * o2).astype(BF).reshape(2, 128, 128)
    back = rcopy(tb.at[other], xb.at[z, core], ss.at[28], rs.at[28], sib)
    back.start()
    xb[z, core] = tb[core]

    def drain():
        @pl.when(core == 0)
        def _():
            for cp in halo:
                cp.wait_send()

        for cp in swap + near + comps + relay + share + [back]:
            cp.wait_send()

    return share[0], back, drain


def z_ring(buf, z, core, e, ss, rs, turn):
    up, down = lax.rem(z + 1, 8), lax.rem(z + 7, 8)

    def copy(way, step, chunk):
        block = lax.rem(z + 8 - step, 8) if way == 0 else lax.rem(z + step, 8)
        slot = way * 7 + 2 * step + (chunk if step < 3 else 0)
        return rcopy(
            buf.at[block, lax.rem(chunk + turn, 2)],
            buf.at[block, lax.rem(chunk + turn, 2)],
            ss.at[slot],
            rs.at[slot],
            (2 * (up if way == 0 else down) + core, e),
        )

    def chunks(way, step):
        return (0, 1) if step < 3 else ((0,) if way == 0 else (1,))

    return copy, chunks


def gather_start(copy, chunk, sent):
    for way in (0, 1):
        cp = copy(way, 0, chunk)
        cp.start()
        sent.append(cp)


def gather_step(copy, chunks, step, sent):
    for chunk in (0, 1):
        for way in (0, 1):
            if chunk in chunks(way, step):
                copy(way, step, chunk).wait_recv()
                if step < 3 and chunk in chunks(way, step + 1):
                    cp = copy(way, step + 1, chunk)
                    cp.start()
                    sent.append(cp)


DA = 4096
DB = 7168 - DA
HA = 3584
HB = 7168 - HA
NEAR = ((0, 1, 7, 2), (6, 3, 5, 4))


def three(x):
    a = x.astype(BF)
    r = x - a.astype(F32)
    b = r.astype(BF)
    return jnp.concatenate([a, b, (r - b.astype(F32)).astype(BF)], 0)


def turned(x):
    if x.shape[0] < 128:
        x = jnp.concatenate([x, jnp.zeros((128 - x.shape[0], 128), F32)], 0)
    return x.T


def one(cond):
    return jnp.where(cond, 1.0, 0.0)


def tail(
    q, k, v, g, cw, wo, res, gain, ids, gts, eg, eu, ed,
    out,
    wp, kb, vb, qb, gb, gs, hk, hv, cb, tb, s0, r0, l0,
    sc, inf, hs, hid,
    xb, pb, a1, a2, a3, sb, c1, c2, c3, rb, ss, rs, s1, r1, s2, r2, s3, r3, si, ri,
    gw, dw, sw, rw, ls,
    oa, aa, xa, ya, rv, mx, fs, ro, ra, tk, tr, sB, aB, yB, rB, zs, zr,
    sa, qa, sg, qg, st, qt, sx, qx, sy, qy, sv, qv, sh, qh, sz, qz,
):
    z, core, e = place()
    ex, ey = lax.div(e, 4), lax.rem(e, 4)
    c = 2 * z + core
    sib = (2 * z + 1 - core, e)
    ring = [
        (ex, lambda t: (c, 4 * lax.rem(t, 4) + ey)),
        (ey, lambda t: (c, 4 * ex + lax.rem(t, 4))),
    ]
    zp = [(2 * lax.rem(z + j, 8) + core, e) for j in range(1, 8)]
    plane = [(c, lax.rem(e + j, 16)) for j in range(1, 16)]
    cross = [(2 * lax.rem(z + j, 8) + 1 - core, e) for j in (1, 7)]
    greet(plane + zp + [sib] + cross)
    outw, swapped, drain = attend(
        z, core, e, q, k, v, g, cw, wo, wp, xb, kb, vb, qb, gb, gs, hk, hv, cb, tb, s0, r0, l0
    )

    copy, chunks = z_ring(xb, z, core, e, ss, rs, core)
    sent = []
    gather_start(copy, 0, sent)

    share = []
    for n, src in enumerate((eg, eu)):
        share.append(rcopy(src, gw.at[:, pl.ds(256 * n + 128, 128)], sw.at[n], rw.at[n], sib))
    share.append(rcopy(ed, dw.at[pl.ds(128, 128), :], sw.at[2], rw.at[2], sib))
    load = [
        pltpu.make_async_copy(eg, gw.at[:, pl.ds(0, 128)], ls.at[0]),
        pltpu.make_async_copy(eu, gw.at[:, pl.ds(256, 128)], ls.at[1]),
        pltpu.make_async_copy(ed, dw.at[pl.ds(0, 128), :], ls.at[2]),
    ]
    for cp in share + load:
        cp.start()

    sc[...] = jnp.zeros_like(sc)
    sc[0:2, 0:8] = ids[...].astype(F32)
    sc[2:4, 0:8] = gts[...]
    cols = sc[...].T
    id0, id1, g0, g1 = (cols[0:8, n : n + 1] for n in range(4))
    lane = lax.broadcasted_iota(jnp.int32, (8, 128), 1)
    lanef = lane.astype(F32)
    named = one(lanef == id0) + one(lanef == id1)
    before, rows = jnp.zeros((1, 128), F32), []
    for t in range(8):
        rows.append(before)
        before = before + named[t : t + 1]
    count = jnp.concatenate(rows, 0)

    def target(i):
        return 2.0 * i + jnp.sum(jnp.where(lanef == i, count, 0.0), axis=1, keepdims=True)

    t0, t1 = target(id0), target(id1)
    inf[0] = jnp.where(
        lane == 0, t0, jnp.where(lane == 1, t1, jnp.where(lane == 2, g0, jnp.where(lane == 3, g1, 0.0)))
    )
    told = [rcopy(inf.at[0], inf.at[8 - j], si.at[j], ri.at[j], zp[j - 1]) for j in range(1, 8)]
    for cp in told:
        cp.start()

    def partial(block, r):
        x0, x1 = xb[block, 0], xb[block, 1]
        dims = (((1,), (1,)), ((), ()))
        y = lax.dot_general(x0, wp[:, :256], dims, preferred_element_type=F32)
        y = y + lax.dot_general(x1, wp[:, 256:], dims, preferred_element_type=F32)
        pb[r] = y.reshape(4, 4, 8, 896).astype(BF)

    swapped.wait_recv()
    gather_start(copy, 1, sent)
    outw.wait_recv()
    partial(z, 0)
    for step in range(4):
        gather_step(copy, chunks, step, sent)
        partial(lax.rem(z + step + 1, 8), step + 1)
        if step < 3:
            partial(lax.rem(z + 7 - step, 8), 7 - step)

    def ring_sum(which, half, piece, first, second, mixed, ssem, rsem):
        p, dev = ring[which]
        nxt, prv = dev(p + 1), dev(p + 3)
        base = 6 * half
        far, nt, pt = lax.rem(p + 2, 4), lax.rem(p + 1, 4), lax.rem(p + 3, 4)
        cps = [
            rcopy(piece(far, 0), first.at[half, 0], ssem.at[base], rsem.at[base], nxt),
            rcopy(piece(far, 1), first.at[half, 1], ssem.at[base + 1], rsem.at[base + 1], prv),
            rcopy(piece(nt, 1), second.at[half, 0, pl.ds(2, 2)], ssem.at[base + 2], rsem.at[base + 2], nxt),
            rcopy(piece(pt, 0), second.at[half, 1, pl.ds(0, 2)], ssem.at[base + 3], rsem.at[base + 3], prv),
            rcopy(mixed.at[half, 0], second.at[half, 0, pl.ds(0, 2)], ssem.at[base + 4], rsem.at[base + 4], nxt),
            rcopy(mixed.at[half, 1], second.at[half, 1, pl.ds(2, 2)], ssem.at[base + 5], rsem.at[base + 5], prv),
        ]

        def start():
            for cp in cps[:4]:
                cp.start()

        def middle():
            cps[0].wait_recv()
            mixed[half, 0] = (first[half, 0].astype(F32) + piece(nt, 0)[...].astype(F32)).astype(BF)
            cps[4].start()
            cps[1].wait_recv()
            mixed[half, 1] = (first[half, 1].astype(F32) + piece(pt, 1)[...].astype(F32)).astype(BF)
            cps[5].start()

        def end():
            for cp in cps[2:]:
                cp.wait_recv()
            return [
                piece(p, n)[...].astype(F32)
                + second[half, 0, 2 * n : 2 * n + 2].astype(F32)
                + second[half, 1, 2 * n : 2 * n + 2].astype(F32)
                for n in range(2)
            ]

        def drain():
            for cp in cps:
                cp.wait_send()

        return start, middle, end, drain

    def piece_a(t, n):
        return pb.at[pl.ds(2 * n, 2), t]

    def piece_b(t, n):
        return pb.at[pl.ds(4 + 2 * n, 2), :, t]

    def piece_of(half):
        return lambda t, n: sb.at[half, pl.ds(2 * n, 2), t]

    wide = [
        ring_sum(0, 0, piece_a, a1, a2, a3, s1, r1),
        ring_sum(1, 1, piece_b, a1, a2, a3, s1, r1),
    ]
    thin = [
        ring_sum(1, 0, piece_of(0), c1, c2, c3, s2, r2),
        ring_sum(0, 1, piece_of(1), c1, c2, c3, s2, r2),
    ]
    for r in wide:
        r[0]()
    for r in wide:
        r[1]()
    for half in range(2):
        lo, hi = wide[half][2]()
        sb[half, 0:2] = lo.astype(BF)
        sb[half, 2:4] = hi.astype(BF)
        thin[half][0]()
    for r in thin:
        r[1]()
    moved = []
    for half in range(2):
        lo, hi = thin[half][2]()
        rb[4 * half : 4 * half + 2] = lo.astype(BF)
        rb[4 * half + 2 : 4 * half + 4] = hi.astype(BF)
        for j in range(4 * half, 4 * half + 4):
            if j:
                cp = rcopy(rb.at[j], hid.at[z], s3.at[j], r3.at[j], zp[j - 1])
                cp.start()
                moved.append(cp)
    hid[z] = rb[0]

    for cp in told:
        cp.wait_recv()
    mine0 = (lanef == t0) | (lanef == t1)
    spread_a = turned(one(mine0))[:32, :16].astype(BF)
    weigh_a = three((jnp.where(lanef == t0, g0, 0.0) + jnp.where(lanef == t1, g1, 0.0))[:, :32])
    slot = lax.broadcasted_iota(jnp.int32, (32, 128), 1)
    token = lax.broadcasted_iota(jnp.int32, (32, 128), 0)
    slotf = (2 * lax.div(slot, 8) + lax.rem(slot, 2)).astype(F32)
    same = lax.rem(lax.div(slot, 2), 4) == lax.div(token, 8)
    spread_b, weigh_b = [], []
    for g in range(2):
        t = jnp.concatenate([inf[r] for r in NEAR[g]], 0)
        hit0, hit1 = same & (slotf == t[:, 0:1]), same & (slotf == t[:, 1:2])
        spread_b.append(turned(one(hit0 | hit1))[:, :32].astype(BF))
        weigh_b.append(three(jnp.where(hit0, t[:, 2:3], 0.0) + jnp.where(hit1, t[:, 3:4], 0.0)))
    pr = lax.broadcasted_iota(jnp.int32, (128, 128), 0)
    pc = lax.broadcasted_iota(jnp.int32, (128, 128), 1)

    def plane_place(n):
        return lax.rem(lax.div(n, 2), 16) * 8 + lax.div(n, 32) * 2 + lax.rem(n, 2)

    order = one(pc == plane_place(pr)).astype(BF)
    unorder = one(pr == plane_place(pc)).astype(BF)

    for cp in moved:
        cp.wait_recv()
    for n in range(8):
        lo, hi = 896 * n, 896 * n + 896
        hs[:, lo:hi] = res[:, lo:hi].astype(F32) + hid[n].astype(F32)
    h = hs[...]
    normed = h * lax.rsqrt(jnp.mean(h * h, axis=1, keepdims=True) + EPS) * gain[...]

    tk[...] = normed[:, DA:].astype(BF)
    tr[0] = tk[...]
    spoke = []
    for j in (1, 7, 2, 6, 3, 5, 4):
        cp = rcopy(tk, tr.at[8 - j], st.at[j], qt.at[8 - j], zp[j - 1])
        cp.start()
        spoke.append(cp)

    padded = jnp.concatenate([normed[:, :DA], jnp.zeros((8, DA), F32)], 0).astype(BF)
    fs[:, :DA] = jnp.dot(spread_a, padded, preferred_element_type=F32)
    for i in range(16):
        oa[i] = fs[2 * i : 2 * i + 2, :DA].astype(BF)
    go = []
    for j in range(1, 16):
        cp = rcopy(oa.at[lax.rem(e + j, 16)], aa.at[e], sa.at[j], qa.at[j], plane[j - 1])
        cp.start()
        go.append(cp)
    aa[e] = oa[e]

    def heard(r):
        rcopy(tk, tr.at[r], st.at[0], qt.at[r], sib).wait_recv()

    def scatter(g):
        for r in NEAR[g]:
            if r:
                heard(r)
        x = jnp.concatenate([tr[r].astype(F32) for r in NEAR[g]], 0).astype(BF)
        y = jnp.dot(spread_b[g], x, preferred_element_type=F32)
        sB[g] = y.reshape(16, 8, DB).astype(BF)
        for j in range(1, 16):
            cp = rcopy(
                sB.at[g, lax.rem(e + j, 16)], aB.at[g, e], sg.at[g, j], qg.at[g, j], plane[j - 1]
            )
            cp.start()
            go.append(cp)
        aB[g, e] = sB[g, e]

    scatter(0)
    for cp in go[:15]:
        cp.wait_recv()
    for i in range(16):
        fs[2 * i : 2 * i + 2, :DA] = aa[i].astype(F32)
    xa[z, 0] = fs[0:16, :DA].astype(BF)
    xa[z, 1] = fs[16:32, :DA].astype(BF)
    copy2, chunks2 = z_ring(xa, z, core, e, sx, qx, 0)
    sent2 = []
    gather_start(copy2, 0, sent2)
    gather_start(copy2, 1, sent2)
    scatter(1)
    for cp in load:
        cp.wait()
    for cp in share:
        cp.wait_recv()

    home = []

    def work(g):
        blocks = [lax.rem(z + r, 8) for r in NEAR[g]]
        x = jnp.concatenate([xa[b, n] for b in blocks for n in range(2)], 0)
        y = jnp.dot(x, gw[0:DA, :], preferred_element_type=F32)
        for j in range(1, 16):
            rcopy(sB.at[g, 0], aB.at[g, 0], sg.at[g, j], qg.at[g, j], sib).wait_recv()
        x = aB[g].astype(F32).reshape(128, DB).astype(BF)
        x = jnp.dot(order, x, preferred_element_type=F32).astype(BF)
        y = y + jnp.dot(x, gw[DA:, :], preferred_element_type=F32)
        gate, lift = y[:, :256], y[:, 256:]
        act = (gate / (1.0 + jnp.exp(-gate)) * lift).astype(BF)
        actp = jnp.dot(unorder, act, preferred_element_type=F32).astype(BF)

        @pl.loop(0, HB // 512)
        def _(n):
            cols = pl.ds(pl.multiple_of(n * 512, 512), 512)
            dcols = pl.ds(pl.multiple_of(HA + n * 512, 512), 512)
            y = jnp.dot(actp, dw[:, dcols], preferred_element_type=F32)
            yB[g, :, :, cols] = y.reshape(16, 8, 512).astype(BF)

        for j in range(1, 16):
            cp = rcopy(
                yB.at[g, lax.rem(e + j, 16)], rB.at[g, e], sy.at[g, j], qy.at[g, j], plane[j - 1]
            )
            cp.start()
            home.append(cp)
        rB[g, e] = yB[g, e]

        @pl.loop(0, HA // 512)
        def _(n):
            cols = pl.ds(pl.multiple_of(n * 512, 512), 512)
            y = jnp.dot(act, dw[:, cols], preferred_element_type=F32).astype(BF)
            for i, b in enumerate(blocks):
                ya[b, 0, :, cols] = y[32 * i : 32 * i + 16]
                ya[b, 1, :, cols] = y[32 * i + 16 : 32 * i + 32]

    gather_step(copy2, chunks2, 0, sent2)
    gather_step(copy2, chunks2, 1, sent2)
    work(0)
    gather_step(copy2, chunks2, 2, sent2)
    gather_step(copy2, chunks2, 3, sent2)
    work(1)

    up, down = zp[0], zp[6]

    def leg(way, n, src):
        return rcopy(
            src, rv.at[way, n], sv.at[way * 7 + n], qv.at[way * 7 + n], up if way == 0 else down
        )

    def mine(way, dist, first):
        block = lax.rem(z + dist, 8) if way == 0 else lax.rem(z + 8 - dist, 8)
        return ya.at[block, first if way == 0 else 1 - first]

    back = []

    def send(way, n, src):
        cp = leg(way, n, src)
        cp.start()
        back.append(cp)

    for way in (0, 1):
        send(way, 0, mine(way, 4, 0))
    for way in (0, 1):
        send(way, 2, mine(way, 3, 1))

    def along(n, dist, first, source):
        for way in (0, 1):
            leg(way, source, rv.at[way, source]).wait_recv()
            mx[way, n] = (
                rv[way, source].astype(F32) + mine(way, dist, first)[...].astype(F32)
            ).astype(BF)
            send(way, n, mx.at[way, n])

    part = []

    def gather_home(g):
        for j in range(1, 16):
            rcopy(yB.at[g, 0], rB.at[g, 0], sy.at[g, j], qy.at[g, j], sib).wait_recv()
        x = rB[g].astype(F32).reshape(128, HB).astype(BF)
        y = jnp.dot(weigh_b[g], x, preferred_element_type=F32)
        y = y[0:32] + y[32:64] + y[64:96]
        for i, r in enumerate(NEAR[g]):
            zs[r] = y[8 * i : 8 * i + 8].astype(BF)
            if r:
                cp = rcopy(zs.at[r], zr.at[8 - r], sz.at[r], qz.at[8 - r], zp[r - 1])
                cp.start()
                part.append(cp)

    along(1, 3, 0, 0)
    along(3, 2, 0, 1)
    along(4, 2, 1, 2)
    gather_home(0)
    along(5, 1, 0, 3)
    along(6, 1, 1, 4)
    for chunk in range(2):
        total = ya[z, chunk].astype(F32)
        for way in (0, 1):
            n = 5 + (chunk if way == 0 else 1 - chunk)
            leg(way, n, rv.at[way, n]).wait_recv()
            total = total + rv[way, n].astype(F32)
        fs[16 * chunk : 16 * chunk + 16, :HA] = total
    for i in range(16):
        ro[i] = fs[2 * i : 2 * i + 2, :HA].astype(BF)
    last = []
    for j in range(1, 16):
        cp = rcopy(ro.at[lax.rem(e + j, 16)], ra.at[e], sh.at[j], qh.at[j], plane[j - 1])
        cp.start()
        last.append(cp)
    ra[e] = ro[e]
    gather_home(1)
    for cp in last:
        cp.wait_recv()
    for i in range(16):
        fs[2 * i : 2 * i + 2, :HA] = ra[i].astype(F32)
    y = jnp.dot(weigh_a, fs[:, :HA].astype(BF), preferred_element_type=F32)
    out[:, :HA] = (hs[:, :HA] + (y[0:8] + y[8:16] + y[16:24])).astype(BF)
    total = hs[:, HA:] + zs[0].astype(F32)
    for r in range(1, 8):
        rcopy(zs.at[0], zr.at[r], sz.at[0], qz.at[r], sib).wait_recv()
        total = total + zr[r].astype(F32)
    out[:, HA:] = total.astype(BF)

    drain()
    for r in wide + thin:
        r[3]()
    for cp in sent + share + told + moved + spoke + go + sent2 + home + back + part + last:
        cp.wait_send()


def run(q, k, v, g, cw, wo, res, gain, ids, gts, eg, eu, ed):
    vm = pl.BlockSpec(memory_space=pltpu.VMEM)
    hbm = pl.BlockSpec(memory_space=pltpu.HBM)

    def dma(*shape):
        return pltpu.SemaphoreType.DMA(shape)

    def bf(*shape):
        return pltpu.VMEM(shape, BF)

    def f32(*shape):
        return pltpu.VMEM(shape, F32)

    return pl.pallas_call(
        tail,
        out_shape=jax.ShapeDtypeStruct((8, 7168), BF),
        in_specs=[hbm] * 3 + [vm] * 2 + [hbm] + [vm] * 4 + [hbm] * 3,
        out_specs=vm,
        scratch_shapes=[
            bf(896, 512),
            bf(3, 2, 128, 256),
            bf(3, 2, 128, 256),
            bf(2, 128, 256),
            f32(2, 2, 4, 128),
            f32(2, 128, 128),
            bf(16, 256),
            bf(16, 256),
            bf(8, 2, 16, 256),
            bf(2, 128, 256),
            dma(29), dma(29), dma(4),
            f32(128, 128),
            f32(8, 8, 128),
            f32(8, 7168),
            bf(8, 8, 896),
            bf(8, 2, 128, 256),
            bf(8, 4, 4, 8, 896),
            bf(2, 2, 2, 4, 8, 896),
            bf(2, 2, 4, 4, 8, 896),
            bf(2, 2, 2, 4, 8, 896),
            bf(2, 4, 4, 8, 896),
            bf(2, 2, 2, 8, 896),
            bf(2, 2, 4, 8, 896),
            bf(2, 2, 2, 8, 896),
            bf(8, 8, 896),
            dma(14), dma(14), dma(12), dma(12), dma(12), dma(12), dma(8), dma(8), dma(8), dma(8),
            bf(7168, 512),
            bf(256, 7168),
            dma(3), dma(3), dma(3),
            bf(16, 2, DA),
            bf(16, 2, DA),
            bf(8, 2, 16, DA),
            bf(8, 2, 16, HA),
            bf(2, 7, 16, HA),
            bf(2, 7, 16, HA),
            f32(32, max(DA, HA)),
            bf(16, 2, HA),
            bf(16, 2, HA),
            bf(8, DB),
            bf(8, 8, DB),
            bf(2, 16, 8, DB),
            bf(2, 16, 8, DB),
            bf(2, 16, 8, HB),
            bf(2, 16, 8, HB),
            bf(8, 8, HB),
            bf(8, 8, HB),
            dma(16), dma(16), dma(2, 16), dma(2, 16), dma(8), dma(8), dma(14), dma(14),
            dma(2, 16), dma(2, 16), dma(14), dma(14), dma(16), dma(16), dma(8), dma(8),
        ],
        compiler_params=pltpu.CompilerParams(
            collective_id=2, has_side_effects=True, vmem_limit_bytes=67043328
        ),
        name="layer",
    )(q, k, v, g, cw, wo, res, gain, ids, gts, eg, eu, ed)


def local(
    query_input,
    key_input,
    value_input,
    gate_logits,
    comp_weight,
    out_proj,
    residual_in,
    ffn_gain,
    expert_ids,
    route_gates,
    expert_gate,
    expert_up,
    expert_down,
):
    gates = gate_logits.transpose(0, 2, 1)
    return run(
        query_input, key_input, value_input, gates, comp_weight.transpose(0, 2, 1), out_proj.T,
        residual_in, ffn_gain.reshape(1, 7168), expert_ids.T, route_gates.T,
        expert_gate[0], expert_up[0], expert_down[0],
    )


def solution(mesh):
    in_specs = (
        P("ctx", "exp"),
        P("ctx", "exp"),
        P("ctx", "exp"),
        P(None, "ctx", "exp"),
        P(None, None, "exp"),
        P("exp", "ctx"),
        P(("ctx", "exp"), None),
        P(),
        P(("ctx", "exp"), None),
        P(("ctx", "exp"), None),
        P("exp", None, "ctx"),
        P("exp", None, "ctx"),
        P("exp", "ctx", None),
    )
    out_specs = P(("ctx", "exp"), None)
    return jax.shard_map(local, mesh=mesh, in_specs=in_specs, out_specs=out_specs, check_vma=False)
```

```python
import math

import jax
import jax.numpy as jnp
from jax import lax
from jax.experimental import pallas as pl
from jax.experimental.pallas import tpu as pltpu
from jax.sharding import PartitionSpec as P

MESH = pl.DeviceIdType.MESH
BF = jnp.bfloat16
F32 = jnp.float32
WINDOW = 512
SCALE = 2.0 / math.sqrt(128)
EPS = 1e-06


def place():
    c = lax.axis_index("ctx")
    e = lax.axis_index("exp")
    return lax.div(c, 2), lax.rem(c, 2), e


def greet(devices):
    bar = pltpu.get_barrier_semaphore()
    for d in devices:
        pl.semaphore_signal(bar, inc=1, device_id=d, device_id_type=MESH)
    pl.semaphore_wait(bar, len(devices))


def rcopy(src, dst, ss, rs, dev):
    return pltpu.make_async_remote_copy(
        src_ref=src, dst_ref=dst, send_sem=ss, recv_sem=rs, device_id=dev, device_id_type=MESH
    )


def unit(x):
    return x * lax.rsqrt(jnp.mean(x * x, axis=1, keepdims=True) + EPS)


def attend(z, core, e, q, k, v, g, cw, wo, wpair, xb, kb, vb, qb, gb, gs, hk, hv, cb, tb, ss, rs, ls):
    other = 1 - core
    up, down = lax.rem(z + 1, 8), lax.rem(z + 7, 8)
    sib = (2 * z + other, e)
    peers = [(2 * lax.rem(z + j, 8) + core, e) for j in range(1, 8)]
    off_other = pl.multiple_of(other * 256, 256)
    off = pl.multiple_of(core * 256, 256)
    near = []
    for a, (src, dst) in enumerate(((k, kb), (v, vb))):
        for kk in range(2):
            near.append(
                rcopy(
                    src.at[:, pl.ds(kk * 256, 256)],
                    dst.at[1, core],
                    ss.at[8 + 2 * kk + a],
                    rs.at[8 + 2 * core + a],
                    (2 * up + kk, e),
                )
            )
    halo = []
    for kk in range(2):
        for a, (src, dst) in enumerate(((k, hk), (v, hv))):
            halo.append(
                rcopy(
                    src.at[pl.ds(0, 16), pl.ds(kk * 256, 256)],
                    dst,
                    ss.at[16 + 2 * kk + a],
                    rs.at[16 + a],
                    (2 * down + kk, e),
                )
            )

    @pl.when(core == 0)
    def _():
        for cp in halo:
            cp.start()

    rows = pl.ds(pl.multiple_of(core * 448, 64), 448)
    own = [
        pltpu.make_async_copy(k.at[:, pl.ds(off, 256)], kb.at[2, core], ls.at[0]),
        pltpu.make_async_copy(v.at[:, pl.ds(off, 256)], vb.at[2, core], ls.at[1]),
        pltpu.make_async_copy(q.at[:, pl.ds(off, 256)], qb.at[core], ls.at[2]),
        pltpu.make_async_copy(wo, wpair.at[rows], ls.at[3]),
    ]
    swap = [
        rcopy(k.at[:, pl.ds(off_other, 256)], kb.at[2, core], ss.at[0], rs.at[0], sib),
        rcopy(v.at[:, pl.ds(off_other, 256)], vb.at[2, core], ss.at[1], rs.at[1], sib),
        rcopy(q.at[:, pl.ds(off_other, 256)], qb.at[core], ss.at[2], rs.at[2], sib),
        rcopy(g, gb.at[core], ss.at[3], rs.at[3], sib),
    ]
    for cp in swap:
        cp.start()
    for cp in near:
        cp.start()
    for cp in own:
        cp.start()
    share = [
        rcopy(wo, wpair.at[rows], ss.at[4], rs.at[4], sib),
    ]
    for cp in share:
        cp.start()

    gb[core] = g[...]

    relay = []

    def pass_on(a, buf):
        for n in range(2):
            rcopy(buf.at[1, n], buf.at[1, n], ss.at[8], rs.at[8 + 2 * n + a], sib).wait_recv()
            cp = rcopy(
                buf.at[1, n],
                buf.at[0, n],
                ss.at[12 + 2 * n + a],
                rs.at[12 + 2 * n + a],
                (2 * up + core, e),
            )
            cp.start()
            relay.append(cp)

    gs[...] = jnp.zeros_like(gs)
    gs[0, 0:4, 0:32] = cw[0]
    gs[0, 4:8, 0:32] = cw[1]
    weights = gs[0].T[0:32]
    lane = lax.broadcasted_iota(jnp.int32, (1, 128), 1)

    def squeeze(a, blocks, tail):
        for h in range(2):
            hs = h * 128
            last = jnp.where(z == 7, 0.0, tail[:, hs : hs + 128].astype(F32))
            x = jnp.concatenate(
                [
                    blocks[2, 0, :, hs : hs + 128].astype(F32),
                    blocks[2, 1, :, hs : hs + 128].astype(F32),
                    last,
                ],
                0,
            ).reshape(17, 16, 128)
            w = jnp.sum(jnp.where(lane == 4 * a + 2 * core + h, weights, 0.0), axis=1, keepdims=True)
            w = jnp.broadcast_to(w, (32, 128))
            y = jnp.sum(x[:16] * w[None, :16], axis=1) + jnp.sum(x[1:] * w[None, 16:], axis=1)
            if a == 0:
                y = unit(y)
            cb[z, a, :, hs : hs + 128] = y.astype(BF)

    for cp in own:
        cp.wait()
    for cp in swap:
        cp.wait_recv()
    for cp in halo[:2]:
        cp.wait_recv()
    squeeze(0, kb, hk)
    squeeze(1, vb, hv)
    comps = [
        rcopy(cb.at[z], cb.at[z], ss.at[20 + j], rs.at[20 + j], peers[j - 1]) for j in range(1, 8)
    ]
    for cp in comps:
        cp.start()
    pass_on(0, kb)
    pass_on(1, vb)
    for cp in comps:
        cp.wait_recv()
    for cp in relay:
        cp.wait_recv()

    pos = z * 256 + lax.broadcasted_iota(jnp.int32, (256, 1), 0)
    block_end = lax.broadcasted_iota(jnp.int32, (1, 128), 1) * 16 + 31
    key_pos = (z - 2) * 256 + lax.broadcasted_iota(jnp.int32, (1, 768), 1)
    for n in range(2):
        gs[n, 0:4] = gb[n, 0]
        gs[n, 4:8] = gb[n, 1]
    gates = jnp.concatenate([gs[0].T, gs[1].T], 0)
    gates = 1.0 / (1.0 + jnp.exp(-gates))
    for h in range(2):
        hs = h * 128
        qn = unit(qb[:, :, hs : hs + 128].reshape(256, 128).astype(F32)).astype(BF)
        ck = cb[:, 0, :, hs : hs + 128].reshape(128, 128)
        cv = cb[:, 1, :, hs : hs + 128].reshape(128, 128)
        s1 = lax.dot_general(qn, ck, (((1,), (1,)), ((), ())), preferred_element_type=F32)
        w1 = jnp.where(block_end <= pos, jnp.exp(SCALE * s1), 0.0)
        t1 = jnp.sum(w1, axis=1, keepdims=True) + (pos < 31).astype(F32)
        o1 = jnp.dot(w1.astype(BF), cv, preferred_element_type=F32) / t1
        kn = unit(kb[:, :, :, hs : hs + 128].reshape(768, 128).astype(F32)).astype(BF)
        vn = vb[:, :, :, hs : hs + 128].reshape(768, 128)
        s2 = lax.dot_general(qn, kn, (((1,), (1,)), ((), ())), preferred_element_type=F32)
        inside = (key_pos <= pos) & (key_pos > pos - WINDOW) & (key_pos >= 0)
        w2 = jnp.where(inside, jnp.exp(SCALE * s2), 0.0)
        t2 = jnp.sum(w2, axis=1, keepdims=True)
        o2 = jnp.dot(w2.astype(BF), vn, preferred_element_type=F32) / t2
        g1 = jnp.sum(jnp.where(lane == 2 * core + h, gates, 0.0), axis=1, keepdims=True)
        g2 = jnp.sum(jnp.where(lane == 4 + 2 * core + h, gates, 0.0), axis=1, keepdims=True)
        tb[:, :, hs : hs + 128] = (g1 * o1 + g2 * o2).astype(BF).reshape(2, 128, 128)
    back = rcopy(tb.at[other], xb.at[z, core], ss.at[28], rs.at[28], sib)
    back.start()
    xb[z, core] = tb[core]

    def drain():
        @pl.when(core == 0)
        def _():
            for cp in halo:
                cp.wait_send()

        for cp in swap + near + comps + relay + share + [back]:
            cp.wait_send()

    return share[0], back, drain


def z_ring(buf, z, core, e, ss, rs, turn):
    up, down = lax.rem(z + 1, 8), lax.rem(z + 7, 8)

    def copy(way, step, chunk):
        block = lax.rem(z + 8 - step, 8) if way == 0 else lax.rem(z + step, 8)
        slot = way * 7 + 2 * step + (chunk if step < 3 else 0)
        return rcopy(
            buf.at[block, lax.rem(chunk + turn, 2)],
            buf.at[block, lax.rem(chunk + turn, 2)],
            ss.at[slot],
            rs.at[slot],
            (2 * (up if way == 0 else down) + core, e),
        )

    def chunks(way, step):
        return (0, 1) if step < 3 else ((0,) if way == 0 else (1,))

    return copy, chunks


def gather_start(copy, chunk, sent, flip=0):
    for way in (0, 1):
        cp = copy(way, 0, (chunk + way * flip) % 2)
        cp.start()
        sent.append(cp)


def gather_step(copy, chunks, step, sent, flip=0):
    for n in (0, 1):
        for way in (0, 1):
            chunk = (n + way * flip) % 2
            if chunk in chunks(way, step):
                copy(way, step, chunk).wait_recv()
                if step < 3 and chunk in chunks(way, step + 1):
                    cp = copy(way, step + 1, chunk)
                    cp.start()
                    sent.append(cp)


DA = 4096
DB = 7168 - DA
HA = 3584
HB = 7168 - HA
NEAR = ((0, 1, 7, 2), (6, 3, 5, 4))


def three(x):
    a = x.astype(BF)
    r = x - a.astype(F32)
    b = r.astype(BF)
    return jnp.concatenate([a, b, (r - b.astype(F32)).astype(BF)], 0)


def turned(x):
    if x.shape[0] < 128:
        x = jnp.concatenate([x, jnp.zeros((128 - x.shape[0], 128), F32)], 0)
    return x.T


def one(cond):
    return jnp.where(cond, 1.0, 0.0)


def tail(
    q, k, v, g, cw, wo, res, gain, ids, gts, eg, eu, ed,
    out,
    wp, kb, vb, qb, gb, gs, hk, hv, cb, tb, s0, r0, l0,
    sc, inf, hs, hid,
    xb, pb, a1, a2, a3, sb, c2, rb, ss, rs, s1, r1, s2, r2, s3, r3, si, ri,
    gw, dw, ys, sw, rw, ls,
    oa, aa, xa, ya, rv, mx, fs, ro, ra, tk, tr, sB, aB, yB, rB, zs, zr,
    sa, qa, sg, qg, st, qt, sx, qx, sy, qy, sv, qv, sh, qh, sz, qz,
):
    z, core, e = place()
    ex, ey = lax.div(e, 4), lax.rem(e, 4)
    c = 2 * z + core
    sib = (2 * z + 1 - core, e)
    ring = [
        (ex, lambda t: (c, 4 * lax.rem(t, 4) + ey)),
        (ey, lambda t: (c, 4 * ex + lax.rem(t, 4))),
    ]
    zp = [(2 * lax.rem(z + j, 8) + core, e) for j in range(1, 8)]
    plane = [(c, lax.rem(e + j, 16)) for j in range(1, 16)]
    cross = [(2 * lax.rem(z + j, 8) + 1 - core, e) for j in (1, 7)]
    greet(plane + zp + [sib] + cross)
    outw, swapped, drain = attend(
        z, core, e, q, k, v, g, cw, wo, wp, xb, kb, vb, qb, gb, gs, hk, hv, cb, tb, s0, r0, l0
    )

    copy, chunks = z_ring(xb, z, core, e, ss, rs, core)
    sent = []
    gather_start(copy, 0, sent)

    share = []
    for n, src in enumerate((eg, eu)):
        share.append(rcopy(src, gw.at[:, pl.ds(256 * n + 128, 128)], sw.at[n], rw.at[n], sib))
    share.append(rcopy(ed, dw.at[pl.ds(128, 128), :], sw.at[2], rw.at[2], sib))
    load = [
        pltpu.make_async_copy(eg, gw.at[:, pl.ds(0, 128)], ls.at[0]),
        pltpu.make_async_copy(eu, gw.at[:, pl.ds(256, 128)], ls.at[1]),
        pltpu.make_async_copy(ed, dw.at[pl.ds(0, 128), :], ls.at[2]),
    ]
    for cp in share + load:
        cp.start()

    sc[...] = jnp.zeros_like(sc)
    sc[0:2, 0:8] = ids[...].astype(F32)
    sc[2:4, 0:8] = gts[...]
    cols = sc[...].T
    id0, id1, g0, g1 = (cols[0:8, n : n + 1] for n in range(4))
    lane = lax.broadcasted_iota(jnp.int32, (8, 128), 1)
    lanef = lane.astype(F32)
    named = one(lanef == id0) + one(lanef == id1)
    before, rows = jnp.zeros((1, 128), F32), []
    for t in range(8):
        rows.append(before)
        before = before + named[t : t + 1]
    count = jnp.concatenate(rows, 0)

    def target(i):
        return 2.0 * i + jnp.sum(jnp.where(lanef == i, count, 0.0), axis=1, keepdims=True)

    t0, t1 = target(id0), target(id1)
    inf[0] = jnp.where(
        lane == 0, t0, jnp.where(lane == 1, t1, jnp.where(lane == 2, g0, jnp.where(lane == 3, g1, 0.0)))
    )
    told = [rcopy(inf.at[0], inf.at[8 - j], si.at[j], ri.at[j], zp[j - 1]) for j in range(1, 8)]
    for cp in told:
        cp.start()

    def partial(block, r):
        x0, x1 = xb[block, 0], xb[block, 1]
        dims = (((1,), (1,)), ((), ()))
        y = lax.dot_general(x0, wp[:, :256], dims, preferred_element_type=F32)
        y = y + lax.dot_general(x1, wp[:, 256:], dims, preferred_element_type=F32)
        pb[r] = y.reshape(4, 4, 8, 896).astype(BF)

    swapped.wait_recv()
    gather_start(copy, 1, sent)
    outw.wait_recv()

    def ring_sum(which, g, half, piece, first, second, mixed, ssem, rsem):
        p, dev = ring[which]
        nxt, prv = dev(p + 1), dev(p + 3)
        base = 12 * g + 6 * half
        far, nt, pt = lax.rem(p + 2, 4), lax.rem(p + 1, 4), lax.rem(p + 3, 4)
        legs = [
            (piece(far, 0), first.at[g, half, 0], nxt),
            (piece(far, 1), first.at[g, half, 1], prv),
            (piece(nt, 1), second.at[g, half, 0, 1], nxt),
            (piece(pt, 0), second.at[g, half, 1, 0], prv),
            (mixed.at[g, half, 0], second.at[g, half, 0, 0], nxt),
            (mixed.at[g, half, 1], second.at[g, half, 1, 1], prv),
        ]
        cps = [
            rcopy(src, dst, ssem.at[base + n], rsem.at[base + n], dev)
            for n, (src, dst, dev) in enumerate(legs)
        ]

        def start():
            for cp in cps[:4]:
                cp.start()

        def middle():
            for n, t in ((0, nt), (1, pt)):
                cps[n].wait_recv()
                mixed[g, half, n] = (
                    first[g, half, n].astype(F32) + piece(t, n)[...].astype(F32)
                ).astype(BF)
                cps[4 + n].start()

        def end():
            for cp in cps[2:]:
                cp.wait_recv()
            return [
                piece(p, n)[...].astype(F32)
                + second[g, half, 0, n].astype(F32)
                + second[g, half, 1, n].astype(F32)
                for n in range(2)
            ]

        def drain():
            for cp in cps:
                cp.wait_send()

        return start, middle, end, drain

    def piece_a(g):
        return lambda t, n: pb.at[4 * g + n, t]

    def piece_b(g):
        return lambda t, n: pb.at[4 * g + 2 + n, :, t]

    wide = [
        [
            ring_sum(0, g, 0, piece_a(g), a1, a2, a3, s1, r1),
            ring_sum(1, g, 1, piece_b(g), a1, a2, a3, s1, r1),
        ]
        for g in range(2)
    ]
    thin = []
    moved = []

    def fan(g, stage):
        for r in wide[g]:
            r[stage]()

    def turn(g):
        for half in range(2):
            for n, y in enumerate(wide[g][half][2]()):
                sb[g, half, :, n] = y.astype(BF)
            p, dev = ring[1 - half]
            for j in (2, 1, 3):
                n = 4 * (2 * g + half) + j
                cp = rcopy(
                    sb.at[g, half, lax.rem(p + j, 4)], c2.at[g, half, j], s2.at[n], r2.at[n], dev(p + j)
                )
                cp.start()
                thin.append(cp)

    def move(g):
        for half in range(2):
            for cp in thin[6 * g + 3 * half : 6 * g + 3 * half + 3]:
                cp.wait_recv()
            total = sb[g, half, ring[1 - half][0]].astype(F32)
            for j in range(1, 4):
                total = total + c2[g, half, j].astype(F32)
            for n in range(2):
                r = NEAR[g][2 * half + n]
                rb[r] = total[n].astype(BF)
                if r:
                    cp = rcopy(rb.at[r], hid.at[z], s3.at[r], r3.at[r], zp[r - 1])
                    cp.start()
                    moved.append(cp)
                else:
                    hid[z] = rb[0]

    def partial(place):
        r = NEAR[place // 4][place % 4]
        block = lax.rem(z + r, 8)
        x0, x1 = xb[block, 0], xb[block, 1]
        dims = (((1,), (1,)), ((), ()))
        y = lax.dot_general(x0, wp[:, :256], dims, preferred_element_type=F32)
        y = y + lax.dot_general(x1, wp[:, 256:], dims, preferred_element_type=F32)
        pb[place] = y.reshape(4, 4, 8, 896).astype(BF)

    partial(0)
    gather_step(copy, chunks, 0, sent)
    partial(1)
    partial(2)
    gather_step(copy, chunks, 1, sent)
    partial(3)
    fan(0, 0)
    partial(4)
    gather_step(copy, chunks, 2, sent)
    fan(0, 1)
    partial(5)
    partial(6)
    turn(0)
    gather_step(copy, chunks, 3, sent)
    partial(7)
    fan(1, 0)
    move(0)
    fan(1, 1)
    turn(1)
    move(1)

    for cp in told:
        cp.wait_recv()
    mine0 = (lanef == t0) | (lanef == t1)
    spread_a = turned(one(mine0))[:32, :16].astype(BF)
    weigh_a = three((jnp.where(lanef == t0, g0, 0.0) + jnp.where(lanef == t1, g1, 0.0))[:, :32])
    slot = lax.broadcasted_iota(jnp.int32, (32, 128), 1)
    token = lax.broadcasted_iota(jnp.int32, (32, 128), 0)
    slotf = (2 * lax.div(slot, 8) + lax.rem(slot, 2)).astype(F32)
    same = lax.rem(lax.div(slot, 2), 4) == lax.div(token, 8)
    spread_b, weigh_b = [], []
    for g in range(2):
        t = jnp.concatenate([inf[r] for r in NEAR[g]], 0)
        hit0, hit1 = same & (slotf == t[:, 0:1]), same & (slotf == t[:, 1:2])
        spread_b.append(turned(one(hit0 | hit1))[:, :32].astype(BF))
        weigh_b.append(three(jnp.where(hit0, t[:, 2:3], 0.0) + jnp.where(hit1, t[:, 3:4], 0.0)))
    pr = lax.broadcasted_iota(jnp.int32, (128, 128), 0)
    pc = lax.broadcasted_iota(jnp.int32, (128, 128), 1)

    def plane_place(n):
        return lax.rem(lax.div(n, 2), 16) * 8 + lax.div(n, 32) * 2 + lax.rem(n, 2)

    order = one(pc == plane_place(pr)).astype(BF)
    unorder = one(pr == plane_place(pc)).astype(BF)

    for cp in moved:
        cp.wait_recv()
    for n in range(8):
        lo, hi = 896 * n, 896 * n + 896
        hs[:, lo:hi] = res[:, lo:hi].astype(F32) + hid[n].astype(F32)
    h = hs[...]
    normed = h * lax.rsqrt(jnp.mean(h * h, axis=1, keepdims=True) + EPS) * gain[...]

    tk[...] = normed[:, DA:].astype(BF)
    tr[0] = tk[...]
    spoke = []
    for j in (1, 7, 2, 6, 3, 5, 4):
        cp = rcopy(tk, tr.at[8 - j], st.at[j], qt.at[8 - j], zp[j - 1])
        cp.start()
        spoke.append(cp)

    padded = jnp.concatenate([normed[:, :DA], jnp.zeros((8, DA), F32)], 0).astype(BF)
    fs[:, :DA] = jnp.dot(spread_a, padded, preferred_element_type=F32)
    for i in range(16):
        oa[i] = fs[2 * i : 2 * i + 2, :DA].astype(BF)
    go = []
    for j in range(1, 16):
        cp = rcopy(oa.at[lax.rem(e + j, 16)], aa.at[e], sa.at[j], qa.at[j], plane[j - 1])
        cp.start()
        go.append(cp)
    aa[e] = oa[e]

    def heard(r):
        rcopy(tk, tr.at[r], st.at[0], qt.at[r], sib).wait_recv()

    def scatter(g):
        for r in NEAR[g]:
            if r:
                heard(r)
        x = jnp.concatenate([tr[r].astype(F32) for r in NEAR[g]], 0).astype(BF)
        y = jnp.dot(spread_b[g], x, preferred_element_type=F32)
        sB[g] = y.reshape(16, 8, DB).astype(BF)
        for j in range(1, 16):
            cp = rcopy(
                sB.at[g, lax.rem(e + j, 16)], aB.at[g, e], sg.at[g, j], qg.at[g, j], plane[j - 1]
            )
            cp.start()
            go.append(cp)
        aB[g, e] = sB[g, e]

    scatter(0)
    for cp in go[:15]:
        cp.wait_recv()
    for i in range(16):
        fs[2 * i : 2 * i + 2, :DA] = aa[i].astype(F32)
    xa[z, 0] = fs[0:16, :DA].astype(BF)
    xa[z, 1] = fs[16:32, :DA].astype(BF)
    copy2, chunks2 = z_ring(xa, z, core, e, sx, qx, 0)
    sent2 = []
    gather_start(copy2, 0, sent2, 1)
    gather_start(copy2, 1, sent2, 1)
    scatter(1)
    for cp in load:
        cp.wait()
    for cp in share:
        cp.wait_recv()

    home = []

    def early(g):
        for j in range(1, 16):
            rcopy(sB.at[g, 0], aB.at[g, 0], sg.at[g, j], qg.at[g, j], sib).wait_recv()
        x = aB[g].astype(F32).reshape(128, DB).astype(BF)
        x = jnp.dot(order, x, preferred_element_type=F32).astype(BF)
        ys[...] = jnp.dot(x, gw[DA:, :], preferred_element_type=F32)

    def work(g):
        blocks = [lax.rem(z + r, 8) for r in NEAR[g]]
        x = jnp.concatenate([xa[b, n] for b in blocks for n in range(2)], 0)
        y = jnp.dot(x, gw[0:DA, :], preferred_element_type=F32) + ys[...]
        gate, lift = y[:, :256], y[:, 256:]
        act = (gate / (1.0 + jnp.exp(-gate)) * lift).astype(BF)
        actp = jnp.dot(unorder, act, preferred_element_type=F32).astype(BF)

        @pl.loop(0, HB // 512)
        def _(n):
            cols = pl.ds(pl.multiple_of(n * 512, 512), 512)
            dcols = pl.ds(pl.multiple_of(HA + n * 512, 512), 512)
            y = jnp.dot(actp, dw[:, dcols], preferred_element_type=F32)
            yB[g, :, :, cols] = y.reshape(16, 8, 512).astype(BF)

        for j in range(1, 16):
            cp = rcopy(
                yB.at[g, lax.rem(e + j, 16)], rB.at[g, e], sy.at[g, j], qy.at[g, j], plane[j - 1]
            )
            cp.start()
            home.append(cp)
        rB[g, e] = yB[g, e]

        @pl.loop(0, HA // 512)
        def _(n):
            cols = pl.ds(pl.multiple_of(n * 512, 512), 512)
            y = jnp.dot(act, dw[:, cols], preferred_element_type=F32).astype(BF)
            for i, b in enumerate(blocks):
                ya[b, 0, :, cols] = y[32 * i : 32 * i + 16]
                ya[b, 1, :, cols] = y[32 * i + 16 : 32 * i + 32]

    gather_step(copy2, chunks2, 0, sent2, 1)
    gather_step(copy2, chunks2, 1, sent2, 1)
    early(0)
    work(0)
    gather_step(copy2, chunks2, 2, sent2, 1)
    early(1)
    gather_step(copy2, chunks2, 3, sent2, 1)
    work(1)

    up, down = zp[0], zp[6]

    def leg(way, n, src):
        return rcopy(
            src, rv.at[way, n], sv.at[way * 7 + n], qv.at[way * 7 + n], up if way == 0 else down
        )

    def mine(way, dist, first):
        block = lax.rem(z + dist, 8) if way == 0 else lax.rem(z + 8 - dist, 8)
        return ya.at[block, first if way == 0 else 1 - first]

    back = []

    def send(way, n, src):
        cp = leg(way, n, src)
        cp.start()
        back.append(cp)

    for way in (0, 1):
        send(way, 0, mine(way, 4, 0))
    for way in (0, 1):
        send(way, 2, mine(way, 3, 1))

    def along(n, dist, first, source):
        for way in (0, 1):
            leg(way, source, rv.at[way, source]).wait_recv()
            mx[way, n] = (
                rv[way, source].astype(F32) + mine(way, dist, first)[...].astype(F32)
            ).astype(BF)
            send(way, n, mx.at[way, n])

    part = []

    def gather_home(g):
        for j in range(1, 16):
            rcopy(yB.at[g, 0], rB.at[g, 0], sy.at[g, j], qy.at[g, j], sib).wait_recv()
        x = rB[g].astype(F32).reshape(128, HB).astype(BF)
        y = jnp.dot(weigh_b[g], x, preferred_element_type=F32)
        y = y[0:32] + y[32:64] + y[64:96]
        for i, r in enumerate(NEAR[g]):
            zs[r] = y[8 * i : 8 * i + 8].astype(BF)
            if r:
                cp = rcopy(zs.at[r], zr.at[8 - r], sz.at[r], qz.at[8 - r], zp[r - 1])
                cp.start()
                part.append(cp)

    along(1, 3, 0, 0)
    along(4, 2, 1, 2)
    along(3, 2, 0, 1)
    gather_home(0)
    along(6, 1, 1, 4)
    along(5, 1, 0, 3)
    for chunk in range(2):
        total = ya[z, chunk].astype(F32)
        for way in (0, 1):
            n = 5 + (chunk if way == 0 else 1 - chunk)
            leg(way, n, rv.at[way, n]).wait_recv()
            total = total + rv[way, n].astype(F32)
        fs[16 * chunk : 16 * chunk + 16, :HA] = total
    for i in range(16):
        ro[i] = fs[2 * i : 2 * i + 2, :HA].astype(BF)
    last = []
    for j in range(1, 16):
        cp = rcopy(ro.at[lax.rem(e + j, 16)], ra.at[e], sh.at[j], qh.at[j], plane[j - 1])
        cp.start()
        last.append(cp)
    ra[e] = ro[e]
    gather_home(1)
    for cp in last:
        cp.wait_recv()
    for i in range(16):
        fs[2 * i : 2 * i + 2, :HA] = ra[i].astype(F32)
    y = jnp.dot(weigh_a, fs[:, :HA].astype(BF), preferred_element_type=F32)
    out[:, :HA] = (hs[:, :HA] + (y[0:8] + y[8:16] + y[16:24])).astype(BF)
    total = hs[:, HA:] + zs[0].astype(F32)
    for r in range(1, 8):
        rcopy(zs.at[0], zr.at[r], sz.at[0], qz.at[r], sib).wait_recv()
        total = total + zr[r].astype(F32)
    out[:, HA:] = total.astype(BF)

    drain()
    for r in wide[0] + wide[1]:
        r[3]()
    for cp in sent + share + told + thin + moved + spoke + go + sent2 + home + back + part + last:
        cp.wait_send()


def run(q, k, v, g, cw, wo, res, gain, ids, gts, eg, eu, ed):
    vm = pl.BlockSpec(memory_space=pltpu.VMEM)
    hbm = pl.BlockSpec(memory_space=pltpu.HBM)

    def dma(*shape):
        return pltpu.SemaphoreType.DMA(shape)

    def bf(*shape):
        return pltpu.VMEM(shape, BF)

    def f32(*shape):
        return pltpu.VMEM(shape, F32)

    return pl.pallas_call(
        tail,
        out_shape=jax.ShapeDtypeStruct((8, 7168), BF),
        in_specs=[hbm] * 3 + [vm] * 2 + [hbm] + [vm] * 4 + [hbm] * 3,
        out_specs=vm,
        scratch_shapes=[
            bf(896, 512),
            bf(3, 2, 128, 256),
            bf(3, 2, 128, 256),
            bf(2, 128, 256),
            f32(2, 2, 4, 128),
            f32(2, 128, 128),
            bf(16, 256),
            bf(16, 256),
            bf(8, 2, 16, 256),
            bf(2, 128, 256),
            dma(29), dma(29), dma(4),
            f32(128, 128),
            f32(8, 8, 128),
            f32(8, 7168),
            bf(8, 8, 896),
            bf(8, 2, 128, 256),
            bf(8, 4, 4, 8, 896),
            bf(2, 2, 2, 4, 8, 896),
            bf(2, 2, 2, 2, 4, 8, 896),
            bf(2, 2, 2, 4, 8, 896),
            bf(2, 2, 4, 2, 8, 896),
            bf(2, 2, 4, 2, 8, 896),
            bf(8, 8, 896),
            dma(14), dma(14), dma(24), dma(24), dma(16), dma(16), dma(8), dma(8), dma(8), dma(8),
            bf(7168, 512),
            bf(256, 7168),
            f32(128, 512),
            dma(3), dma(3), dma(3),
            bf(16, 2, DA),
            bf(16, 2, DA),
            bf(8, 2, 16, DA),
            bf(8, 2, 16, HA),
            bf(2, 7, 16, HA),
            bf(2, 7, 16, HA),
            f32(32, max(DA, HA)),
            bf(16, 2, HA),
            bf(16, 2, HA),
            bf(8, DB),
            bf(8, 8, DB),
            bf(2, 16, 8, DB),
            bf(2, 16, 8, DB),
            bf(2, 16, 8, HB),
            bf(2, 16, 8, HB),
            bf(8, 8, HB),
            bf(8, 8, HB),
            dma(16), dma(16), dma(2, 16), dma(2, 16), dma(8), dma(8), dma(14), dma(14),
            dma(2, 16), dma(2, 16), dma(14), dma(14), dma(16), dma(16), dma(8), dma(8),
        ],
        compiler_params=pltpu.CompilerParams(
            collective_id=2, has_side_effects=True, vmem_limit_bytes=67043328
        ),
        name="layer",
    )(q, k, v, g, cw, wo, res, gain, ids, gts, eg, eu, ed)


def local(
    query_input,
    key_input,
    value_input,
    gate_logits,
    comp_weight,
    out_proj,
    residual_in,
    ffn_gain,
    expert_ids,
    route_gates,
    expert_gate,
    expert_up,
    expert_down,
):
    gates = gate_logits.transpose(0, 2, 1)
    return run(
        query_input, key_input, value_input, gates, comp_weight.transpose(0, 2, 1), out_proj.T,
        residual_in, ffn_gain.reshape(1, 7168), expert_ids.T, route_gates.T,
        expert_gate[0], expert_up[0], expert_down[0],
    )


def solution(mesh):
    in_specs = (
        P("ctx", "exp"),
        P("ctx", "exp"),
        P("ctx", "exp"),
        P(None, "ctx", "exp"),
        P(None, None, "exp"),
        P("exp", "ctx"),
        P(("ctx", "exp"), None),
        P(),
        P(("ctx", "exp"), None),
        P(("ctx", "exp"), None),
        P("exp", None, "ctx"),
        P("exp", None, "ctx"),
        P("exp", "ctx", None),
    )
    out_specs = P(("ctx", "exp"), None)
    return jax.shard_map(local, mesh=mesh, in_specs=in_specs, out_specs=out_specs, check_vma=False)
```

```python
import math

import jax
import jax.numpy as jnp
from jax import lax
from jax.experimental import pallas as pl
from jax.experimental.pallas import tpu as pltpu
from jax.sharding import PartitionSpec as P

MESH = pl.DeviceIdType.MESH
BF = jnp.bfloat16
F32 = jnp.float32
WINDOW = 512
SCALE = 2.0 / math.sqrt(128)
EPS = 1e-06


def place():
    c = lax.axis_index("ctx")
    e = lax.axis_index("exp")
    return lax.div(c, 2), lax.rem(c, 2), e


def greet(devices):
    bar = pltpu.get_barrier_semaphore()
    for d in devices:
        pl.semaphore_signal(bar, inc=1, device_id=d, device_id_type=MESH)
    pl.semaphore_wait(bar, len(devices))


def rcopy(src, dst, ss, rs, dev):
    return pltpu.make_async_remote_copy(
        src_ref=src, dst_ref=dst, send_sem=ss, recv_sem=rs, device_id=dev, device_id_type=MESH
    )


def unit(x):
    return x * lax.rsqrt(jnp.mean(x * x, axis=1, keepdims=True) + EPS)


def attend(z, core, e, q, k, v, g, cw, wo, wpair, xb, kb, vb, qb, gb, gs, hk, hv, cb, tb, ss, rs, ls):
    other = 1 - core
    up, down = lax.rem(z + 1, 8), lax.rem(z + 7, 8)
    sib = (2 * z + other, e)
    peers = [(2 * lax.rem(z + j, 8) + core, e) for j in range(1, 8)]
    off_other = pl.multiple_of(other * 256, 256)
    off = pl.multiple_of(core * 256, 256)
    near = []
    for a, (src, dst) in enumerate(((k, kb), (v, vb))):
        for kk in range(2):
            near.append(
                rcopy(
                    src.at[:, pl.ds(kk * 256, 256)],
                    dst.at[1, core],
                    ss.at[8 + 2 * kk + a],
                    rs.at[8 + 2 * core + a],
                    (2 * up + kk, e),
                )
            )
    halo = []
    for kk in range(2):
        for a, (src, dst) in enumerate(((k, hk), (v, hv))):
            halo.append(
                rcopy(
                    src.at[pl.ds(0, 16), pl.ds(kk * 256, 256)],
                    dst,
                    ss.at[16 + 2 * kk + a],
                    rs.at[16 + a],
                    (2 * down + kk, e),
                )
            )

    @pl.when(core == 0)
    def _():
        for cp in halo:
            cp.start()

    rows = pl.ds(pl.multiple_of(core * 448, 64), 448)
    own = [
        pltpu.make_async_copy(k.at[:, pl.ds(off, 256)], kb.at[2, core], ls.at[0]),
        pltpu.make_async_copy(v.at[:, pl.ds(off, 256)], vb.at[2, core], ls.at[1]),
        pltpu.make_async_copy(q.at[:, pl.ds(off, 256)], qb.at[core], ls.at[2]),
        pltpu.make_async_copy(wo, wpair.at[rows], ls.at[3]),
    ]
    swap = [
        rcopy(k.at[:, pl.ds(off_other, 256)], kb.at[2, core], ss.at[0], rs.at[0], sib),
        rcopy(v.at[:, pl.ds(off_other, 256)], vb.at[2, core], ss.at[1], rs.at[1], sib),
        rcopy(q.at[:, pl.ds(off_other, 256)], qb.at[core], ss.at[2], rs.at[2], sib),
        rcopy(g, gb.at[core], ss.at[3], rs.at[3], sib),
    ]
    for cp in swap:
        cp.start()
    for cp in near:
        cp.start()
    for cp in own:
        cp.start()
    share = [
        rcopy(wo, wpair.at[rows], ss.at[4], rs.at[4], sib),
    ]
    for cp in share:
        cp.start()

    gb[core] = g[...]

    relay = []

    def pass_on(a, buf):
        for n in range(2):
            rcopy(buf.at[1, n], buf.at[1, n], ss.at[8], rs.at[8 + 2 * n + a], sib).wait_recv()
            cp = rcopy(
                buf.at[1, n],
                buf.at[0, n],
                ss.at[12 + 2 * n + a],
                rs.at[12 + 2 * n + a],
                (2 * up + core, e),
            )
            cp.start()
            relay.append(cp)

    gs[...] = jnp.zeros_like(gs)
    gs[0, 0:4, 0:32] = cw[0]
    gs[0, 4:8, 0:32] = cw[1]
    weights = gs[0].T[0:32]
    lane = lax.broadcasted_iota(jnp.int32, (1, 128), 1)

    def squeeze(a, blocks, tail):
        for h in range(2):
            hs = h * 128
            last = jnp.where(z == 7, 0.0, tail[:, hs : hs + 128].astype(F32))
            x = jnp.concatenate(
                [
                    blocks[2, 0, :, hs : hs + 128].astype(F32),
                    blocks[2, 1, :, hs : hs + 128].astype(F32),
                    last,
                ],
                0,
            ).reshape(17, 16, 128)
            w = jnp.sum(jnp.where(lane == 4 * a + 2 * core + h, weights, 0.0), axis=1, keepdims=True)
            w = jnp.broadcast_to(w, (32, 128))
            y = jnp.sum(x[:16] * w[None, :16], axis=1) + jnp.sum(x[1:] * w[None, 16:], axis=1)
            if a == 0:
                y = unit(y)
            cb[z, a, :, hs : hs + 128] = y.astype(BF)

    for cp in own:
        cp.wait()
    for cp in swap:
        cp.wait_recv()
    for cp in halo[:2]:
        cp.wait_recv()
    squeeze(0, kb, hk)
    squeeze(1, vb, hv)
    comps = [
        rcopy(cb.at[z], cb.at[z], ss.at[20 + j], rs.at[20 + j], peers[j - 1])
        for j in (4, 3, 5, 2, 6, 1, 7)
    ]
    for cp in comps:
        cp.start()
    pass_on(0, kb)
    pass_on(1, vb)
    for cp in comps:
        cp.wait_recv()
    for cp in relay:
        cp.wait_recv()

    pos = z * 256 + lax.broadcasted_iota(jnp.int32, (256, 1), 0)
    block_end = lax.broadcasted_iota(jnp.int32, (1, 128), 1) * 16 + 31
    key_pos = (z - 2) * 256 + lax.broadcasted_iota(jnp.int32, (1, 768), 1)
    for n in range(2):
        gs[n, 0:4] = gb[n, 0]
        gs[n, 4:8] = gb[n, 1]
    gates = jnp.concatenate([gs[0].T, gs[1].T], 0)
    gates = 1.0 / (1.0 + jnp.exp(-gates))
    for h in range(2):
        hs = h * 128
        qn = unit(qb[:, :, hs : hs + 128].reshape(256, 128).astype(F32)).astype(BF)
        ck = cb[:, 0, :, hs : hs + 128].reshape(128, 128)
        cv = cb[:, 1, :, hs : hs + 128].reshape(128, 128)
        s1 = lax.dot_general(qn, ck, (((1,), (1,)), ((), ())), preferred_element_type=F32)
        w1 = jnp.where(block_end <= pos, jnp.exp(SCALE * s1), 0.0)
        t1 = jnp.sum(w1, axis=1, keepdims=True) + (pos < 31).astype(F32)
        o1 = jnp.dot(w1.astype(BF), cv, preferred_element_type=F32) / t1
        kn = unit(kb[:, :, :, hs : hs + 128].reshape(768, 128).astype(F32)).astype(BF)
        vn = vb[:, :, :, hs : hs + 128].reshape(768, 128)
        s2 = lax.dot_general(qn, kn, (((1,), (1,)), ((), ())), preferred_element_type=F32)
        inside = (key_pos <= pos) & (key_pos > pos - WINDOW) & (key_pos >= 0)
        w2 = jnp.where(inside, jnp.exp(SCALE * s2), 0.0)
        t2 = jnp.sum(w2, axis=1, keepdims=True)
        o2 = jnp.dot(w2.astype(BF), vn, preferred_element_type=F32) / t2
        g1 = jnp.sum(jnp.where(lane == 2 * core + h, gates, 0.0), axis=1, keepdims=True)
        g2 = jnp.sum(jnp.where(lane == 4 + 2 * core + h, gates, 0.0), axis=1, keepdims=True)
        tb[:, :, hs : hs + 128] = (g1 * o1 + g2 * o2).astype(BF).reshape(2, 128, 128)
    back = rcopy(tb.at[other], xb.at[z, core], ss.at[28], rs.at[28], sib)
    back.start()
    xb[z, core] = tb[core]

    def drain():
        @pl.when(core == 0)
        def _():
            for cp in halo:
                cp.wait_send()

        for cp in swap + near + comps + relay + share + [back]:
            cp.wait_send()

    return share[0], back, drain


def z_ring(buf, z, core, e, ss, rs, turn):
    up, down = lax.rem(z + 1, 8), lax.rem(z + 7, 8)

    def copy(way, step, chunk):
        block = lax.rem(z + 8 - step, 8) if way == 0 else lax.rem(z + step, 8)
        slot = way * 7 + 2 * step + (chunk if step < 3 else 0)
        return rcopy(
            buf.at[block, lax.rem(chunk + turn, 2)],
            buf.at[block, lax.rem(chunk + turn, 2)],
            ss.at[slot],
            rs.at[slot],
            (2 * (up if way == 0 else down) + core, e),
        )

    def chunks(way, step):
        return (0, 1) if step < 3 else ((0,) if way == 0 else (1,))

    return copy, chunks


def gather_start(copy, chunk, sent, flip=0):
    for way in (0, 1):
        cp = copy(way, 0, (chunk + way * flip) % 2)
        cp.start()
        sent.append(cp)


def gather_step(copy, chunks, step, sent, flip=0):
    for n in (0, 1):
        for way in (0, 1):
            chunk = (n + way * flip) % 2
            if chunk in chunks(way, step):
                copy(way, step, chunk).wait_recv()
                if step < 3 and chunk in chunks(way, step + 1):
                    cp = copy(way, step + 1, chunk)
                    cp.start()
                    sent.append(cp)


DA = 4352
DB = 7168 - DA
HA = 3584
HB = 7168 - HA
FAR = (
    (2, 2), (2, 1), (1, 2), (2, 3), (3, 2), (1, 1), (3, 3), (1, 3), (3, 1), (2, 0), (0, 2),
    (1, 0), (0, 1), (3, 0), (0, 3),
)
NEAR = ((0, 1, 7, 2), (6, 3, 5, 4))


def three(x):
    a = x.astype(BF)
    r = x - a.astype(F32)
    b = r.astype(BF)
    return jnp.concatenate([a, b, (r - b.astype(F32)).astype(BF)], 0)


def turned(x):
    if x.shape[0] < 128:
        x = jnp.concatenate([x, jnp.zeros((128 - x.shape[0], 128), F32)], 0)
    return x.T


def one(cond):
    return jnp.where(cond, 1.0, 0.0)


def tail(
    q, k, v, g, cw, wo, res, gain, ids, gts, eg, eu, ed,
    out,
    wp, kb, vb, qb, gb, gs, hk, hv, cb, tb, s0, r0, l0,
    sc, inf, hs, hid,
    xb, pb, a1, a2, a3, sb, c2, rb, ss, rs, s1, r1, s2, r2, s3, r3, si, ri,
    gw, dw, ys, sw, rw, ls,
    oa, aa, xa, ya, rv, mx, fs, ro, ra, tr, sB, aB, yB, rB, zs, zr,
    sa, qa, sg, qg, st, qt, sx, qx, sy, qy, sv, qv, sh, qh, sz, qz,
):
    z, core, e = place()
    ex, ey = lax.div(e, 4), lax.rem(e, 4)
    c = 2 * z + core
    sib = (2 * z + 1 - core, e)
    ring = [
        (ex, lambda t: (c, 4 * lax.rem(t, 4) + ey)),
        (ey, lambda t: (c, 4 * ex + lax.rem(t, 4))),
    ]
    zp = [(2 * lax.rem(z + j, 8) + core, e) for j in range(1, 8)]
    dest = [4 * lax.rem(ex + a, 4) + lax.rem(ey + b, 4) for a, b in FAR]
    plane = [(c, d) for d in dest]
    cross = [(2 * lax.rem(z + j, 8) + 1 - core, e) for j in (1, 7)]
    greet(plane + zp + [sib] + cross)
    outw, swapped, drain = attend(
        z, core, e, q, k, v, g, cw, wo, wp, xb, kb, vb, qb, gb, gs, hk, hv, cb, tb, s0, r0, l0
    )

    copy, chunks = z_ring(xb, z, core, e, ss, rs, core)
    sent = []
    gather_start(copy, 0, sent)

    share = []
    for n, src in enumerate((eg, eu)):
        share.append(rcopy(src, gw.at[:, pl.ds(256 * n + 128, 128)], sw.at[n], rw.at[n], sib))
    share.append(rcopy(ed, dw.at[pl.ds(128, 128), :], sw.at[2], rw.at[2], sib))
    load = [
        pltpu.make_async_copy(eg, gw.at[:, pl.ds(0, 128)], ls.at[0]),
        pltpu.make_async_copy(eu, gw.at[:, pl.ds(256, 128)], ls.at[1]),
        pltpu.make_async_copy(ed, dw.at[pl.ds(0, 128), :], ls.at[2]),
    ]
    for cp in share + load:
        cp.start()

    sc[...] = jnp.zeros_like(sc)
    sc[0:2, 0:8] = ids[...].astype(F32)
    sc[2:4, 0:8] = gts[...]
    cols = sc[...].T
    id0, id1, g0, g1 = (cols[0:8, n : n + 1] for n in range(4))
    lane = lax.broadcasted_iota(jnp.int32, (8, 128), 1)
    lanef = lane.astype(F32)
    named = one(lanef == id0) + one(lanef == id1)
    before, rows = jnp.zeros((1, 128), F32), []
    for t in range(8):
        rows.append(before)
        before = before + named[t : t + 1]
    count = jnp.concatenate(rows, 0)

    def target(i):
        return 2.0 * i + jnp.sum(jnp.where(lanef == i, count, 0.0), axis=1, keepdims=True)

    t0, t1 = target(id0), target(id1)
    inf[0] = jnp.where(
        lane == 0, t0, jnp.where(lane == 1, t1, jnp.where(lane == 2, g0, jnp.where(lane == 3, g1, 0.0)))
    )
    told = [rcopy(inf.at[0], inf.at[8 - j], si.at[j], ri.at[j], zp[j - 1]) for j in range(1, 8)]
    for cp in told:
        cp.start()

    def partial(block, r):
        x0, x1 = xb[block, 0], xb[block, 1]
        dims = (((1,), (1,)), ((), ()))
        y = lax.dot_general(x0, wp[:, :256], dims, preferred_element_type=F32)
        y = y + lax.dot_general(x1, wp[:, 256:], dims, preferred_element_type=F32)
        pb[r] = y.reshape(4, 4, 8, 896).astype(BF)

    swapped.wait_recv()
    gather_start(copy, 1, sent)
    outw.wait_recv()

    def ring_sum(which, g, half, piece, first, second, mixed, ssem, rsem):
        p, dev = ring[which]
        nxt, prv = dev(p + 1), dev(p + 3)
        base = 12 * g + 6 * half
        far, nt, pt = lax.rem(p + 2, 4), lax.rem(p + 1, 4), lax.rem(p + 3, 4)
        legs = [
            (piece(far, 0), first.at[g, half, 0], nxt),
            (piece(far, 1), first.at[g, half, 1], prv),
            (piece(nt, 1), second.at[g, half, 0, 1], nxt),
            (piece(pt, 0), second.at[g, half, 1, 0], prv),
            (mixed.at[g, half, 0], second.at[g, half, 0, 0], nxt),
            (mixed.at[g, half, 1], second.at[g, half, 1, 1], prv),
        ]
        cps = [
            rcopy(src, dst, ssem.at[base + n], rsem.at[base + n], dev)
            for n, (src, dst, dev) in enumerate(legs)
        ]

        def start():
            for cp in cps[:4]:
                cp.start()

        def middle():
            for n, t in ((0, nt), (1, pt)):
                cps[n].wait_recv()
                mixed[g, half, n] = (
                    first[g, half, n].astype(F32) + piece(t, n)[...].astype(F32)
                ).astype(BF)
                cps[4 + n].start()

        def end():
            for cp in cps[2:]:
                cp.wait_recv()
            return [
                piece(p, n)[...].astype(F32)
                + second[g, half, 0, n].astype(F32)
                + second[g, half, 1, n].astype(F32)
                for n in range(2)
            ]

        def drain():
            for cp in cps:
                cp.wait_send()

        return start, middle, end, drain

    def piece_a(g):
        return lambda t, n: pb.at[4 * g + n, t]

    def piece_b(g):
        return lambda t, n: pb.at[4 * g + 2 + n, :, t]

    wide = [
        [
            ring_sum(0, g, 0, piece_a(g), a1, a2, a3, s1, r1),
            ring_sum(1, g, 1, piece_b(g), a1, a2, a3, s1, r1),
        ]
        for g in range(2)
    ]
    thin = []
    moved = []

    def fan(g, stage):
        for r in wide[g]:
            r[stage]()

    def turn(g):
        for half in range(2):
            for n, y in enumerate(wide[g][half][2]()):
                sb[g, half, :, n] = y.astype(BF)
            p, dev = ring[1 - half]
            for j in (2, 1, 3):
                n = 4 * (2 * g + half) + j
                cp = rcopy(
                    sb.at[g, half, lax.rem(p + j, 4)], c2.at[g, half, j], s2.at[n], r2.at[n], dev(p + j)
                )
                cp.start()
                thin.append(cp)

    def move(g):
        for half in range(2):
            for cp in thin[6 * g + 3 * half : 6 * g + 3 * half + 3]:
                cp.wait_recv()
            total = sb[g, half, ring[1 - half][0]].astype(F32)
            for j in range(1, 4):
                total = total + c2[g, half, j].astype(F32)
            for n in range(2):
                r = NEAR[g][2 * half + n]
                rb[r] = total[n].astype(BF)
                if r:
                    cp = rcopy(rb.at[r], hid.at[z], s3.at[r], r3.at[r], zp[r - 1])
                    cp.start()
                    moved.append(cp)
                else:
                    hid[z] = rb[0]

    def partial(place):
        r = NEAR[place // 4][place % 4]
        block = lax.rem(z + r, 8)
        x0, x1 = xb[block, 0], xb[block, 1]
        dims = (((1,), (1,)), ((), ()))
        y = lax.dot_general(x0, wp[:, :256], dims, preferred_element_type=F32)
        y = y + lax.dot_general(x1, wp[:, 256:], dims, preferred_element_type=F32)
        pb[place] = y.reshape(4, 4, 8, 896).astype(BF)

    partial(0)
    gather_step(copy, chunks, 0, sent)
    partial(1)
    partial(2)
    gather_step(copy, chunks, 1, sent)
    partial(3)
    fan(0, 0)
    partial(4)
    gather_step(copy, chunks, 2, sent)
    fan(0, 1)
    partial(5)
    partial(6)
    turn(0)
    gather_step(copy, chunks, 3, sent)
    partial(7)
    fan(1, 0)
    move(0)
    fan(1, 1)
    turn(1)
    move(1)

    for cp in told:
        cp.wait_recv()
    mine0 = (lanef == t0) | (lanef == t1)
    spread_a = turned(one(mine0))[:32, :16].astype(BF)
    weigh_a = three((jnp.where(lanef == t0, g0, 0.0) + jnp.where(lanef == t1, g1, 0.0))[:, :32])
    slot = lax.broadcasted_iota(jnp.int32, (32, 128), 1)
    token = lax.broadcasted_iota(jnp.int32, (32, 128), 0)
    slotf = (2 * lax.div(slot, 8) + lax.rem(slot, 2)).astype(F32)
    same = lax.rem(lax.div(slot, 2), 4) == lax.div(token, 8)
    spread_b, weigh_b = [], []
    for g in range(2):
        t = jnp.concatenate([inf[r] for r in NEAR[g]], 0)
        hit0, hit1 = same & (slotf == t[:, 0:1]), same & (slotf == t[:, 1:2])
        spread_b.append(turned(one(hit0 | hit1))[:, :32].astype(BF))
        weigh_b.append(three(jnp.where(hit0, t[:, 2:3], 0.0) + jnp.where(hit1, t[:, 3:4], 0.0)))
    pr = lax.broadcasted_iota(jnp.int32, (128, 128), 0)
    pc = lax.broadcasted_iota(jnp.int32, (128, 128), 1)

    def plane_place(n):
        return lax.rem(lax.div(n, 2), 16) * 8 + lax.div(n, 32) * 2 + lax.rem(n, 2)

    order = one(pc == plane_place(pr)).astype(BF)
    unorder = one(pr == plane_place(pc)).astype(BF)

    for cp in moved:
        cp.wait_recv()
    for n in range(8):
        lo, hi = 896 * n, 896 * n + 896
        hs[:, lo:hi] = res[:, lo:hi].astype(F32) + hid[n].astype(F32)
    h = hs[...]
    normed = h * lax.rsqrt(jnp.mean(h * h, axis=1, keepdims=True) + EPS) * gain[...]

    tr[0] = normed[:, DA:].astype(BF)
    spoke = []

    def tell(r):
        src, dev = (tr.at[r - 1], zp[6]) if r <= 4 else (tr.at[(r + 1) % 8], zp[0])
        cp = rcopy(src, tr.at[r], st.at[r], qt.at[r], dev)
        cp.start()
        spoke.append(cp)

    def heard(r):
        rcopy(tr.at[0], tr.at[r], st.at[0], qt.at[r], sib).wait_recv()

    tell(1)
    tell(7)

    padded = jnp.concatenate([normed[:, :DA], jnp.zeros((8, DA), F32)], 0).astype(BF)
    fs[:, :DA] = jnp.dot(spread_a, padded, preferred_element_type=F32)
    for i in range(16):
        oa[i] = fs[2 * i : 2 * i + 2, :DA].astype(BF)
    go = []
    for j in range(1, 16):
        cp = rcopy(oa.at[dest[j - 1]], aa.at[e], sa.at[j], qa.at[j], plane[j - 1])
        cp.start()
        go.append(cp)
    aa[e] = oa[e]

    def scatter(g):
        x = jnp.concatenate([tr[r].astype(F32) for r in NEAR[g]], 0).astype(BF)
        y = jnp.dot(spread_b[g], x, preferred_element_type=F32)
        sB[g] = y.reshape(16, 8, DB).astype(BF)
        for j in range(1, 16):
            cp = rcopy(
                sB.at[g, dest[j - 1]], aB.at[g, e], sg.at[g, j], qg.at[g, j], plane[j - 1]
            )
            cp.start()
            go.append(cp)
        aB[g, e] = sB[g, e]

    heard(1)
    tell(2)
    heard(7)
    tell(6)
    heard(2)
    tell(3)
    heard(6)
    tell(5)
    scatter(0)
    for cp in go[:15]:
        cp.wait_recv()
    for i in range(16):
        fs[2 * i : 2 * i + 2, :DA] = aa[i].astype(F32)
    xa[z, 0] = fs[0:16, :DA].astype(BF)
    xa[z, 1] = fs[16:32, :DA].astype(BF)
    copy2, chunks2 = z_ring(xa, z, core, e, sx, qx, 0)
    sent2 = []
    gather_start(copy2, 0, sent2, 1)
    gather_start(copy2, 1, sent2, 1)
    for cp in load:
        cp.wait()
    for cp in share:
        cp.wait_recv()
    heard(3)
    tell(4)
    heard(5)

    home = []

    def early(g):
        for j in range(1, 16):
            rcopy(sB.at[g, 0], aB.at[g, 0], sg.at[g, j], qg.at[g, j], sib).wait_recv()
        x = aB[g].astype(F32).reshape(128, DB).astype(BF)
        x = jnp.dot(order, x, preferred_element_type=F32).astype(BF)
        ys[...] = jnp.dot(x, gw[DA:, :], preferred_element_type=F32)

    def work(g):
        blocks = [lax.rem(z + r, 8) for r in NEAR[g]]
        x = jnp.concatenate([xa[b, n] for b in blocks for n in range(2)], 0)
        y = jnp.dot(x, gw[0:DA, :], preferred_element_type=F32) + ys[...]
        gate, lift = y[:, :256], y[:, 256:]
        act = (gate / (1.0 + jnp.exp(-gate)) * lift).astype(BF)
        actp = jnp.dot(unorder, act, preferred_element_type=F32).astype(BF)

        @pl.loop(0, HB // 512)
        def _(n):
            cols = pl.ds(pl.multiple_of(n * 512, 512), 512)
            dcols = pl.ds(pl.multiple_of(HA + n * 512, 512), 512)
            y = jnp.dot(actp, dw[:, dcols], preferred_element_type=F32)
            yB[g, :, :, cols] = y.reshape(16, 8, 512).astype(BF)

        for j in range(1, 16):
            cp = rcopy(
                yB.at[g, dest[j - 1]], rB.at[g, e], sy.at[g, j], qy.at[g, j], plane[j - 1]
            )
            cp.start()
            home.append(cp)
        rB[g, e] = yB[g, e]

        @pl.loop(0, HA // 512)
        def _(n):
            cols = pl.ds(pl.multiple_of(n * 512, 512), 512)
            y = jnp.dot(act, dw[:, cols], preferred_element_type=F32).astype(BF)
            for i, b in enumerate(blocks):
                ya[b, 0, :, cols] = y[32 * i : 32 * i + 16]
                ya[b, 1, :, cols] = y[32 * i + 16 : 32 * i + 32]

    gather_step(copy2, chunks2, 0, sent2, 1)
    heard(4)
    scatter(1)
    gather_step(copy2, chunks2, 1, sent2, 1)
    early(0)
    work(0)
    gather_step(copy2, chunks2, 2, sent2, 1)
    early(1)
    gather_step(copy2, chunks2, 3, sent2, 1)
    work(1)

    up, down = zp[0], zp[6]

    def leg(way, n, src):
        return rcopy(
            src, rv.at[way, n], sv.at[way * 7 + n], qv.at[way * 7 + n], up if way == 0 else down
        )

    def mine(way, dist, first):
        block = lax.rem(z + dist, 8) if way == 0 else lax.rem(z + 8 - dist, 8)
        return ya.at[block, first if way == 0 else 1 - first]

    back = []

    def send(way, n, src):
        cp = leg(way, n, src)
        cp.start()
        back.append(cp)

    for way in (0, 1):
        send(way, 0, mine(way, 4, 0))
    for way in (0, 1):
        send(way, 2, mine(way, 3, 1))

    def along(n, dist, first, source):
        for way in (0, 1):
            leg(way, source, rv.at[way, source]).wait_recv()
            mx[way, n] = (
                rv[way, source].astype(F32) + mine(way, dist, first)[...].astype(F32)
            ).astype(BF)
            send(way, n, mx.at[way, n])

    part = []

    def gather_home(g):
        for j in range(1, 16):
            rcopy(yB.at[g, 0], rB.at[g, 0], sy.at[g, j], qy.at[g, j], sib).wait_recv()
        x = rB[g].astype(F32).reshape(128, HB).astype(BF)
        y = jnp.dot(weigh_b[g], x, preferred_element_type=F32)
        y = y[0:32] + y[32:64] + y[64:96]
        for i, r in enumerate(NEAR[g]):
            zs[r] = y[8 * i : 8 * i + 8].astype(BF)
            if r:
                cp = rcopy(zs.at[r], zr.at[8 - r], sz.at[r], qz.at[8 - r], zp[r - 1])
                cp.start()
                part.append(cp)

    along(1, 3, 0, 0)
    along(4, 2, 1, 2)
    along(3, 2, 0, 1)
    gather_home(0)
    along(6, 1, 1, 4)
    along(5, 1, 0, 3)
    gather_home(1)
    for chunk in range(2):
        total = ya[z, chunk].astype(F32)
        for way in (0, 1):
            n = 5 + (chunk if way == 0 else 1 - chunk)
            leg(way, n, rv.at[way, n]).wait_recv()
            total = total + rv[way, n].astype(F32)
        fs[16 * chunk : 16 * chunk + 16, :HA] = total
    for i in range(16):
        ro[i] = fs[2 * i : 2 * i + 2, :HA].astype(BF)
    last = []
    for j in range(1, 16):
        cp = rcopy(ro.at[dest[j - 1]], ra.at[e], sh.at[j], qh.at[j], plane[j - 1])
        cp.start()
        last.append(cp)
    ra[e] = ro[e]
    for cp in last:
        cp.wait_recv()
    for i in range(16):
        fs[2 * i : 2 * i + 2, :HA] = ra[i].astype(F32)
    y = jnp.dot(weigh_a, fs[:, :HA].astype(BF), preferred_element_type=F32)
    out[:, :HA] = (hs[:, :HA] + (y[0:8] + y[8:16] + y[16:24])).astype(BF)
    total = hs[:, HA:] + zs[0].astype(F32)
    for r in range(1, 8):
        rcopy(zs.at[0], zr.at[r], sz.at[0], qz.at[r], sib).wait_recv()
        total = total + zr[r].astype(F32)
    out[:, HA:] = total.astype(BF)

    drain()
    for r in wide[0] + wide[1]:
        r[3]()
    for cp in sent + share + told + thin + moved + spoke + go + sent2 + home + back + part + last:
        cp.wait_send()


def run(q, k, v, g, cw, wo, res, gain, ids, gts, eg, eu, ed):
    vm = pl.BlockSpec(memory_space=pltpu.VMEM)
    hbm = pl.BlockSpec(memory_space=pltpu.HBM)

    def dma(*shape):
        return pltpu.SemaphoreType.DMA(shape)

    def bf(*shape):
        return pltpu.VMEM(shape, BF)

    def f32(*shape):
        return pltpu.VMEM(shape, F32)

    return pl.pallas_call(
        tail,
        out_shape=jax.ShapeDtypeStruct((8, 7168), BF),
        in_specs=[hbm] * 3 + [vm] * 2 + [hbm] + [vm] * 4 + [hbm] * 3,
        out_specs=vm,
        scratch_shapes=[
            bf(896, 512),
            bf(3, 2, 128, 256),
            bf(3, 2, 128, 256),
            bf(2, 128, 256),
            f32(2, 2, 4, 128),
            f32(2, 128, 128),
            bf(16, 256),
            bf(16, 256),
            bf(8, 2, 16, 256),
            bf(2, 128, 256),
            dma(29), dma(29), dma(4),
            f32(128, 128),
            f32(8, 8, 128),
            f32(8, 7168),
            bf(8, 8, 896),
            bf(8, 2, 128, 256),
            bf(8, 4, 4, 8, 896),
            bf(2, 2, 2, 4, 8, 896),
            bf(2, 2, 2, 2, 4, 8, 896),
            bf(2, 2, 2, 4, 8, 896),
            bf(2, 2, 4, 2, 8, 896),
            bf(2, 2, 4, 2, 8, 896),
            bf(8, 8, 896),
            dma(14), dma(14), dma(24), dma(24), dma(16), dma(16), dma(8), dma(8), dma(8), dma(8),
            bf(7168, 512),
            bf(256, 7168),
            f32(128, 512),
            dma(3), dma(3), dma(3),
            bf(16, 2, DA),
            bf(16, 2, DA),
            bf(8, 2, 16, DA),
            bf(8, 2, 16, HA),
            bf(2, 7, 16, HA),
            bf(2, 7, 16, HA),
            f32(32, max(DA, HA)),
            bf(16, 2, HA),
            bf(16, 2, HA),
            bf(8, 8, DB),
            bf(2, 16, 8, DB),
            bf(2, 16, 8, DB),
            bf(2, 16, 8, HB),
            bf(2, 16, 8, HB),
            bf(8, 8, HB),
            bf(8, 8, HB),
            dma(16), dma(16), dma(2, 16), dma(2, 16), dma(8), dma(8), dma(14), dma(14),
            dma(2, 16), dma(2, 16), dma(14), dma(14), dma(16), dma(16), dma(8), dma(8),
        ],
        compiler_params=pltpu.CompilerParams(
            collective_id=2, has_side_effects=True, vmem_limit_bytes=67043328
        ),
        name="layer",
    )(q, k, v, g, cw, wo, res, gain, ids, gts, eg, eu, ed)


def local(
    query_input,
    key_input,
    value_input,
    gate_logits,
    comp_weight,
    out_proj,
    residual_in,
    ffn_gain,
    expert_ids,
    route_gates,
    expert_gate,
    expert_up,
    expert_down,
):
    gates = gate_logits.transpose(0, 2, 1)
    return run(
        query_input, key_input, value_input, gates, comp_weight.transpose(0, 2, 1), out_proj.T,
        residual_in, ffn_gain.reshape(1, 7168), expert_ids.T, route_gates.T,
        expert_gate[0], expert_up[0], expert_down[0],
    )


def solution(mesh):
    in_specs = (
        P("ctx", "exp"),
        P("ctx", "exp"),
        P("ctx", "exp"),
        P(None, "ctx", "exp"),
        P(None, None, "exp"),
        P("exp", "ctx"),
        P(("ctx", "exp"), None),
        P(),
        P(("ctx", "exp"), None),
        P(("ctx", "exp"), None),
        P("exp", None, "ctx"),
        P("exp", None, "ctx"),
        P("exp", "ctx", None),
    )
    out_specs = P(("ctx", "exp"), None)
    return jax.shard_map(local, mesh=mesh, in_specs=in_specs, out_specs=out_specs, check_vma=False)
```

```python
import math

import jax
import jax.numpy as jnp
from jax import lax
from jax.experimental import pallas as pl
from jax.experimental.pallas import tpu as pltpu
from jax.sharding import PartitionSpec as P

MESH = pl.DeviceIdType.MESH
BF = jnp.bfloat16
F32 = jnp.float32
WINDOW = 512
SCALE = 2.0 / math.sqrt(128)
EPS = 1e-06


def place():
    c = lax.axis_index("ctx")
    e = lax.axis_index("exp")
    return lax.div(c, 2), lax.rem(c, 2), e


def greet(devices):
    bar = pltpu.get_barrier_semaphore()
    for d in devices:
        pl.semaphore_signal(bar, inc=1, device_id=d, device_id_type=MESH)
    pl.semaphore_wait(bar, len(devices))


def rcopy(src, dst, ss, rs, dev):
    return pltpu.make_async_remote_copy(
        src_ref=src, dst_ref=dst, send_sem=ss, recv_sem=rs, device_id=dev, device_id_type=MESH
    )


def unit(x):
    return x * lax.rsqrt(jnp.mean(x * x, axis=1, keepdims=True) + EPS)


def attend(z, core, e, q, k, v, g, cw, wo, wpair, xb, kb, vb, qb, gb, gs, hk, hv, cb, tb, ss, rs, ls):
    other = 1 - core
    up, down = lax.rem(z + 1, 8), lax.rem(z + 7, 8)
    sib = (2 * z + other, e)
    peers = [(2 * lax.rem(z + j, 8) + core, e) for j in range(1, 8)]
    off_other = pl.multiple_of(other * 256, 256)
    off = pl.multiple_of(core * 256, 256)
    near = []
    for a, (src, dst) in enumerate(((k, kb), (v, vb))):
        for kk in range(2):
            near.append(
                rcopy(
                    src.at[:, pl.ds(kk * 256, 256)],
                    dst.at[1, core],
                    ss.at[8 + 2 * kk + a],
                    rs.at[8 + 2 * core + a],
                    (2 * up + kk, e),
                )
            )
    halo = []
    for kk in range(2):
        for a, (src, dst) in enumerate(((k, hk), (v, hv))):
            halo.append(
                rcopy(
                    src.at[pl.ds(0, 16), pl.ds(kk * 256, 256)],
                    dst,
                    ss.at[16 + 2 * kk + a],
                    rs.at[16 + a],
                    (2 * down + kk, e),
                )
            )

    @pl.when(core == 0)
    def _():
        for cp in halo:
            cp.start()

    rows = pl.ds(pl.multiple_of(core * 448, 64), 448)
    own = [
        pltpu.make_async_copy(k.at[:, pl.ds(off, 256)], kb.at[2, core], ls.at[0]),
        pltpu.make_async_copy(v.at[:, pl.ds(off, 256)], vb.at[2, core], ls.at[1]),
        pltpu.make_async_copy(q.at[:, pl.ds(off, 256)], qb.at[core], ls.at[2]),
        pltpu.make_async_copy(wo, wpair.at[rows], ls.at[3]),
    ]
    swap = [
        rcopy(k.at[:, pl.ds(off_other, 256)], kb.at[2, core], ss.at[0], rs.at[0], sib),
        rcopy(v.at[:, pl.ds(off_other, 256)], vb.at[2, core], ss.at[1], rs.at[1], sib),
        rcopy(q.at[:, pl.ds(off_other, 256)], qb.at[core], ss.at[2], rs.at[2], sib),
        rcopy(g, gb.at[core], ss.at[3], rs.at[3], sib),
    ]
    for cp in swap:
        cp.start()
    for cp in near:
        cp.start()
    for cp in own:
        cp.start()
    share = [
        rcopy(wo, wpair.at[rows], ss.at[4], rs.at[4], sib),
    ]
    for cp in share:
        cp.start()

    gb[core] = g[...]

    relay = []

    def pass_on(a, buf):
        for n in range(2):
            rcopy(buf.at[1, n], buf.at[1, n], ss.at[8], rs.at[8 + 2 * n + a], sib).wait_recv()
            cp = rcopy(
                buf.at[1, n],
                buf.at[0, n],
                ss.at[12 + 2 * n + a],
                rs.at[12 + 2 * n + a],
                (2 * up + core, e),
            )
            cp.start()
            relay.append(cp)

    gs[...] = jnp.zeros_like(gs)
    gs[0, 0:4, 0:32] = cw[0]
    gs[0, 4:8, 0:32] = cw[1]
    weights = gs[0].T[0:32]
    lane = lax.broadcasted_iota(jnp.int32, (1, 128), 1)

    def squeeze(a, blocks, tail):
        for h in range(2):
            hs = h * 128
            last = jnp.where(z == 7, 0.0, tail[:, hs : hs + 128].astype(F32))
            x = jnp.concatenate(
                [
                    blocks[2, 0, :, hs : hs + 128].astype(F32),
                    blocks[2, 1, :, hs : hs + 128].astype(F32),
                    last,
                ],
                0,
            ).reshape(17, 16, 128)
            w = jnp.sum(jnp.where(lane == 4 * a + 2 * core + h, weights, 0.0), axis=1, keepdims=True)
            w = jnp.broadcast_to(w, (32, 128))
            y = jnp.sum(x[:16] * w[None, :16], axis=1) + jnp.sum(x[1:] * w[None, 16:], axis=1)
            if a == 0:
                y = unit(y)
            cb[z, a, :, hs : hs + 128] = y.astype(BF)

    for cp in own:
        cp.wait()
    for cp in swap:
        cp.wait_recv()
    for cp in halo[:2]:
        cp.wait_recv()
    squeeze(0, kb, hk)
    squeeze(1, vb, hv)
    comps = [
        rcopy(cb.at[z], cb.at[z], ss.at[20 + j], rs.at[20 + j], peers[j - 1])
        for j in (4, 3, 5, 2, 6, 1, 7)
    ]
    for cp in comps:
        cp.start()
    pass_on(0, kb)
    pass_on(1, vb)
    for cp in comps:
        cp.wait_recv()
    for cp in relay:
        cp.wait_recv()

    pos = z * 256 + lax.broadcasted_iota(jnp.int32, (256, 1), 0)
    block_end = lax.broadcasted_iota(jnp.int32, (1, 128), 1) * 16 + 31
    key_pos = (z - 2) * 256 + lax.broadcasted_iota(jnp.int32, (1, 768), 1)
    for n in range(2):
        gs[n, 0:4] = gb[n, 0]
        gs[n, 4:8] = gb[n, 1]
    gates = jnp.concatenate([gs[0].T, gs[1].T], 0)
    gates = 1.0 / (1.0 + jnp.exp(-gates))
    for h in range(2):
        hs = h * 128
        qn = unit(qb[:, :, hs : hs + 128].reshape(256, 128).astype(F32)).astype(BF)
        ck = cb[:, 0, :, hs : hs + 128].reshape(128, 128)
        cv = cb[:, 1, :, hs : hs + 128].reshape(128, 128)
        s1 = lax.dot_general(qn, ck, (((1,), (1,)), ((), ())), preferred_element_type=F32)
        w1 = jnp.where(block_end <= pos, jnp.exp(SCALE * s1), 0.0)
        t1 = jnp.sum(w1, axis=1, keepdims=True) + (pos < 31).astype(F32)
        o1 = jnp.dot(w1.astype(BF), cv, preferred_element_type=F32) / t1
        kn = unit(kb[:, :, :, hs : hs + 128].reshape(768, 128).astype(F32)).astype(BF)
        vn = vb[:, :, :, hs : hs + 128].reshape(768, 128)
        s2 = lax.dot_general(qn, kn, (((1,), (1,)), ((), ())), preferred_element_type=F32)
        inside = (key_pos <= pos) & (key_pos > pos - WINDOW) & (key_pos >= 0)
        w2 = jnp.where(inside, jnp.exp(SCALE * s2), 0.0)
        t2 = jnp.sum(w2, axis=1, keepdims=True)
        o2 = jnp.dot(w2.astype(BF), vn, preferred_element_type=F32) / t2
        g1 = jnp.sum(jnp.where(lane == 2 * core + h, gates, 0.0), axis=1, keepdims=True)
        g2 = jnp.sum(jnp.where(lane == 4 + 2 * core + h, gates, 0.0), axis=1, keepdims=True)
        tb[:, :, hs : hs + 128] = (g1 * o1 + g2 * o2).astype(BF).reshape(2, 128, 128)
    back = rcopy(tb.at[other], xb.at[z, core], ss.at[28], rs.at[28], sib)
    back.start()
    xb[z, core] = tb[core]

    def drain():
        @pl.when(core == 0)
        def _():
            for cp in halo:
                cp.wait_send()

        for cp in swap + near + comps + relay + share + [back]:
            cp.wait_send()

    return share[0], back, drain


def z_ring(buf, z, core, e, ss, rs, turn):
    up, down = lax.rem(z + 1, 8), lax.rem(z + 7, 8)

    def copy(way, step, chunk):
        block = lax.rem(z + 8 - step, 8) if way == 0 else lax.rem(z + step, 8)
        slot = way * 7 + 2 * step + (chunk if step < 3 else 0)
        return rcopy(
            buf.at[block, lax.rem(chunk + turn, 2)],
            buf.at[block, lax.rem(chunk + turn, 2)],
            ss.at[slot],
            rs.at[slot],
            (2 * (up if way == 0 else down) + core, e),
        )

    def chunks(way, step):
        return (0, 1) if step < 3 else ((0,) if way == 0 else (1,))

    return copy, chunks


def gather_start(copy, chunk, sent, flip=0):
    for way in (0, 1):
        cp = copy(way, 0, (chunk + way * flip) % 2)
        cp.start()
        sent.append(cp)


def gather_step(copy, chunks, step, sent, flip=0):
    for n in (0, 1):
        for way in (0, 1):
            chunk = (n + way * flip) % 2
            if chunk in chunks(way, step):
                copy(way, step, chunk).wait_recv()
                if step < 3 and chunk in chunks(way, step + 1):
                    cp = copy(way, step + 1, chunk)
                    cp.start()
                    sent.append(cp)


DA = 4608
DB = 7168 - DA
HA = 3584
HB = 7168 - HA
FAR = (
    (2, 2), (2, 1), (1, 2), (2, 3), (3, 2), (1, 1), (3, 3), (1, 3), (3, 1), (2, 0), (0, 2),
    (1, 0), (0, 1), (3, 0), (0, 3),
)
NEAR = ((0, 1, 7, 2), (6, 3, 5, 4))


def three(x):
    a = x.astype(BF)
    r = x - a.astype(F32)
    b = r.astype(BF)
    return jnp.concatenate([a, b, (r - b.astype(F32)).astype(BF)], 0)


def turned(x):
    if x.shape[0] < 128:
        x = jnp.concatenate([x, jnp.zeros((128 - x.shape[0], 128), F32)], 0)
    return x.T


def one(cond):
    return jnp.where(cond, 1.0, 0.0)


def tail(
    q, k, v, g, cw, wo, res, gain, ids, gts, eg, eu, ed,
    out,
    wp, kb, vb, qb, gb, gs, hk, hv, cb, tb, s0, r0, l0,
    sc, inf, hs, hid,
    xb, pb, a1, a2, a3, sb, c2, rb, ss, rs, s1, r1, s2, r2, s3, r3, si, ri,
    gw, dw, ys, sw, rw, ls,
    oa, aa, xa, ya, rv, mx, fs, ro, ra, tr, sB, aB, yB, rB, zs, zr,
    sa, qa, sg, qg, st, qt, sx, qx, sy, qy, sv, qv, sh, qh, sz, qz,
):
    z, core, e = place()
    ex, ey = lax.div(e, 4), lax.rem(e, 4)
    c = 2 * z + core
    sib = (2 * z + 1 - core, e)
    ring = [
        (ex, lambda t: (c, 4 * lax.rem(t, 4) + ey)),
        (ey, lambda t: (c, 4 * ex + lax.rem(t, 4))),
    ]
    zp = [(2 * lax.rem(z + j, 8) + core, e) for j in range(1, 8)]
    dest = [4 * lax.rem(ex + a, 4) + lax.rem(ey + b, 4) for a, b in FAR]
    plane = [(c, d) for d in dest]
    cross = [(2 * lax.rem(z + j, 8) + 1 - core, e) for j in (1, 7)]
    greet(plane + zp + [sib] + cross)
    outw, swapped, drain = attend(
        z, core, e, q, k, v, g, cw, wo, wp, xb, kb, vb, qb, gb, gs, hk, hv, cb, tb, s0, r0, l0
    )

    copy, chunks = z_ring(xb, z, core, e, ss, rs, core)
    sent = []
    gather_start(copy, 0, sent)

    share = []
    for n, src in enumerate((eg, eu)):
        share.append(rcopy(src, gw.at[:, pl.ds(256 * n + 128, 128)], sw.at[n], rw.at[n], sib))
    share.append(rcopy(ed, dw.at[pl.ds(128, 128), :], sw.at[2], rw.at[2], sib))
    load = [
        pltpu.make_async_copy(eg, gw.at[:, pl.ds(0, 128)], ls.at[0]),
        pltpu.make_async_copy(eu, gw.at[:, pl.ds(256, 128)], ls.at[1]),
        pltpu.make_async_copy(ed, dw.at[pl.ds(0, 128), :], ls.at[2]),
    ]
    for cp in share + load:
        cp.start()

    sc[...] = jnp.zeros_like(sc)
    sc[0:2, 0:8] = ids[...].astype(F32)
    sc[2:4, 0:8] = gts[...]
    cols = sc[...].T
    id0, id1, g0, g1 = (cols[0:8, n : n + 1] for n in range(4))
    lane = lax.broadcasted_iota(jnp.int32, (8, 128), 1)
    lanef = lane.astype(F32)
    named = one(lanef == id0) + one(lanef == id1)
    before, rows = jnp.zeros((1, 128), F32), []
    for t in range(8):
        rows.append(before)
        before = before + named[t : t + 1]
    count = jnp.concatenate(rows, 0)

    def target(i):
        return 2.0 * i + jnp.sum(jnp.where(lanef == i, count, 0.0), axis=1, keepdims=True)

    t0, t1 = target(id0), target(id1)
    inf[0] = jnp.where(
        lane == 0, t0, jnp.where(lane == 1, t1, jnp.where(lane == 2, g0, jnp.where(lane == 3, g1, 0.0)))
    )
    told = [rcopy(inf.at[0], inf.at[8 - j], si.at[j], ri.at[j], zp[j - 1]) for j in range(1, 8)]
    for cp in told:
        cp.start()

    def partial(block, r):
        x0, x1 = xb[block, 0], xb[block, 1]
        dims = (((1,), (1,)), ((), ()))
        y = lax.dot_general(x0, wp[:, :256], dims, preferred_element_type=F32)
        y = y + lax.dot_general(x1, wp[:, 256:], dims, preferred_element_type=F32)
        pb[r] = y.reshape(4, 4, 8, 896).astype(BF)

    swapped.wait_recv()
    gather_start(copy, 1, sent)
    outw.wait_recv()

    def ring_sum(which, g, half, piece, first, second, mixed, ssem, rsem):
        p, dev = ring[which]
        nxt, prv = dev(p + 1), dev(p + 3)
        base = 12 * g + 6 * half
        far, nt, pt = lax.rem(p + 2, 4), lax.rem(p + 1, 4), lax.rem(p + 3, 4)
        legs = [
            (piece(far, 0), first.at[g, half, 0], nxt),
            (piece(far, 1), first.at[g, half, 1], prv),
            (piece(nt, 1), second.at[g, half, 0, 1], nxt),
            (piece(pt, 0), second.at[g, half, 1, 0], prv),
            (mixed.at[g, half, 0], second.at[g, half, 0, 0], nxt),
            (mixed.at[g, half, 1], second.at[g, half, 1, 1], prv),
        ]
        cps = [
            rcopy(src, dst, ssem.at[base + n], rsem.at[base + n], dev)
            for n, (src, dst, dev) in enumerate(legs)
        ]

        def start():
            for cp in cps[:4]:
                cp.start()

        def middle():
            for n, t in ((0, nt), (1, pt)):
                cps[n].wait_recv()
                mixed[g, half, n] = (
                    first[g, half, n].astype(F32) + piece(t, n)[...].astype(F32)
                ).astype(BF)
                cps[4 + n].start()

        def end():
            for cp in cps[2:]:
                cp.wait_recv()
            return [
                piece(p, n)[...].astype(F32)
                + second[g, half, 0, n].astype(F32)
                + second[g, half, 1, n].astype(F32)
                for n in range(2)
            ]

        def drain():
            for cp in cps:
                cp.wait_send()

        return start, middle, end, drain

    def piece_a(g):
        return lambda t, n: pb.at[4 * g + n, t]

    def piece_b(g):
        return lambda t, n: pb.at[4 * g + 2 + n, :, t]

    wide = [
        [
            ring_sum(0, g, 0, piece_a(g), a1, a2, a3, s1, r1),
            ring_sum(1, g, 1, piece_b(g), a1, a2, a3, s1, r1),
        ]
        for g in range(2)
    ]
    thin = []
    moved = []

    def fan(g, stage):
        for r in wide[g]:
            r[stage]()

    def turn(g):
        for half in range(2):
            for n, y in enumerate(wide[g][half][2]()):
                sb[g, half, :, n] = y.astype(BF)
            p, dev = ring[1 - half]
            for j in (2, 1, 3):
                n = 4 * (2 * g + half) + j
                cp = rcopy(
                    sb.at[g, half, lax.rem(p + j, 4)], c2.at[g, half, j], s2.at[n], r2.at[n], dev(p + j)
                )
                cp.start()
                thin.append(cp)

    def move(g):
        for half in range(2):
            for cp in thin[6 * g + 3 * half : 6 * g + 3 * half + 3]:
                cp.wait_recv()
            total = sb[g, half, ring[1 - half][0]].astype(F32)
            for j in range(1, 4):
                total = total + c2[g, half, j].astype(F32)
            for n in range(2):
                r = NEAR[g][2 * half + n]
                rb[r] = total[n].astype(BF)
                if r:
                    cp = rcopy(rb.at[r], hid.at[z], s3.at[r], r3.at[r], zp[r - 1])
                    cp.start()
                    moved.append(cp)
                else:
                    hid[z] = rb[0]

    def partial(place):
        r = NEAR[place // 4][place % 4]
        block = lax.rem(z + r, 8)
        x0, x1 = xb[block, 0], xb[block, 1]
        dims = (((1,), (1,)), ((), ()))
        y = lax.dot_general(x0, wp[:, :256], dims, preferred_element_type=F32)
        y = y + lax.dot_general(x1, wp[:, 256:], dims, preferred_element_type=F32)
        pb[place] = y.reshape(4, 4, 8, 896).astype(BF)

    partial(0)
    gather_step(copy, chunks, 0, sent)
    partial(1)
    partial(2)
    gather_step(copy, chunks, 1, sent)
    partial(3)
    fan(0, 0)
    partial(4)
    gather_step(copy, chunks, 2, sent)
    fan(0, 1)
    partial(5)
    partial(6)
    turn(0)
    gather_step(copy, chunks, 3, sent)
    partial(7)
    fan(1, 0)
    move(0)
    fan(1, 1)
    turn(1)
    move(1)

    for cp in told:
        cp.wait_recv()
    mine0 = (lanef == t0) | (lanef == t1)
    spread_a = turned(one(mine0))[:32, :16].astype(BF)
    weigh_a = three((jnp.where(lanef == t0, g0, 0.0) + jnp.where(lanef == t1, g1, 0.0))[:, :32])
    slot = lax.broadcasted_iota(jnp.int32, (32, 128), 1)
    token = lax.broadcasted_iota(jnp.int32, (32, 128), 0)
    slotf = (2 * lax.div(slot, 8) + lax.rem(slot, 2)).astype(F32)
    same = lax.rem(lax.div(slot, 2), 4) == lax.div(token, 8)
    spread_b, weigh_b = [], []
    for g in range(2):
        t = jnp.concatenate([inf[r] for r in NEAR[g]], 0)
        hit0, hit1 = same & (slotf == t[:, 0:1]), same & (slotf == t[:, 1:2])
        spread_b.append(turned(one(hit0 | hit1))[:, :32].astype(BF))
        weigh_b.append(three(jnp.where(hit0, t[:, 2:3], 0.0) + jnp.where(hit1, t[:, 3:4], 0.0)))
    pr = lax.broadcasted_iota(jnp.int32, (128, 128), 0)
    pc = lax.broadcasted_iota(jnp.int32, (128, 128), 1)

    def plane_place(n):
        return lax.rem(lax.div(n, 2), 16) * 8 + lax.div(n, 32) * 2 + lax.rem(n, 2)

    order = one(pc == plane_place(pr)).astype(BF)
    unorder = one(pr == plane_place(pc)).astype(BF)

    for cp in moved:
        cp.wait_recv()
    for n in range(8):
        lo, hi = 896 * n, 896 * n + 896
        hs[:, lo:hi] = res[:, lo:hi].astype(F32) + hid[n].astype(F32)
    h = hs[...]
    normed = h * lax.rsqrt(jnp.mean(h * h, axis=1, keepdims=True) + EPS) * gain[...]

    tr[0] = normed[:, DA:].astype(BF)
    spoke = []

    def tell(r):
        src, dev = (tr.at[r - 1], zp[6]) if r <= 4 else (tr.at[(r + 1) % 8], zp[0])
        cp = rcopy(src, tr.at[r], st.at[r], qt.at[r], dev)
        cp.start()
        spoke.append(cp)

    def heard(r):
        rcopy(tr.at[0], tr.at[r], st.at[0], qt.at[r], sib).wait_recv()

    tell(1)
    tell(7)

    padded = jnp.concatenate([normed[:, :DA], jnp.zeros((8, DA), F32)], 0).astype(BF)
    fs[:, :DA] = jnp.dot(spread_a, padded, preferred_element_type=F32)
    for i in range(16):
        oa[i] = fs[2 * i : 2 * i + 2, :DA].astype(BF)
    go = []
    for j in range(1, 16):
        cp = rcopy(oa.at[dest[j - 1]], aa.at[e], sa.at[j], qa.at[j], plane[j - 1])
        cp.start()
        go.append(cp)
    aa[e] = oa[e]

    def scatter(g):
        x = jnp.concatenate([tr[r].astype(F32) for r in NEAR[g]], 0).astype(BF)
        y = jnp.dot(spread_b[g], x, preferred_element_type=F32)
        sB[g] = y.reshape(16, 8, DB).astype(BF)
        for j in range(1, 16):
            cp = rcopy(
                sB.at[g, dest[j - 1]], aB.at[g, e], sg.at[g, j], qg.at[g, j], plane[j - 1]
            )
            cp.start()
            go.append(cp)
        aB[g, e] = sB[g, e]

    heard(1)
    tell(2)
    heard(7)
    tell(6)
    heard(2)
    tell(3)
    heard(6)
    tell(5)
    scatter(0)
    for cp in go[:15]:
        cp.wait_recv()
    for i in range(16):
        fs[2 * i : 2 * i + 2, :DA] = aa[i].astype(F32)
    xa[z, 0] = fs[0:16, :DA].astype(BF)
    xa[z, 1] = fs[16:32, :DA].astype(BF)
    copy2, chunks2 = z_ring(xa, z, core, e, sx, qx, 0)
    sent2 = []
    gather_start(copy2, 0, sent2, 1)
    gather_start(copy2, 1, sent2, 1)
    for cp in load:
        cp.wait()
    for cp in share:
        cp.wait_recv()
    heard(3)
    tell(4)
    heard(5)

    home = []

    def early(g):
        for j in range(1, 16):
            rcopy(sB.at[g, 0], aB.at[g, 0], sg.at[g, j], qg.at[g, j], sib).wait_recv()
        x = aB[g].astype(F32).reshape(128, DB).astype(BF)
        x = jnp.dot(order, x, preferred_element_type=F32).astype(BF)
        ys[...] = jnp.dot(x, gw[DA:, :], preferred_element_type=F32)

    def work(g):
        blocks = [lax.rem(z + r, 8) for r in NEAR[g]]
        x = jnp.concatenate([xa[b, n] for b in blocks for n in range(2)], 0)
        y = jnp.dot(x, gw[0:DA, :], preferred_element_type=F32) + ys[...]
        gate, lift = y[:, :256], y[:, 256:]
        act = (gate / (1.0 + jnp.exp(-gate)) * lift).astype(BF)
        actp = jnp.dot(unorder, act, preferred_element_type=F32).astype(BF)

        @pl.loop(0, HB // 512)
        def _(n):
            cols = pl.ds(pl.multiple_of(n * 512, 512), 512)
            dcols = pl.ds(pl.multiple_of(HA + n * 512, 512), 512)
            y = jnp.dot(actp, dw[:, dcols], preferred_element_type=F32)
            yB[g, :, :, cols] = y.reshape(16, 8, 512).astype(BF)

        for j in range(1, 16):
            cp = rcopy(
                yB.at[g, dest[j - 1]], rB.at[g, e], sy.at[g, j], qy.at[g, j], plane[j - 1]
            )
            cp.start()
            home.append(cp)
        rB[g, e] = yB[g, e]

        @pl.loop(0, HA // 512)
        def _(n):
            cols = pl.ds(pl.multiple_of(n * 512, 512), 512)
            y = jnp.dot(act, dw[:, cols], preferred_element_type=F32).astype(BF)
            for i, b in enumerate(blocks):
                ya[b, 0, :, cols] = y[32 * i : 32 * i + 16]
                ya[b, 1, :, cols] = y[32 * i + 16 : 32 * i + 32]

    gather_step(copy2, chunks2, 0, sent2, 1)
    heard(4)
    scatter(1)
    gather_step(copy2, chunks2, 1, sent2, 1)
    early(0)
    work(0)
    gather_step(copy2, chunks2, 2, sent2, 1)
    early(1)
    gather_step(copy2, chunks2, 3, sent2, 1)
    work(1)

    up, down = zp[0], zp[6]

    def leg(way, n, src):
        return rcopy(
            src, rv.at[way, n], sv.at[way * 7 + n], qv.at[way * 7 + n], up if way == 0 else down
        )

    def mine(way, dist, first):
        block = lax.rem(z + dist, 8) if way == 0 else lax.rem(z + 8 - dist, 8)
        return ya.at[block, first if way == 0 else 1 - first]

    back = []

    def send(way, n, src):
        cp = leg(way, n, src)
        cp.start()
        back.append(cp)

    for way in (0, 1):
        send(way, 0, mine(way, 4, 0))
    for way in (0, 1):
        send(way, 2, mine(way, 3, 1))

    def along(n, dist, first, source):
        for way in (0, 1):
            leg(way, source, rv.at[way, source]).wait_recv()
            mx[way, n] = (
                rv[way, source].astype(F32) + mine(way, dist, first)[...].astype(F32)
            ).astype(BF)
            send(way, n, mx.at[way, n])

    part = []

    def gather_home(g):
        for j in range(1, 16):
            rcopy(yB.at[g, 0], rB.at[g, 0], sy.at[g, j], qy.at[g, j], sib).wait_recv()
        x = rB[g].astype(F32).reshape(128, HB).astype(BF)
        y = jnp.dot(weigh_b[g], x, preferred_element_type=F32)
        y = y[0:32] + y[32:64] + y[64:96]
        for i, r in enumerate(NEAR[g]):
            zs[r] = y[8 * i : 8 * i + 8].astype(BF)
            if r:
                cp = rcopy(zs.at[r], zr.at[8 - r], sz.at[r], qz.at[8 - r], zp[r - 1])
                cp.start()
                part.append(cp)

    along(1, 3, 0, 0)
    along(4, 2, 1, 2)
    along(3, 2, 0, 1)
    gather_home(0)
    along(6, 1, 1, 4)
    along(5, 1, 0, 3)
    gather_home(1)
    for chunk in range(2):
        total = ya[z, chunk].astype(F32)
        for way in (0, 1):
            n = 5 + (chunk if way == 0 else 1 - chunk)
            leg(way, n, rv.at[way, n]).wait_recv()
            total = total + rv[way, n].astype(F32)
        fs[16 * chunk : 16 * chunk + 16, :HA] = total
    for i in range(16):
        ro[i] = fs[2 * i : 2 * i + 2, :HA].astype(BF)
    last = []
    for j in range(1, 16):
        cp = rcopy(ro.at[dest[j - 1]], ra.at[e], sh.at[j], qh.at[j], plane[j - 1])
        cp.start()
        last.append(cp)
    ra[e] = ro[e]
    for cp in last:
        cp.wait_recv()
    for i in range(16):
        fs[2 * i : 2 * i + 2, :HA] = ra[i].astype(F32)
    y = jnp.dot(weigh_a, fs[:, :HA].astype(BF), preferred_element_type=F32)
    out[:, :HA] = (hs[:, :HA] + (y[0:8] + y[8:16] + y[16:24])).astype(BF)
    total = hs[:, HA:] + zs[0].astype(F32)
    for r in range(1, 8):
        rcopy(zs.at[0], zr.at[r], sz.at[0], qz.at[r], sib).wait_recv()
        total = total + zr[r].astype(F32)
    out[:, HA:] = total.astype(BF)

    drain()
    for r in wide[0] + wide[1]:
        r[3]()
    for cp in sent + share + told + thin + moved + spoke + go + sent2 + home + back + part + last:
        cp.wait_send()


def run(q, k, v, g, cw, wo, res, gain, ids, gts, eg, eu, ed):
    vm = pl.BlockSpec(memory_space=pltpu.VMEM)
    hbm = pl.BlockSpec(memory_space=pltpu.HBM)

    def dma(*shape):
        return pltpu.SemaphoreType.DMA(shape)

    def bf(*shape):
        return pltpu.VMEM(shape, BF)

    def f32(*shape):
        return pltpu.VMEM(shape, F32)

    return pl.pallas_call(
        tail,
        out_shape=jax.ShapeDtypeStruct((8, 7168), BF),
        in_specs=[hbm] * 3 + [vm] * 2 + [hbm] + [vm] * 4 + [hbm] * 3,
        out_specs=vm,
        scratch_shapes=[
            bf(896, 512),
            bf(3, 2, 128, 256),
            bf(3, 2, 128, 256),
            bf(2, 128, 256),
            f32(2, 2, 4, 128),
            f32(2, 128, 128),
            bf(16, 256),
            bf(16, 256),
            bf(8, 2, 16, 256),
            bf(2, 128, 256),
            dma(29), dma(29), dma(4),
            f32(128, 128),
            f32(8, 8, 128),
            f32(8, 7168),
            bf(8, 8, 896),
            bf(8, 2, 128, 256),
            bf(8, 4, 4, 8, 896),
            bf(2, 2, 2, 4, 8, 896),
            bf(2, 2, 2, 2, 4, 8, 896),
            bf(2, 2, 2, 4, 8, 896),
            bf(2, 2, 4, 2, 8, 896),
            bf(2, 2, 4, 2, 8, 896),
            bf(8, 8, 896),
            dma(14), dma(14), dma(24), dma(24), dma(16), dma(16), dma(8), dma(8), dma(8), dma(8),
            bf(7168, 512),
            bf(256, 7168),
            f32(128, 512),
            dma(3), dma(3), dma(3),
            bf(16, 2, DA),
            bf(16, 2, DA),
            bf(8, 2, 16, DA),
            bf(8, 2, 16, HA),
            bf(2, 7, 16, HA),
            bf(2, 7, 16, HA),
            f32(32, max(DA, HA)),
            bf(16, 2, HA),
            bf(16, 2, HA),
            bf(8, 8, DB),
            bf(2, 16, 8, DB),
            bf(2, 16, 8, DB),
            bf(2, 16, 8, HB),
            bf(2, 16, 8, HB),
            bf(8, 8, HB),
            bf(8, 8, HB),
            dma(16), dma(16), dma(2, 16), dma(2, 16), dma(8), dma(8), dma(14), dma(14),
            dma(2, 16), dma(2, 16), dma(14), dma(14), dma(16), dma(16), dma(8), dma(8),
        ],
        compiler_params=pltpu.CompilerParams(
            collective_id=2, has_side_effects=True, vmem_limit_bytes=67043328
        ),
        name="layer",
    )(q, k, v, g, cw, wo, res, gain, ids, gts, eg, eu, ed)


def local(
    query_input,
    key_input,
    value_input,
    gate_logits,
    comp_weight,
    out_proj,
    residual_in,
    ffn_gain,
    expert_ids,
    route_gates,
    expert_gate,
    expert_up,
    expert_down,
):
    gates = gate_logits.transpose(0, 2, 1)
    return run(
        query_input, key_input, value_input, gates, comp_weight.transpose(0, 2, 1), out_proj.T,
        residual_in, ffn_gain.reshape(1, 7168), expert_ids.T, route_gates.T,
        expert_gate[0], expert_up[0], expert_down[0],
    )


def solution(mesh):
    in_specs = (
        P("ctx", "exp"),
        P("ctx", "exp"),
        P("ctx", "exp"),
        P(None, "ctx", "exp"),
        P(None, None, "exp"),
        P("exp", "ctx"),
        P(("ctx", "exp"), None),
        P(),
        P(("ctx", "exp"), None),
        P(("ctx", "exp"), None),
        P("exp", None, "ctx"),
        P("exp", None, "ctx"),
        P("exp", "ctx", None),
    )
    out_specs = P(("ctx", "exp"), None)
    return jax.shard_map(local, mesh=mesh, in_specs=in_specs, out_specs=out_specs, check_vma=False)
```
